32 devices in a mesh: region: 8 (over z, x), scen: 4 (over y, core).
Axes of the slice: x: 2, y: 2, z: 4, core: 2. Of those that a mesh axis runs over, the one named last changes fastest.
Arguments:
- inv_blocks: float32 [192, 128, 128], P('region'), may hold values from -0.02 to 3, as said below
- src_amp: float32 [24576], P('region'), may hold values from -5 to 5
- src_phase: float32 [24576], P('region'), may hold values from -3.140625 to 3.140625
- line_a: int32 [8, 256], P('region'), may hold values from 0 to 3071
- line_b: int32 [8, 256], P('region'), may hold values from 0 to 3071
- line_delay: int32 [8, 256], P('region'), may hold values from 2 to 6
- line_yc: float32 [8, 256], P('region'), may hold values from 0.05 to 0.35
- line_atten: float32 [8, 256], P('region'), may hold values from 0.6 to 1
- hist_ua: float32 [8, 6, 128, 256], P('region', None, 'scen'), may hold values from -3 to 3
- hist_ub: float32 [8, 6, 128, 256], P('region', None, 'scen'), may hold values from -3 to 3
- send_node: int32 [8, 8, 64], P('region'), may hold values from -1 to 3071, as said below
- recv_slot: int32 [8, 128], P('region'), may hold values from 0 to 511, as said below
- conv_par: float32 [6, 1024], P(None, 'region'), may hold values from -1.5 to 3, as said below
- conv_state: float32 [2, 128, 1024], P(None, 'scen', 'region'), may hold values from -3 to 3
- fault_node: int32 [128], P('scen'), may hold values from 0 to 24575
- fault_step: int32 [128], P('scen'), may hold values from 0 to 7
- fault_cond: float32 [128], P('scen'), may hold values from 2 to 20
Outputs:
- volts: float32 [128, 24576], P('scen', 'region')
- conv_current: float32 [128, 1024], P('scen', 'region')
- rms_volt: float32 [24576], P('region')
The draws below stay inside these ranges and needn't reach their ends.
Inputs may be any that keep to these rules, and one draw needn't show every extreme that they name: `send_node`: each region places the same number of converters in every group, and one region places 64 in every group; entries c at or beyond that number are -1, the others are nodes of the region. `recv_slot`: each group's 128 slots name distinct live entries of send_node, and every live entry is named by exactly one slot of its group. `conv_par`: retention lies in 0.5 to 0.98, filter rate in 0.2 to 0.8, current limit in 0.5 to 3. `inv_blocks`: each block is symmetric with a positive diagonal larger than the sum of its row's other magnitudes.
All inputs are finite; a program needn't handle non-finite values.
Results may differ from the reference program's by a relative error of at most 0.0003.
Values sent between devices are 32-bit elements; how exact they have to be, the bound alone decides.
No kernel may reach another device: no remote copies, remote signals or barrier semaphores. Data moves between devices by JAX's collectives and lax.ppermute only.
A program may use at most 64 MiB of HBM per device.

```python
import math
import jax
import jax.numpy as jnp
from jax import lax

BLK = 128
LDEV = 256
GS = 128
STEPS = 8
MAXD = 6
DMIN = 2
NREG = 3072
REGIONS = 8
BLOCKS = 192
NODES = 24576
SCEN = 128
CAP = 64
CONVS = 1024


def conv_plan(key):
    base_key = jax.random.fold_in(key, 7)
    k_order, k_move, k_perm, k_node = jax.random.split(base_key, 4)
    order = jax.random.permutation(k_order, REGIONS)
    others = REGIONS - 1
    spare = GS - CAP
    base = spare // others
    extra = spare - base * others
    position = jnp.arange(others, dtype=jnp.int32)
    counts_rest = base + (position < extra).astype(jnp.int32)
    moved = jax.random.randint(k_move, (others,), 0, base)
    given = jnp.where((position % 2 == 0) & (position + 1 < others), moved, 0)
    counts_rest = counts_rest - given + jnp.roll(given, 1)
    counts = jnp.zeros((REGIONS,), jnp.int32).at[order[1:]].set(counts_rest).at[order[0]].set(CAP)
    ends = jnp.cumsum(counts)
    starts = ends - counts
    ranks = jnp.arange(GS, dtype=jnp.int32)
    region_of = jnp.sum((ends[None, :] <= ranks[:, None]).astype(jnp.int32), axis=1)
    placed = ranks - starts[region_of]
    values = region_of * CAP + placed
    perms = jax.vmap(lambda sub_key: jax.random.permutation(sub_key, GS))(jax.random.split(k_perm, REGIONS))
    inverse = jnp.argsort(perms, axis=1)
    received = values[inverse]
    nodes = jax.random.randint(k_node, (REGIONS, REGIONS, CAP), 0, NREG)
    live = jnp.arange(CAP)[None, None, :] < counts[:, None, None]
    sent = jnp.where(live, nodes, -1)
    return (sent.astype(jnp.int32), received.astype(jnp.int32))


def draw_send_node(key, part):
    return conv_plan(key)[0]


def draw_recv_slot(key, part):
    return conv_plan(key)[1]


def draw_inv_blocks(key, part):
    k_off, k_diag = jax.random.split(jax.random.fold_in(key, 3))
    scale = 0.8 / BLK
    diagonal = jax.random.uniform(k_diag, (BLOCKS, BLK), jnp.float32, 0.9, 2.0)
    raw = jax.random.uniform(k_off, (BLOCKS, BLK, BLK), jnp.float32, -1.0, 1.0) * scale
    symmetric = 0.5 * (raw + jnp.swapaxes(raw, 1, 2))
    identity = jnp.eye(BLK, dtype=jnp.float32)
    return symmetric * (1.0 - identity)[None] + identity[None] * diagonal[:, :, None]


def draw_conv_par(key, part):
    keys = jax.random.split(jax.random.fold_in(key, 5), 6)
    setpoint = jax.random.normal(keys[0], (CONVS,), jnp.float32).clip(-1.5, 1.5) * 0.6
    power = jax.random.normal(keys[4], (CONVS,), jnp.float32).clip(-1.5, 1.5) * 0.6
    retain = jax.random.uniform(keys[1], (CONVS,), jnp.float32, 0.5, 0.98)
    gain = jnp.exp(jax.random.uniform(keys[2], (CONVS,), jnp.float32, -2.3, 0.0))
    rate = jax.random.uniform(keys[3], (CONVS,), jnp.float32, 0.2, 0.8)
    limit = jnp.exp(jax.random.uniform(keys[5], (CONVS,), jnp.float32, -0.69, 1.09))
    return jnp.stack([setpoint, retain, gain, rate, power, limit])


def set_ends(result, key, least, largest):
    longest = result.shape.index(max(result.shape))
    spots = []
    for shift in (0, 1):
        where = [jax.random.randint(jax.random.fold_in(key, axis), (), 0, length) for axis, length in enumerate(result.shape)]
        where[longest] = (where[longest] + shift) % result.shape[longest]
        spots.append(tuple(where))
    return result.at[spots[0]].set(least).at[spots[1]].set(largest)


def block_scale(rng, shape, cuts, low, high):
    level, own = 1.0, jax.random.fold_in(rng, 6)
    for dim, parts in cuts:
        steps = jnp.exp(jax.random.uniform(jax.random.fold_in(own, dim), (parts,), jnp.float32, low / len(cuts), high / len(cuts)))
        level = level * jnp.repeat(steps, shape[dim] // parts).reshape([-1 if axis == dim else 1 for axis in range(len(shape))])
    return level


def normal_values(key, dims, deviation, most, cuts=(), kind=jnp.bfloat16):
    factor_of = block_scale(key, dims, cuts, -0.22, 0.18) if cuts else 1.0
    result = jax.random.normal(key, dims, jnp.float32) * deviation * factor_of
    return jnp.minimum(jnp.maximum(result, -most), most).astype(kind)


def setup_inputs(seed: int = 0) -> dict:
    splits = jax.random.split(jax.random.key(seed), 18)
    inv_blocks = draw_inv_blocks(jax.random.fold_in(splits[17], 71), 0)
    src_amp = normal_values(splits[1], (NODES,), 1.0, 5.0, ((0, 8),), jnp.float32)
    src_phase = jnp.clip(jax.random.uniform(splits[2], (NODES,), jnp.float32, -3.140625, 3.140625), -3.140625, 3.140625)
    line_a = set_ends(jax.random.randint(splits[3], (REGIONS, LDEV), 0, NREG), jax.random.fold_in(splits[3], 1), 0, NREG - 1).astype(jnp.int32)
    line_b = set_ends(jax.random.randint(splits[4], (REGIONS, LDEV), 0, NREG), jax.random.fold_in(splits[4], 1), 0, NREG - 1).astype(jnp.int32)
    line_delay = set_ends(jax.random.randint(splits[5], (REGIONS, LDEV), DMIN, MAXD + 1), jax.random.fold_in(splits[5], 1), DMIN, MAXD).astype(jnp.int32)
    line_yc = jnp.clip(jnp.exp(math.log(0.35) - 1.9459101 * jax.random.uniform(splits[6], (REGIONS, LDEV), jnp.float32) ** block_scale(splits[6], (REGIONS, LDEV), ((0, 8),), -0.2, 0.2)), 0.05, 0.35)
    line_atten = jnp.clip(0.6 + 0.39999998 * jax.random.uniform(splits[7], (REGIONS, LDEV), jnp.float32) ** block_scale(splits[7], (REGIONS, LDEV), ((0, 8),), -0.2, 0.2), 0.6, 1.0)
    hist_ua = normal_values(splits[8], (REGIONS, MAXD, SCEN, LDEV), 0.5, 3.0, ((0, 8), (2, 4)), jnp.float32)
    hist_ub = normal_values(splits[9], (REGIONS, MAXD, SCEN, LDEV), 0.5, 3.0, ((0, 8), (2, 4)), jnp.float32)
    send_node = draw_send_node(jax.random.fold_in(splits[17], 71), 0)
    recv_slot = draw_recv_slot(jax.random.fold_in(splits[17], 71), 0)
    conv_par = draw_conv_par(jax.random.fold_in(splits[17], 71), 0)
    conv_state = normal_values(splits[13], (2, SCEN, CONVS), 0.5, 3.0, ((1, 4), (2, 8)), jnp.float32)
    fault_node = set_ends(jax.random.randint(splits[14], (SCEN,), 0, NODES), jax.random.fold_in(splits[14], 1), 0, NODES - 1).astype(jnp.int32)
    fault_step = set_ends(jax.random.randint(splits[15], (SCEN,), 0, STEPS), jax.random.fold_in(splits[15], 1), 0, STEPS - 1).astype(jnp.int32)
    fault_cond = jnp.clip(jnp.exp(math.log(20.0) - 2.3025851 * jax.random.uniform(splits[16], (SCEN,), jnp.float32) ** block_scale(splits[16], (SCEN,), ((0, 4),), -0.2, 0.2)), 2.0, 20.0)
    return dict(inv_blocks=inv_blocks, src_amp=src_amp, src_phase=src_phase, line_a=line_a, line_b=line_b, line_delay=line_delay, line_yc=line_yc, line_atten=line_atten, hist_ua=hist_ua, hist_ub=hist_ub, send_node=send_node, recv_slot=recv_slot, conv_par=conv_par, conv_state=conv_state, fault_node=fault_node, fault_step=fault_step, fault_cond=fault_cond)


OMEGA = 0.01884955592153876
EPS = 1e-06

def pick_delayed(history, delays, instant):
    total = jnp.zeros_like(history[0])
    for lag_steps in range(DMIN, MAXD + 1):
        total = total + jnp.where(delays[None, :] == lag_steps, history[MAXD + instant - lag_steps], 0.0)
    return total

def converter_update(state, volts, params):
    first = params[1] * state[0] + params[2] * (params[0] - volts)
    second = state[1] + params[3] * (first - state[1])
    return ((first, second), params[5] * jnp.tanh((params[4] + second) / params[5]))

def reference(inv_blocks, src_amp, src_phase, line_a, line_b, line_delay, line_yc, line_atten, hist_ua, hist_ub, send_node, recv_slot, conv_par, conv_state, fault_node, fault_step, fault_cond):
    regions = jnp.arange(REGIONS, dtype=jnp.int32)
    following = (regions + 1) % REGIONS
    glob_a = (regions[:, None] * NREG + line_a).reshape(-1)
    glob_b = (following[:, None] * NREG + line_b[following]).reshape(-1)
    delays = line_delay.reshape(-1)
    admit = line_yc.reshape(-1)[None, :]
    atten = line_atten.reshape(-1)[None, :]
    out_hist = [jnp.transpose(hist_ua[:, lag_steps], (1, 0, 2)).reshape(SCEN, -1) for lag_steps in range(MAXD)]
    back_hist = [jnp.transpose(hist_ub[:, lag_steps], (1, 0, 2)).reshape(SCEN, -1) for lag_steps in range(MAXD)]
    source_region = recv_slot // CAP
    source_place = recv_slot % CAP
    groups = jnp.arange(REGIONS, dtype=jnp.int32)[:, None]
    conv_nodes = (source_region * NREG + send_node[source_region, groups, source_place]).reshape(-1)
    params = [conv_par[row][None, :] for row in range(6)]
    state = (conv_state[0], conv_state[1])
    current = params[5] * jnp.tanh((params[4] + state[1]) / params[5])
    block_of = (fault_node // BLK).astype(jnp.int32)
    within = (fault_node % BLK).astype(jnp.int32)
    columns = inv_blocks[block_of, :, within]
    self_imp = inv_blocks[block_of, within, within]
    scen_rows = jnp.arange(SCEN, dtype=jnp.int32)
    targets = block_of[:, None] * BLK + jnp.arange(BLK, dtype=jnp.int32)[None, :]
    direction = jnp.zeros((SCEN, NODES), jnp.float32).at[scen_rows[:, None], targets].set(columns)
    ratio_fault = fault_cond / (1.0 + fault_cond * self_imp)
    squares = jnp.zeros((NODES,), jnp.float32)
    potential = jnp.zeros((SCEN, NODES), jnp.float32)
    for instant in range(STEPS):
        source = src_amp * jnp.cos(OMEGA * instant + src_phase)
        into_a = pick_delayed(back_hist, delays, instant)
        into_b = pick_delayed(out_hist, delays, instant)
        injection = jnp.broadcast_to(source[None, :], (SCEN, NODES))
        injection = injection.at[:, glob_a].add(into_a).at[:, glob_b].add(into_b).at[:, conv_nodes].add(current)
        potential = jnp.einsum('kij,skj->ski', inv_blocks, injection.reshape(SCEN, BLOCKS, BLK), precision=lax.Precision.HIGHEST).reshape(SCEN, NODES)
        active = (fault_step <= instant).astype(jnp.float32)
        coef = active * ratio_fault * potential[scen_rows, fault_node]
        potential = potential - direction * coef[:, None]
        squares = squares + lax.optimization_barrier(jnp.sum(potential * potential, axis=0))
        if instant <= STEPS - 1 - DMIN:
            out_hist.append(atten * (2.0 * admit * potential[:, glob_a] - into_a))
            back_hist.append(atten * (2.0 * admit * potential[:, glob_b] - into_b))
        state, current = converter_update(state, potential[:, conv_nodes], params)
    rms_volt = jnp.sqrt(squares / (SCEN * STEPS) + EPS)
    return (potential, current, rms_volt)
```

```python
import functools
from types import SimpleNamespace as Space

import jax
import jax.numpy as jnp
from jax import lax
from jax.experimental import pallas as pl
from jax.experimental.pallas import tpu as pltpu
from jax.sharding import PartitionSpec as P

STEPS = 8
DMIN = 2
LANES = 128
OMEGA = 0.01884955592153876
EPS = 1e-06
F32 = jnp.float32
BF16 = jnp.bfloat16
NN = (((1,), (0,)), ((), ()))
NT = (((1,), (1,)), ((), ()))


def shifted(value, axis, steps):
    count = lax.axis_size(axis)
    pairs = [(source, (source + steps) % count) for source in range(count)]
    return lax.ppermute(value, axis, pairs)


def call(body, name, ins, outs, scratch=(), cost=(1e9, 4e6)):
    leaves, tree = jax.tree.flatten(ins)
    out_names = list(outs)

    def kernel(*refs):
        first, second = len(leaves), len(leaves) + len(out_names)
        i = Space(**jax.tree.unflatten(tree, refs[:first]))
        o = Space(**dict(zip(out_names, refs[first:second])))
        body(i, o, *refs[second:])

    results = pl.pallas_call(
        kernel,
        name=name,
        out_shape=[jax.ShapeDtypeStruct(*outs[key]) for key in out_names],
        in_specs=[pl.BlockSpec(memory_space=pltpu.VMEM)] * len(leaves),
        out_specs=[pl.BlockSpec(memory_space=pltpu.VMEM)] * len(out_names),
        scratch_shapes=list(scratch),
        compiler_params=pltpu.CompilerParams(vmem_limit_bytes=24 << 20),
        cost_estimate=pl.CostEstimate(
            flops=int(cost[0]), bytes_accessed=int(cost[1]), transcendentals=0
        ),
    )(*leaves)
    return Space(**dict(zip(out_names, results)))


def iota(shape, dim):
    return lax.broadcasted_iota(jnp.int32, shape, dim)


def onehot(mask):
    return jnp.where(mask, 1.0, 0.0).astype(BF16)


def dot(left, right, dims=NN):
    return lax.dot_general(left, right, dims, preferred_element_type=F32)


def split2(value):
    high = value.astype(BF16)
    return high, (value - high.astype(F32)).astype(BF16)


def split3(value):
    high, rest = value.astype(BF16), value
    rest = value - high.astype(F32)
    mid = rest.astype(BF16)
    return high, mid, (rest - mid.astype(F32)).astype(BF16)


def product3(left, right_high, right_low, dims=NN):
    rows = left.shape[0]
    high, low = split2(left)
    both = dot(jnp.concatenate([high, low], axis=0), right_high, dims)
    return both[:rows] + both[rows:] + dot(high, right_low, dims)


def as_column(row, size):
    wide = jnp.broadcast_to(row, (size, size))
    return jnp.sum(
        jnp.where(iota((size, size), 0) == iota((size, size), 1), wide, 0.0), axis=1, keepdims=True
    )


def pick(wave, delays, instant, maxd):
    total = None
    for lag in range(DMIN, maxd + 1):
        term = jnp.where(delays == lag, wave(instant - lag), 0.0)
        total = term if total is None else total + term
    return total


def start_body(sizes, i, o):
    regions, cap, half, scen, group, maxd = sizes
    packed = 2 * cap == LANES
    slots = i.slots[...]
    rows = iota((regions * 2 * cap, group), 0)
    if packed:
        target = (slots // cap) * (2 * cap) + slots % cap
        moved = target + cap
    else:
        target = slots
        moved = slots + regions * cap
    left, right = onehot(rows == target), onehot(rows == moved)
    pad = jnp.zeros((half - scen - 6, group), F32)
    upper = jnp.concatenate([i.state[0], i.par[...], pad], axis=0)
    lower = jnp.concatenate([i.state[1], jnp.zeros((half - scen, group), F32)], axis=0)
    buffer = None
    for part, mask in ((upper, left), (lower, right)):
        both = dot(jnp.concatenate(split3(part), axis=0), mask, NT)
        value = both[:half] + both[half : 2 * half] + both[2 * half :]
        buffer = value if buffer is None else buffer + value
    if packed:
        for region in range(regions):
            o.send[region] = buffer[:, region * LANES : (region + 1) * LANES]
    else:
        o.send[...] = buffer
    delays = i.delay[...]
    for step in range(2):
        o.into[step] = pick(lambda t: i.hist[t + maxd], delays, step, maxd)


def model_body(sizes, i, o, spots, base, acc):
    nreg, nblk, lines, width, scen = sizes
    blk = LANES
    points = 2 * lines + width
    whole = points + blk
    spots[...] = jnp.full((1, whole), -1, jnp.int32)
    spots[:, 0:lines] = i.end_a[...]
    spots[:, lines : 2 * lines] = i.end_b[...]
    spots[:, 2 * lines : points] = i.conv[...]
    region = lax.axis_index("region")
    fault = i.fault_node[...] - region * nreg
    fault = jnp.where((fault >= 0) & (fault < nreg), fault, -1)
    spots[:, points : points + scen] = fault
    row = spots[...]
    row_blk, row_in = row >> 7, row & 127
    column = jnp.transpose(jnp.broadcast_to(row.astype(F32), (blk, whole))).astype(jnp.int32)
    column_blk = column >> 7
    o.spots[...] = column[:points]
    o.fault_blk[...] = column_blk[points : points + scen]
    z = i.inv[...].reshape(nreg, blk)
    z_high, z_low = split2(z)
    o.zcat[:, 0:blk] = z_high
    o.zcat[:, blk:] = z_low
    acc[...] = jnp.zeros_like(acc)
    lane = iota((whole, blk), 1)
    span = 2 * blk

    def gather(step, carry):
        start = pl.multiple_of(step * span, span)
        mine = jnp.concatenate(
            [onehot(column == lane + start), onehot(column == lane + (start + blk))], axis=1
        )
        acc[...] += dot(mine, o.zcat[pl.ds(start, span), :])
        return carry

    lax.fori_loop(0, nblk // 2, gather, 0)
    inside = onehot(iota((blk, points), 0) == row_in[:, :points])
    row_blk_p = row_blk[:, :points]

    def between(step, carry):
        start = pl.multiple_of(step * blk, blk)
        rows = acc[pl.ds(start, blk), :].astype(BF16)
        mine = o.spots[pl.ds(start, blk), :][:, 0:1] >> 7
        same = mine == row_blk_p
        both = dot(jnp.concatenate([rows[:, :blk], rows[:, blk:]], axis=0), inside)
        o.m_high[pl.ds(start, blk), :] = jnp.where(same, both[:blk], 0.0).astype(BF16)
        o.m_low[pl.ds(start, blk), :] = jnp.where(same, both[blk:], 0.0).astype(BF16)
        return carry

    lax.fori_loop(0, points // blk, between, 0)
    fault_rows = acc[points : points + scen, :]
    fault_z = fault_rows[:, :blk] + fault_rows[:, blk:]
    o.fault_z[...] = fault_z
    fault_blk = column_blk[points : points + scen]
    both = dot(
        jnp.concatenate([fault_rows[:, :blk], fault_rows[:, blk:]], axis=0).astype(BF16), inside
    )
    o.fault_p[...] = jnp.where(
        fault_blk[:, 0:1] == row_blk_p, both[:scen] + both[scen:], 0.0
    )
    instant = iota((STEPS, nreg), 0).astype(F32)
    source = i.amp[...] * jnp.cos(OMEGA * instant + i.phase[...])
    base[...] = jnp.concatenate(
        [source[:, k * blk : (k + 1) * blk] for k in range(nblk)], axis=0
    )
    for k in range(nblk):
        mine = o.zcat[k * blk : (k + 1) * blk, :]
        o.base[:, k * blk : (k + 1) * blk] = product3(
            base[k * STEPS : (k + 1) * STEPS, :], mine[:, :blk], mine[:, blk:]
        )
    rows = acc[...].astype(BF16)
    spread = product3(base[...], rows[:, :blk], rows[:, blk:], NT)
    at_points = jnp.zeros((STEPS, whole), F32)
    for k in range(nblk):
        at_points = at_points + jnp.where(row_blk == k, spread[k * STEPS : (k + 1) * STEPS], 0.0)
    o.base_p[...] = at_points[:, :points]
    tail = jnp.concatenate(
        [at_points[:, points:], jnp.zeros((blk - STEPS, blk), F32)], axis=0
    )
    o.fault_base[...] = jnp.transpose(tail)[:scen]
    self_imp = jnp.sum(
        jnp.where(iota((scen, blk), 1) == (column[points : points + scen] & 127), fault_z, 0.0),
        axis=1,
        keepdims=True,
    )
    cond = as_column(i.fault_cond[...], scen)
    closes = as_column(i.fault_step[...].astype(F32), scen)
    ratio = cond / (1.0 + cond * self_imp)
    o.fault_ratio[...] = jnp.where(
        closes <= iota((scen, blk), 1).astype(F32), jnp.broadcast_to(ratio, (scen, blk)), 0.0
    )


def advance_body(sizes, pair, i, o):
    lines, width, scen, cap, maxd, packed = sizes
    t0 = 2 * pair
    delays = i.delay[...]
    scale = i.atten[...]
    twice = 2.0 * i.admit[...]
    last = STEPS - 1

    fresh = {}
    if pair:
        for j in range(2):
            fresh[t0 - 2 + j] = scale * (twice * i.far_volts[j] - i.into_prev[j])
            if hasattr(o, "back"):
                o.back[j] = fresh[t0 - 2 + j]

    def back(t):
        if t in fresh:
            return fresh[t]
        if t < 0:
            return i.hist_b[t + maxd]
        return i.backs[t // 2][t % 2]

    made = {}

    def out(t):
        if t in made:
            return made[t]
        if t < 0:
            return i.hist_a[t + maxd]
        return i.made[t // 2][t % 2]

    live = i.conv[...] >= 0
    if packed:
        low = iota((1, LANES), 1) < cap
        params = []
        for row in range(6):
            pieces = []
            for j in range(width // LANES):
                one = i.recv[2 * j][scen + row : scen + row + 1, :]
                two = i.recv[2 * j + 1][scen + row : scen + row + 1, :]
                pieces.append(jnp.where(low, one, pltpu.roll(two, cap, 1)))
            params.append(jnp.concatenate(pieces, axis=1))
    else:
        params = [i.recv[0, scen + row : scen + row + 1, :] for row in range(6)]
    params[5] = jnp.where(live, params[5], 1.0)

    def drive(second):
        return params[5] * jnp.tanh((params[4] + second) / params[5])

    if pair:
        first, second, current = i.state[0], i.state[1], i.current[...]
    else:
        if packed:
            ups, downs = [], []
            for j in range(width // LANES):
                one, two = i.recv[2 * j][:scen], i.recv[2 * j + 1][:scen]
                ups.append(jnp.where(low, one, pltpu.roll(two, cap, 1)))
                downs.append(jnp.where(low, pltpu.roll(one, cap, 1), two))
            first, second = jnp.concatenate(ups, axis=1), jnp.concatenate(downs, axis=1)
        else:
            first, second = i.recv[0, :scen], i.recv[1, :scen]
        current = drive(second)

    fault_p = i.fault_p[...]
    for j in range(2):
        t = t0 + j
        into = pick(back, delays, t, maxd)
        x = jnp.concatenate([into, i.far_in[j], current], axis=1)
        high, low_part = split2(x)
        o.x[j * scen : (j + 1) * scen, :] = high
        o.x[(2 + j) * scen : (3 + j) * scen, :] = low_part
        both = dot(jnp.concatenate([high, low_part], axis=0), i.m_high[...])
        volts = both[:scen] + both[scen:] + dot(high, i.m_low[...])
        volts = volts + i.base_p[t : t + 1, :]
        at_fault = i.fault_base[:, t : t + 1] + jnp.sum(x * fault_p, axis=1, keepdims=True)
        coef = i.fault_ratio[:, t : t + 1] * at_fault
        o.coef[j * scen : (j + 1) * scen, :] = jnp.broadcast_to(coef, (scen, LANES))
        volts = volts - fault_p * coef
        if t <= last - DMIN:
            made[t] = scale * (twice * volts[:, :lines] - into)
            o.ends[j] = volts[:, lines : 2 * lines]
            if hasattr(o, "out"):
                o.out[j] = made[t]
        node = volts[:, 2 * lines :]
        first = params[1] * first + params[2] * (params[0] - node)
        second = second + params[3] * (first - second)
        current = drive(second)
    if hasattr(o, "into"):
        for j in range(2):
            o.into[j] = pick(out, delays, t0 + 2 + j, maxd)
    if hasattr(o, "state"):
        o.state[0] = first
        o.state[1] = second
    if t0 + 2 < STEPS or not packed:
        o.current[...] = current
    else:
        half = scen // 2
        for j in range(width // LANES):
            mine = current[:, j * LANES : (j + 1) * LANES]
            top, bottom = mine[:half], mine[half:]
            o.current[2 * j] = jnp.where(low, top, pltpu.roll(bottom, cap, 1))
            o.current[2 * j + 1] = jnp.where(low, pltpu.roll(top, cap, 1), bottom)


def full_body(sizes, pair, i, o):
    nblk, points, scen = sizes
    blk = LANES
    t0 = 2 * pair
    spots = i.spots
    fault_z = i.fault_z[...]
    fault_blk = i.fault_blk[...]
    x = i.x[...]
    lane = iota((points, blk), 1)
    coef = i.coef[...]

    def step(index, carry):
        start = pl.multiple_of(index * 2 * blk, 2 * blk)
        where = spots[...]
        mine = jnp.concatenate(
            [onehot(where == lane + start), onehot(where == lane + (start + blk))], axis=1
        )
        both = dot(x, mine)
        inject = both[: 2 * scen] + both[2 * scen :]
        for j in range(2):
            here = pl.ds(pl.multiple_of(start + j * blk, blk), blk)
            z = i.zcat[here, :]
            volts = product3(inject[:, j * blk : (j + 1) * blk], z[:, :blk], z[:, blk:])
            base = i.base[:, here]
            volts = volts + jnp.concatenate(
                [
                    jnp.broadcast_to(base[t0 + m : t0 + m + 1, :], (scen, blk))
                    for m in range(2)
                ],
                axis=0,
            )
            column = jnp.where(fault_blk == 2 * index + j, fault_z, 0.0)
            volts = volts - jnp.concatenate([column, column], axis=0) * coef
            total = jnp.sum(volts * volts, axis=0, keepdims=True)
            if hasattr(i, "squares"):
                total = total + i.squares[:, here]
            o.squares[:, here] = total
            if hasattr(o, "volts"):
                o.volts[:, here] = volts[scen:]
        return carry

    lax.fori_loop(0, nblk // 2, step, 0)


def finish_body(sizes, i, o):
    regions, cap, scen, group, count, packed = sizes
    parts = [i.parts[k][...] for k in range(count)]
    while len(parts) > 1:
        parts = [parts[k] + parts[k + 1] for k in range(0, len(parts), 2)]
    o.rms[...] = jnp.sqrt(parts[0] / (scen * count * STEPS) + EPS)
    slots = i.slots[...]
    if packed:
        half = scen // 2
        lane = iota((LANES, group), 0)
        top = bottom = None
        for region in range(regions):
            left = onehot((lane < cap) & (slots == region * cap + lane))
            right = onehot((lane >= cap) & (slots == (region - 1) * cap + lane))
            both = dot(
                jnp.concatenate(split3(i.recv[region]), axis=0),
                jnp.concatenate([left, right], axis=1),
            )
            value = both[:half] + both[half : 2 * half] + both[2 * half :]
            top = value if top is None else top + value
        o.current[:half, :] = top[:, :group]
        o.current[half:, :] = top[:, group:]
    else:
        mask = onehot(iota((regions * cap, group), 0) == slots)
        both = dot(jnp.concatenate(split3(i.recv[...]), axis=0), mask)
        o.current[...] = both[:scen] + both[scen : 2 * scen] + both[2 * scen :]


def per_device(
    inv_blocks,
    src_amp,
    src_phase,
    line_a,
    line_b,
    line_delay,
    line_yc,
    line_atten,
    hist_ua,
    hist_ub,
    send_node,
    recv_slot,
    conv_par,
    conv_state,
    fault_node,
    fault_step,
    fault_cond,
):
    nblk, blk = inv_blocks.shape[0], inv_blocks.shape[1]
    nreg = nblk * blk
    lines = line_a.shape[1]
    maxd, scen = hist_ua.shape[1], hist_ua.shape[2]
    regions, cap = send_node.shape[1], send_node.shape[2]
    group = recv_slot.shape[1]
    width = regions * cap
    points = 2 * lines + width
    count = lax.axis_size("scen")
    packed = 2 * cap == LANES
    half = scen + 8
    hist_a, hist_b = hist_ua[0], hist_ub[0]
    conv = send_node.reshape(1, width)

    send_shape = (regions, half, LANES) if packed else (half, regions * 2 * cap)
    head = call(
        functools.partial(start_body, (regions, cap, half, scen, group, maxd)),
        "start",
        dict(slots=recv_slot, par=conv_par, state=conv_state, hist=hist_a, delay=line_delay),
        dict(send=(send_shape, F32), into=((2, scen, lines), F32)),
    )
    send = head.send
    if packed:
        recv = lax.all_to_all(send, "region", split_axis=0, concat_axis=0, tiled=True)
    else:
        send = send.reshape(half, 2, regions, cap).transpose(2, 1, 0, 3)
        recv = lax.all_to_all(send, "region", split_axis=0, concat_axis=0, tiled=True)
        recv = recv.transpose(1, 2, 0, 3).reshape(2, half, width)
    into = head.into
    far_in = shifted(into, "region", 1)

    model = call(
        functools.partial(model_body, (nreg, nblk, lines, width, scen)),
        "model",
        dict(
            inv=inv_blocks,
            amp=src_amp.reshape(1, nreg),
            phase=src_phase.reshape(1, nreg),
            end_a=line_a,
            end_b=line_b,
            conv=conv,
            fault_node=fault_node.reshape(1, scen),
            fault_step=fault_step.reshape(1, scen),
            fault_cond=fault_cond.reshape(1, scen),
        ),
        dict(
            spots=((points, blk), jnp.int32),
            zcat=((nreg, 2 * blk), BF16),
            m_high=((points, points), BF16),
            m_low=((points, points), BF16),
            base=((STEPS, nreg), F32),
            base_p=((STEPS, points), F32),
            fault_p=((scen, points), F32),
            fault_z=((scen, blk), F32),
            fault_blk=((scen, blk), jnp.int32),
            fault_base=((scen, blk), F32),
            fault_ratio=((scen, blk), F32),
        ),
        scratch=(
            pltpu.VMEM((1, points + blk), jnp.int32),
            pltpu.VMEM((STEPS * nblk, blk), F32),
            pltpu.VMEM((points + blk, 2 * blk), F32),
        ),
        cost=(4e9, 2e7),
    )

    wave = ((2, scen, lines), F32)
    mades, backs, carry = {}, {}, {}
    squares = far_volts = sent = None
    for pair in range(STEPS // 2):
        t0 = 2 * pair
        final = t0 + 2 >= STEPS
        ins = dict(
            delay=line_delay,
            atten=line_atten,
            admit=line_yc,
            conv=conv,
            recv=recv,
            far_in=far_in,
            m_high=model.m_high,
            m_low=model.m_low,
            base_p=model.base_p,
            fault_p=model.fault_p,
            fault_base=model.fault_base,
            fault_ratio=model.fault_ratio,
            **carry,
        )
        if t0 - maxd < 0:
            ins.update(hist_b=hist_b)
        if pair:
            ins.update(far_volts=far_volts, into_prev=sent)
        first = max(0, pair - 3)
        ins.update(backs={k: v for k, v in backs.items() if k >= first})
        if not final:
            ins.update(made={k: v for k, v in mades.items() if k >= pair - 2})
            if t0 + 2 - maxd < 0:
                ins.update(hist_a=hist_a)
        outs = dict(x=((4 * scen, points), BF16), coef=((2 * scen, LANES), F32))
        if not final:
            outs.update(
                ends=wave,
                out=wave,
                into=wave,
                state=((2, scen, width), F32),
                current=((scen, width), F32),
            )
            if pair:
                outs.update(back=wave)
        else:
            shape = (regions, scen // 2, LANES) if packed else (scen, width)
            outs.update(current=(shape, F32))
        made = call(
            functools.partial(advance_body, (lines, width, scen, cap, maxd, packed), pair),
            "advance",
            ins,
            outs,
        )
        if not final:
            sent, into = into, made.into
            far_in = shifted(into, "region", 1)
            far_volts = shifted(made.ends, "region", -1)
            mades[pair] = made.out
            if pair:
                backs[pair - 1] = made.back
            carry = dict(state=made.state, current=made.current)
        else:
            current = made.current
            if packed:
                returned = lax.all_to_all(
                    current, "region", split_axis=0, concat_axis=0, tiled=True
                )
            else:
                current = current.reshape(scen, regions, cap).transpose(1, 0, 2)
                returned = lax.all_to_all(
                    current, "region", split_axis=0, concat_axis=0, tiled=True
                )
                returned = returned.transpose(1, 0, 2).reshape(scen, width)
        ins = dict(
            x=made.x,
            coef=made.coef,
            spots=model.spots,
            zcat=model.zcat,
            base=model.base,
            fault_z=model.fault_z,
            fault_blk=model.fault_blk,
        )
        if pair:
            ins.update(squares=squares)
        outs = dict(squares=((1, nreg), F32))
        if final:
            outs.update(volts=((scen, nreg), F32))
        full = call(
            functools.partial(full_body, (nblk, points, scen), pair),
            "full",
            ins,
            outs,
            cost=(4e9, 1e7),
        )
        squares = full.squares

    parts = [squares]
    for offset in range(1, count):
        pairs = [(source, source ^ offset) for source in range(count)]
        parts.append(lax.ppermute(squares, "scen", pairs))
    tail = call(
        functools.partial(finish_body, (regions, cap, scen, group, count, packed)),
        "finish",
        dict(slots=recv_slot, recv=returned, parts=parts),
        dict(rms=((1, nreg), F32), current=((scen, group), F32)),
    )
    return full.volts, tail.current, tail.rms.reshape(nreg)


def solution(mesh):
    return jax.shard_map(
        per_device,
        mesh=mesh,
        in_specs=(
            P("region", None, None),
            P("region"),
            P("region"),
            P("region", None),
            P("region", None),
            P("region", None),
            P("region", None),
            P("region", None),
            P("region", None, "scen", None),
            P("region", None, "scen", None),
            P("region", None, None),
            P("region", None),
            P(None, "region"),
            P(None, "scen", "region"),
            P("scen"),
            P("scen"),
            P("scen"),
        ),
        out_specs=(P("scen", "region"), P("scen", "region"), P("region")),
        check_vma=False,
    )
```

```python
import functools
from types import SimpleNamespace as Space

import jax
import jax.numpy as jnp
from jax import lax
from jax.experimental import pallas as pl
from jax.experimental.pallas import tpu as pltpu
from jax.sharding import PartitionSpec as P

STEPS = 8
DMIN = 2
LANES = 128
VMEM = 67043328
ROOM = 1600 << 10
OMEGA = 0.01884955592153876
EPS = 1e-06
F32 = jnp.float32
BF16 = jnp.bfloat16
NN = (((1,), (0,)), ((), ()))
NT = (((1,), (1,)), ((), ()))


def shifted(value, axis, steps):
    count = lax.axis_size(axis)
    pairs = [(source, (source + steps) % count) for source in range(count)]
    return lax.ppermute(value, axis, pairs)


def swapped(value, axis, first):
    count = lax.axis_size(axis)
    pairs = []
    for left in range(first, count, 2):
        right = (left + 1) % count
        pairs += [(left, right), (right, left)]
    return lax.ppermute(value, axis, pairs)


def call(body, name, ins, outs, scratch=(), hbm=None, hbm_outs=None, limit=20 << 20, cost=None):
    leaves, tree = jax.tree.flatten(ins)
    far, far_outs = dict(hbm or {}), dict(hbm_outs or {})
    names = [list(far), list(outs), list(far_outs)]
    sizes = [len(leaves)] + [len(group) for group in names] + [len(far), len(far_outs)]
    ends = [sum(sizes[:k]) for k in range(len(sizes) + 1)]
    count = len(far) + len(far_outs)

    def kernel(*refs):
        near, sources, near_outs, targets, held, made = [
            refs[ends[k] : ends[k + 1]] for k in range(len(sizes))
        ]
        rest = refs[ends[-1] :]
        arriving, leaving, pending = {}, {}, []
        if count:
            sems, rest = rest[0], rest[1:]
            for k, key in enumerate(far):
                arriving[key] = pltpu.make_async_copy(sources[k], held[k], sems.at[k])
                arriving[key].start()
            for k, key in enumerate(far_outs):
                leaving[key] = pltpu.make_async_copy(made[k], targets[k], sems.at[len(far) + k])
        i = Space(**jax.tree.unflatten(tree, near), **dict(zip(far, held)))
        o = Space(**dict(zip(outs, near_outs)), **dict(zip(far_outs, made)))

        def flush(key):
            pending.append(leaving.pop(key))
            pending[-1].start()

        i.ready = lambda *keys: [arriving.pop(key).wait() for key in keys]
        o.flush = flush
        body(i, o, *rest)
        for key in list(leaving):
            flush(key)
        for copy in pending:
            copy.wait()

    buffers = [pltpu.VMEM(value.shape, value.dtype) for value in far.values()]
    buffers += [pltpu.VMEM(*shape) for shape in far_outs.values()]
    if count:
        buffers.append(pltpu.SemaphoreType.DMA((count,)))
    every = list(outs.values()) + list(far_outs.values())
    near_spec, far_spec = (pl.BlockSpec(memory_space=space) for space in (pltpu.VMEM, pltpu.HBM))
    flops, moved = cost or (1e9, 4e6)
    results = pl.pallas_call(
        kernel,
        name=name,
        out_shape=[jax.ShapeDtypeStruct(*shape) for shape in every],
        in_specs=[near_spec] * len(leaves) + [far_spec] * len(far),
        out_specs=[near_spec] * len(outs) + [far_spec] * len(far_outs),
        scratch_shapes=buffers + list(scratch),
        compiler_params=pltpu.CompilerParams(vmem_limit_bytes=limit),
        cost_estimate=pl.CostEstimate(
            flops=int(flops), bytes_accessed=int(moved), transcendentals=0
        ),
    )(*leaves, *far.values())
    return Space(**dict(zip(names[1] + names[2], results)))


def iota(shape, dim):
    return lax.broadcasted_iota(jnp.int32, shape, dim)


def onehot(mask):
    return jnp.where(mask, 1.0, 0.0).astype(BF16)


def dot(left, right, dims=NN):
    return lax.dot_general(left, right, dims, preferred_element_type=F32)


def split2(value):
    high = value.astype(BF16)
    return high, (value - high.astype(F32)).astype(BF16)


def split3(value):
    high, rest = value.astype(BF16), value
    rest = value - high.astype(F32)
    mid = rest.astype(BF16)
    return high, mid, (rest - mid.astype(F32)).astype(BF16)


def product3(left, right_high, right_low, dims=NN):
    rows = left.shape[0]
    high, low = split2(left)
    both = dot(jnp.concatenate([high, low], axis=0), right_high, dims)
    return both[:rows] + both[rows:] + dot(high, right_low, dims)


def as_column(row, size):
    wide = jnp.broadcast_to(row, (size, size))
    return jnp.sum(
        jnp.where(iota((size, size), 0) == iota((size, size), 1), wide, 0.0), axis=1, keepdims=True
    )


def pick(wave, delays, instant, maxd):
    total = None
    for lag in range(DMIN, maxd + 1):
        term = jnp.where(delays == lag, wave(instant - lag), 0.0)
        total = term if total is None else total + term
    return total


def start_body(sizes, i, o):
    regions, cap, half, scen, group, maxd = sizes
    packed = 2 * cap == LANES
    i.ready("slots", "par", "state")
    slots = i.slots[...]
    rows = iota((regions * 2 * cap, group), 0)
    if packed:
        target = (slots // cap) * (2 * cap) + slots % cap
        moved = target + cap
    else:
        target = slots
        moved = slots + regions * cap
    left, right = onehot(rows == target), onehot(rows == moved)
    pad = jnp.zeros((half - scen - 6, group), F32)
    upper = jnp.concatenate([i.state[0], i.par[...], pad], axis=0)
    lower = jnp.concatenate([i.state[1], jnp.zeros((half - scen, group), F32)], axis=0)
    buffer = None
    for part, mask in ((upper, left), (lower, right)):
        both = dot(jnp.concatenate(split3(part), axis=0), mask, NT)
        value = both[:half] + both[half : 2 * half] + both[2 * half :]
        buffer = value if buffer is None else buffer + value
    if packed:
        for region in range(regions):
            o.send[region] = buffer[:, region * LANES : (region + 1) * LANES]
    else:
        o.send[...] = buffer
    o.flush("send")
    i.ready("hist", "delay")
    delays = i.delay[...]
    for step in range(2):
        o.into[step] = pick(lambda t: i.hist[0, t + maxd], delays, step, maxd)


def sources(amp, phase):
    instant = iota((STEPS, amp.shape[1]), 0).astype(F32)
    return amp * jnp.cos(OMEGA * instant + phase)


def rows_body(sizes, i, o, place, source_rows):
    nreg, nblk, lines, regions, cap, scen = sizes
    blk = LANES
    width = regions * cap
    points = 2 * lines + width
    whole = points + blk
    i.ready("end_a", "end_b", "conv", "fault_node")
    o.row[...] = jnp.full((1, whole), -1, jnp.int32)
    o.row[:, 0:lines] = i.end_a[...]
    o.row[:, lines : 2 * lines] = i.end_b[...]
    for group in range(regions):
        start = 2 * lines + group * cap
        o.row[:, start : start + cap] = i.conv[0, group : group + 1, :]
    region = lax.axis_index("region")
    fault = i.fault_node[...] - region * nreg
    fault = jnp.where((fault >= 0) & (fault < nreg), fault, -1)
    o.row[:, points : points + scen] = fault
    row = o.row[...]
    column = jnp.transpose(jnp.broadcast_to(row.astype(F32), (blk, whole))).astype(jnp.int32)
    o.column[...] = column
    lane = iota((whole, blk), 1)
    for k in range(nblk):
        place[:, k * blk : (k + 1) * blk] = onehot(o.column[...] == lane + k * blk)
    i.ready("inv")
    z_high, z_low = split2(i.inv[...].reshape(nreg, blk))
    o.zcat[:, 0:blk] = z_high
    o.zcat[:, blk:] = z_low
    o.flush("zcat")
    o.rows[...] = dot(place[...], o.zcat[...]).astype(BF16)
    i.ready("amp", "phase")
    source = sources(i.amp[...], i.phase[...])
    for k in range(nblk):
        source_rows[k * STEPS : (k + 1) * STEPS, :] = source[:, k * blk : (k + 1) * blk]
    spread = product3(source_rows[...], o.rows[:, :blk], o.rows[:, blk:], NT)
    row_blk = row >> 7
    at_points = jnp.zeros((STEPS, whole), F32)
    for k in range(nblk):
        at_points = at_points + jnp.where(row_blk == k, spread[k * STEPS : (k + 1) * STEPS], 0.0)
    o.base_p[...] = at_points[:, :points]
    tail = jnp.concatenate(
        [at_points[:, points:], jnp.zeros((blk - STEPS, blk), F32)], axis=0
    )
    o.fault_base[...] = jnp.transpose(tail)[:scen]
    fault_rows = o.rows[points : points + scen, :].astype(F32)
    fault_z = fault_rows[:, :blk] + fault_rows[:, blk:]
    o.fault_z[...] = fault_z
    self_imp = jnp.sum(
        jnp.where(iota((scen, blk), 1) == (column[points : points + scen] & 127), fault_z, 0.0),
        axis=1,
        keepdims=True,
    )
    i.ready("fault_cond", "fault_step")
    cond = as_column(i.fault_cond[...], scen)
    closes = as_column(i.fault_step[...].astype(F32), scen)
    ratio = cond / (1.0 + cond * self_imp)
    o.fault_ratio[...] = jnp.where(
        closes <= iota((scen, blk), 1).astype(F32), jnp.broadcast_to(ratio, (scen, blk)), 0.0
    )


def between_body(sizes, i, o):
    points, scen = sizes
    blk = LANES
    row = i.row[:, :points]
    row_blk = row >> 7
    inside = onehot(iota((blk, points), 0) == (row & 127))
    for k in range(points // blk):
        here = slice(k * blk, (k + 1) * blk)
        same = (i.column[here, 0:1] >> 7) == row_blk
        both = dot(jnp.concatenate([i.rows[here, :blk], i.rows[here, blk:]], axis=0), inside)
        o.m_high[here, :] = jnp.where(same, both[:blk], 0.0).astype(BF16)
        o.m_low[here, :] = jnp.where(same, both[blk:], 0.0).astype(BF16)
    here = slice(points, points + scen)
    both = dot(jnp.concatenate([i.rows[here, :blk], i.rows[here, blk:]], axis=0), inside)
    same = (i.column[here, 0:1] >> 7) == row_blk
    o.fault_p[...] = jnp.where(same, both[:scen] + both[scen:], 0.0)


def advance_body(sizes, pair, i, o):
    lines, width, scen, cap, maxd, packed = sizes
    t0 = 2 * pair
    delays = i.delay[...]
    scale = i.atten[...]
    twice = 2.0 * i.admit[...]
    last = STEPS - 1

    even = lax.rem(lax.axis_index("region"), 2) == 0
    fresh = {}
    if pair:
        far_in = [jnp.where(even, i.swap_b[j], i.swap_a[j]) for j in range(2)]
        for j in range(2):
            far_volts = jnp.where(even, i.swap_a[j], i.swap_b[j])
            fresh[t0 - 2 + j] = scale * (twice * far_volts - i.into_prev[j])
            if hasattr(o, "back"):
                o.back[j] = fresh[t0 - 2 + j]
    else:
        far_in = [i.far_in[j] for j in range(2)]

    def back(t):
        if t in fresh:
            return fresh[t]
        if t < 0:
            return i.hist_b[0, t + maxd]
        return i.backs[t // 2][t % 2]

    made = {}

    def out(t):
        if t in made:
            return made[t]
        if t < 0:
            return i.hist_a[0, t + maxd]
        return i.made[t // 2][t % 2]

    live = i.row[:, 2 * lines : 2 * lines + width] >= 0
    if packed:
        low = iota((1, LANES), 1) < cap
        params = []
        for row in range(6):
            pieces = []
            for j in range(width // LANES):
                one = i.recv[2 * j][scen + row : scen + row + 1, :]
                two = i.recv[2 * j + 1][scen + row : scen + row + 1, :]
                pieces.append(jnp.where(low, one, pltpu.roll(two, cap, 1)))
            params.append(jnp.concatenate(pieces, axis=1))
    else:
        params = [i.recv[0, scen + row : scen + row + 1, :] for row in range(6)]
    params[5] = jnp.where(live, params[5], 1.0)

    def drive(second):
        return params[5] * jnp.tanh((params[4] + second) / params[5])

    if pair:
        first, second, current = i.state[0], i.state[1], i.current[...]
    else:
        if packed:
            ups, downs = [], []
            for j in range(width // LANES):
                one, two = i.recv[2 * j][:scen], i.recv[2 * j + 1][:scen]
                ups.append(jnp.where(low, one, pltpu.roll(two, cap, 1)))
                downs.append(jnp.where(low, pltpu.roll(one, cap, 1), two))
            first, second = jnp.concatenate(ups, axis=1), jnp.concatenate(downs, axis=1)
        else:
            first, second = i.recv[0, :scen], i.recv[1, :scen]
        current = drive(second)

    fault_p = i.fault_p[...]
    ends = 2 * lines
    sides = []
    arrivals = [pick(back, delays, t0 + j, maxd) for j in range(2)]
    waves = [jnp.concatenate([arrivals[j], far_in[j]], axis=1) for j in range(2)]
    pairs = split2(jnp.concatenate(waves, axis=0))
    for part in range(2):
        o.x[part * 2 * scen : (part + 1) * 2 * scen, :ends] = pairs[part]
    both = dot(jnp.concatenate(pairs, axis=0), i.m_high[:ends, :])
    of_lines = both[: 2 * scen] + both[2 * scen :] + dot(pairs[0], i.m_low[:ends, :])
    for j in range(2):
        t = t0 + j
        into = arrivals[j]
        x = jnp.concatenate([waves[j], current], axis=1)
        high, low_part = split2(current)
        o.x[j * scen : (j + 1) * scen, ends:] = high
        o.x[(2 + j) * scen : (3 + j) * scen, ends:] = low_part
        both = dot(jnp.concatenate([high, low_part], axis=0), i.m_high[ends:, :])
        volts = both[:scen] + both[scen:] + dot(high, i.m_low[ends:, :])
        volts = volts + of_lines[j * scen : (j + 1) * scen] + i.base_p[t : t + 1, :]
        at_fault = i.fault_base[:, t : t + 1] + jnp.sum(x * fault_p, axis=1, keepdims=True)
        coef = i.fault_ratio[:, t : t + 1] * at_fault
        o.coef[j * scen : (j + 1) * scen, :] = jnp.broadcast_to(coef, (scen, LANES))
        volts = volts - fault_p * coef
        if t <= last - DMIN:
            made[t] = scale * (twice * volts[:, :lines] - into)
            sides.append(volts[:, lines : 2 * lines])
            if hasattr(o, "out"):
                o.out[j] = made[t]
        node = volts[:, 2 * lines :]
        first = params[1] * first + params[2] * (params[0] - node)
        second = second + params[3] * (first - second)
        current = drive(second)
    if hasattr(o, "into"):
        for j in range(2):
            onward = pick(out, delays, t0 + 2 + j, maxd)
            o.into[j] = onward
            o.swap_a[j] = jnp.where(even, onward, sides[j])
            o.swap_b[j] = jnp.where(even, sides[j], onward)
    if hasattr(o, "state"):
        o.state[0] = first
        o.state[1] = second
    if t0 + 2 < STEPS or not packed:
        o.current[...] = current
    else:
        half = scen // 2
        for j in range(width // LANES):
            mine = current[:, j * LANES : (j + 1) * LANES]
            top, bottom = mine[:half], mine[half:]
            o.current[2 * j] = jnp.where(low, top, pltpu.roll(bottom, cap, 1))
            o.current[2 * j + 1] = jnp.where(low, pltpu.roll(top, cap, 1), bottom)


def full_body(sizes, pair, i, o):
    nblk, points, scen = sizes
    blk = LANES
    t0 = 2 * pair
    fault_z = i.fault_z[...]
    fault_blk = i.column[points : points + scen, :] >> 7
    x = i.x[...]
    coef = i.coef[...]
    lane = iota((points, blk), 1)
    if pair:
        all_base = i.base
    else:
        all_base = o.base
        source = sources(i.amp[...], i.phase[...])
        for k in range(nblk):
            here = slice(k * blk, (k + 1) * blk)
            z = i.zcat[here, :]
            o.base[:, here] = product3(source[:, here], z[:, :blk], z[:, blk:])
    for k in range(0, nblk, 2):
        mine = jnp.concatenate(
            [onehot(i.column[:points, :] == lane + (k + j) * blk) for j in range(2)], axis=1
        )
        both = dot(x, mine)
        inject = both[: 2 * scen] + both[2 * scen :]
        for j in range(2):
            here = slice((k + j) * blk, (k + j + 1) * blk)
            z = i.zcat[here, :]
            volts = product3(inject[:, j * blk : (j + 1) * blk], z[:, :blk], z[:, blk:])
            base = [
                jnp.broadcast_to(all_base[t0 + m : t0 + m + 1, here], (scen, blk))
                for m in range(2)
            ]
            column = jnp.where(fault_blk == k + j, fault_z, 0.0)
            volts = volts + jnp.concatenate(base, axis=0)
            volts = volts - jnp.concatenate([column, column], axis=0) * coef
            total = jnp.sum(volts * volts, axis=0, keepdims=True)
            if hasattr(i, "squares"):
                total = total + i.squares[:, here]
            o.squares[:, here] = total
            if hasattr(o, "volts"):
                o.volts[:, here] = volts[scen:]


def finish_body(sizes, i, o):
    regions, cap, scen, group, count, packed = sizes
    parts = [i.parts[k][...] for k in range(count)]
    while len(parts) > 1:
        parts = [parts[k] + parts[k + 1] for k in range(0, len(parts), 2)]
    o.rms[...] = jnp.sqrt(parts[0] / (scen * count * STEPS) + EPS)
    slots = i.slots[...]
    if packed:
        half = scen // 2
        lane = iota((LANES, group), 0)
        top = bottom = None
        for region in range(regions):
            left = onehot((lane < cap) & (slots == region * cap + lane))
            right = onehot((lane >= cap) & (slots == (region - 1) * cap + lane))
            both = dot(
                jnp.concatenate(split3(i.recv[region]), axis=0),
                jnp.concatenate([left, right], axis=1),
            )
            value = both[:half] + both[half : 2 * half] + both[2 * half :]
            top = value if top is None else top + value
        o.current[:half, :] = top[:, :group]
        o.current[half:, :] = top[:, group:]
    else:
        mask = onehot(iota((regions * cap, group), 0) == slots)
        both = dot(jnp.concatenate(split3(i.recv[...]), axis=0), mask)
        o.current[...] = both[:scen] + both[scen : 2 * scen] + both[2 * scen :]


def per_device(
    inv_blocks,
    src_amp,
    src_phase,
    line_a,
    line_b,
    line_delay,
    line_yc,
    line_atten,
    hist_ua,
    hist_ub,
    send_node,
    recv_slot,
    conv_par,
    conv_state,
    fault_node,
    fault_step,
    fault_cond,
):
    nblk, blk = inv_blocks.shape[0], inv_blocks.shape[1]
    nreg = nblk * blk
    lines = line_a.shape[1]
    maxd, scen = hist_ua.shape[1], hist_ua.shape[2]
    regions, cap = send_node.shape[1], send_node.shape[2]
    group = recv_slot.shape[1]
    width = regions * cap
    points = 2 * lines + width
    count = lax.axis_size("scen")
    packed = 2 * cap == LANES
    half = scen + 8

    send_shape = (regions, half, LANES) if packed else (half, regions * 2 * cap)
    head = call(
        functools.partial(start_body, (regions, cap, half, scen, group, maxd)),
        "start",
        {},
        {},
        hbm_outs=dict(send=(send_shape, F32), into=((2, scen, lines), F32)),
        limit=VMEM,
        hbm=dict(slots=recv_slot, par=conv_par, state=conv_state, hist=hist_ua, delay=line_delay),
    )
    send = head.send
    if packed:
        recv = lax.all_to_all(send, "region", split_axis=0, concat_axis=0, tiled=True)
    else:
        send = send.reshape(half, 2, regions, cap).transpose(2, 1, 0, 3)
        recv = lax.all_to_all(send, "region", split_axis=0, concat_axis=0, tiled=True)
        recv = recv.transpose(1, 2, 0, 3).reshape(2, half, width)
    into = head.into
    far_in = shifted(into, "region", 1)

    whole = points + blk
    model = call(
        functools.partial(rows_body, (nreg, nblk, lines, regions, cap, scen)),
        "rows",
        {},
        dict(
            row=((1, whole), jnp.int32),
            column=((whole, blk), jnp.int32),
            rows=((whole, 2 * blk), BF16),
            base_p=((STEPS, points), F32),
            fault_z=((scen, blk), F32),
            fault_base=((scen, blk), F32),
            fault_ratio=((scen, blk), F32),
        ),
        hbm_outs=dict(zcat=((nreg, 2 * blk), BF16)),
        hbm=dict(
            end_a=line_a,
            end_b=line_b,
            conv=send_node,
            fault_node=fault_node.reshape(1, scen),
            inv=inv_blocks,
            amp=src_amp.reshape(1, nreg),
            phase=src_phase.reshape(1, nreg),
            fault_step=fault_step.reshape(1, scen),
            fault_cond=fault_cond.reshape(1, scen),
        ),
        scratch=(pltpu.VMEM((whole, nreg), BF16), pltpu.VMEM((STEPS * nblk, blk), F32)),
        limit=VMEM - ROOM,
        cost=(4e9, 2e7),
    )
    matrix = call(
        functools.partial(between_body, (points, scen)),
        "between",
        dict(row=model.row, column=model.column, rows=model.rows, recv=recv),
        dict(
            m_high=((points, points), BF16),
            m_low=((points, points), BF16),
            fault_p=((scen, points), F32),
        ),
    )

    wave = ((2, scen, lines), F32)
    mades, backs, carry = {}, {}, {}
    squares = swap_a = swap_b = sent = base = None
    for pair in range(STEPS // 2):
        t0 = 2 * pair
        final = t0 + 2 >= STEPS
        ins = dict(
            delay=line_delay,
            atten=line_atten,
            admit=line_yc,
            row=model.row,
            recv=recv,
            m_high=matrix.m_high,
            m_low=matrix.m_low,
            base_p=model.base_p,
            fault_p=matrix.fault_p,
            fault_base=model.fault_base,
            fault_ratio=model.fault_ratio,
            **carry,
        )
        if t0 - maxd < 0:
            ins.update(hist_b=hist_ub)
        if pair:
            ins.update(swap_a=swap_a, swap_b=swap_b, into_prev=sent)
        else:
            ins.update(far_in=far_in)
        first = max(0, pair - 3)
        ins.update(backs={k: v for k, v in backs.items() if k >= first})
        if not final:
            ins.update(made={k: v for k, v in mades.items() if k >= pair - 2})
            if t0 + 2 - maxd < 0:
                ins.update(hist_a=hist_ua)
        outs = dict(x=((4 * scen, points), BF16), coef=((2 * scen, LANES), F32))
        if not final:
            outs.update(
                swap_a=wave,
                swap_b=wave,
                out=wave,
                into=wave,
                state=((2, scen, width), F32),
                current=((scen, width), F32),
            )
            if pair:
                outs.update(back=wave)
        else:
            shape = (regions, scen // 2, LANES) if packed else (scen, width)
            outs.update(current=(shape, F32))
        made = call(
            functools.partial(advance_body, (lines, width, scen, cap, maxd, packed), pair),
            "advance",
            ins,
            outs,
        )
        if not final:
            sent, into = into, made.into
            swap_a = swapped(made.swap_a, "region", 0)
            swap_b = swapped(made.swap_b, "region", 1)
            mades[pair] = made.out
            if pair:
                backs[pair - 1] = made.back
            carry = dict(state=made.state, current=made.current)
        else:
            current = made.current
            if packed:
                returned = lax.all_to_all(current, "region", split_axis=0, concat_axis=0, tiled=True)
            else:
                current = current.reshape(scen, regions, cap).transpose(1, 0, 2)
                returned = lax.all_to_all(current, "region", split_axis=0, concat_axis=0, tiled=True)
                returned = returned.transpose(1, 0, 2).reshape(scen, width)
        ins = dict(
            x=made.x,
            coef=made.coef,
            column=model.column,
            zcat=model.zcat,
            fault_z=model.fault_z,
        )
        if pair:
            ins.update(squares=squares, base=base)
        else:
            ins.update(amp=src_amp.reshape(1, nreg), phase=src_phase.reshape(1, nreg))
        outs = dict(squares=((1, nreg), F32))
        if final:
            outs.update(volts=((scen, nreg), F32))
        if not pair:
            outs.update(base=((STEPS, nreg), F32))
        full = call(
            functools.partial(full_body, (nblk, points, scen), pair),
            "full",
            ins,
            outs,
            cost=(4e9, 1e7),
        )
        squares = full.squares
        if not pair:
            base = full.base

    parts = [squares]
    for offset in range(1, count):
        pairs = [(source, source ^ offset) for source in range(count)]
        parts.append(lax.ppermute(squares, "scen", pairs))
    tail = call(
        functools.partial(finish_body, (regions, cap, scen, group, count, packed)),
        "finish",
        dict(slots=recv_slot, recv=returned, parts=parts),
        dict(rms=((1, nreg), F32), current=((scen, group), F32)),
    )
    return full.volts, tail.current, tail.rms.reshape(nreg)


def solution(mesh):
    return jax.shard_map(
        per_device,
        mesh=mesh,
        in_specs=(
            P("region", None, None),
            P("region"),
            P("region"),
            P("region", None),
            P("region", None),
            P("region", None),
            P("region", None),
            P("region", None),
            P("region", None, "scen", None),
            P("region", None, "scen", None),
            P("region", None, None),
            P("region", None),
            P(None, "region"),
            P(None, "scen", "region"),
            P("scen"),
            P("scen"),
            P("scen"),
        ),
        out_specs=(P("scen", "region"), P("scen", "region"), P("region")),
        check_vma=False,
    )
```

```python
import functools
from types import SimpleNamespace as Space

import jax
import jax.numpy as jnp
from jax import lax
from jax.experimental import pallas as pl
from jax.experimental.pallas import tpu as pltpu
from jax.sharding import PartitionSpec as P

STEPS = 8
DMIN = 2
LANES = 128
VMEM = 67043328
ROOM = 30000 << 10
WIDE = 4
OMEGA = 0.01884955592153876
EPS = 1e-06
F32 = jnp.float32
BF16 = jnp.bfloat16
NN = (((1,), (0,)), ((), ()))
NT = (((1,), (1,)), ((), ()))


def shifted(value, axis, steps):
    count = lax.axis_size(axis)
    pairs = [(source, (source + steps) % count) for source in range(count)]
    return lax.ppermute(value, axis, pairs)


def swapped(value, axis, first):
    count = lax.axis_size(axis)
    pairs = []
    for left in range(first, count, 2):
        right = (left + 1) % count
        pairs += [(left, right), (right, left)]
    return lax.ppermute(value, axis, pairs)


def call(body, name, ins, outs, scratch=(), hbm=None, hbm_outs=None, limit=20 << 20, cost=None):
    leaves, tree = jax.tree.flatten(ins)
    far, far_outs = dict(hbm or {}), dict(hbm_outs or {})
    names = [list(far), list(outs), list(far_outs)]
    sizes = [len(leaves)] + [len(group) for group in names] + [len(far), len(far_outs)]
    ends = [sum(sizes[:k]) for k in range(len(sizes) + 1)]
    count = len(far) + len(far_outs)

    def kernel(*refs):
        near, sources, near_outs, targets, held, made = [
            refs[ends[k] : ends[k + 1]] for k in range(len(sizes))
        ]
        rest = refs[ends[-1] :]
        arriving, leaving, pending = {}, {}, []
        if count:
            sems, rest = rest[0], rest[1:]
            for k, key in enumerate(far):
                arriving[key] = pltpu.make_async_copy(sources[k], held[k], sems.at[k])
                arriving[key].start()
            for k, key in enumerate(far_outs):
                leaving[key] = pltpu.make_async_copy(made[k], targets[k], sems.at[len(far) + k])
        i = Space(**jax.tree.unflatten(tree, near), **dict(zip(far, held)))
        o = Space(**dict(zip(outs, near_outs)), **dict(zip(far_outs, made)))

        def flush(key):
            pending.append(leaving.pop(key))
            pending[-1].start()

        i.ready = lambda *keys: [arriving.pop(key).wait() for key in keys]
        o.flush = flush
        body(i, o, *rest)
        for key in list(leaving):
            flush(key)
        for copy in pending:
            copy.wait()

    buffers = [pltpu.VMEM(value.shape, value.dtype) for value in far.values()]
    buffers += [pltpu.VMEM(*shape) for shape in far_outs.values()]
    if count:
        buffers.append(pltpu.SemaphoreType.DMA((count,)))
    every = list(outs.values()) + list(far_outs.values())
    near_spec, far_spec = (pl.BlockSpec(memory_space=space) for space in (pltpu.VMEM, pltpu.HBM))
    flops, moved = cost or (1e9, 4e6)
    results = pl.pallas_call(
        kernel,
        name=name,
        out_shape=[jax.ShapeDtypeStruct(*shape) for shape in every],
        in_specs=[near_spec] * len(leaves) + [far_spec] * len(far),
        out_specs=[near_spec] * len(outs) + [far_spec] * len(far_outs),
        scratch_shapes=buffers + list(scratch),
        compiler_params=pltpu.CompilerParams(vmem_limit_bytes=limit),
        cost_estimate=pl.CostEstimate(
            flops=int(flops), bytes_accessed=int(moved), transcendentals=0
        ),
    )(*leaves, *far.values())
    return Space(**dict(zip(names[1] + names[2], results)))


def iota(shape, dim):
    return lax.broadcasted_iota(jnp.int32, shape, dim)


def onehot(mask):
    return jnp.where(mask, 1.0, 0.0).astype(BF16)


def owned(mark, k):
    return jnp.where(mark == jnp.asarray(k, BF16), jnp.asarray(1, BF16), jnp.asarray(0, BF16))


def owner_of(mark):
    return jnp.max(mark.astype(F32), axis=1, keepdims=True)


def dot(left, right, dims=NN):
    return lax.dot_general(left, right, dims, preferred_element_type=F32)


def split2(value):
    high = value.astype(BF16)
    return high, (value - high.astype(F32)).astype(BF16)


def split3(value):
    high, rest = value.astype(BF16), value
    rest = value - high.astype(F32)
    mid = rest.astype(BF16)
    return high, mid, (rest - mid.astype(F32)).astype(BF16)


def product3(left, right_high, right_low, dims=NN):
    rows = left.shape[0]
    high, low = split2(left)
    both = dot(jnp.concatenate([high, low], axis=0), right_high, dims)
    return both[:rows] + both[rows:] + dot(high, right_low, dims)


def as_column(row, size):
    wide = jnp.broadcast_to(row, (size, size))
    return jnp.sum(
        jnp.where(iota((size, size), 0) == iota((size, size), 1), wide, 0.0), axis=1, keepdims=True
    )


def pick(wave, delays, instant, maxd):
    total = None
    for lag in range(DMIN, maxd + 1):
        term = jnp.where(delays == lag, wave(instant - lag), 0.0)
        total = term if total is None else total + term
    return total


def start_body(sizes, i, o):
    regions, cap, half, scen, group, maxd, lines, nreg = sizes
    packed = 2 * cap == LANES
    i.ready("slots", "par", "state")
    slots = i.slots[...]
    rows = iota((regions * 2 * cap, group), 0)
    if packed:
        target = (slots // cap) * (2 * cap) + slots % cap
        moved = target + cap
    else:
        target = slots
        moved = slots + regions * cap
    left, right = onehot(rows == target), onehot(rows == moved)
    pad = jnp.zeros((half - scen - 6, group), F32)
    upper = jnp.concatenate([i.state[0], i.par[...], pad], axis=0)
    lower = jnp.concatenate([i.state[1], jnp.zeros((half - scen, group), F32)], axis=0)
    buffer = None
    for part, mask in ((upper, left), (lower, right)):
        both = dot(jnp.concatenate(split3(part), axis=0), mask, NT)
        value = both[:half] + both[half : 2 * half] + both[2 * half :]
        buffer = value if buffer is None else buffer + value
    if packed:
        for region in range(regions):
            o.send[region] = buffer[:, region * LANES : (region + 1) * LANES]
    else:
        o.send[...] = buffer
    o.flush("send")
    i.ready("hist", "delay")
    delays = i.delay[...]
    for step in range(2):
        o.into[step] = pick(lambda t: i.hist[0, t + maxd], delays, step, maxd)
    o.flush("into")
    i.ready("end_a", "end_b", "conv", "fault_node", "fault_step", "fault_cond", "amp", "phase")
    pack = o.pack
    pack[0:1, :] = i.amp[...]
    pack[1:2, :] = i.phase[...]
    pack[2:3, 0:scen] = i.fault_step[...].astype(F32)
    pack[3:4, 0:scen] = i.fault_cond[...]
    points = 2 * lines + regions * cap
    pack[4:5, 0 : points + LANES] = jnp.full((1, points + LANES), -1.0, F32)
    pack[4:5, 0:lines] = i.end_a[...].astype(F32)
    pack[4:5, lines : 2 * lines] = i.end_b[...].astype(F32)
    for index in range(regions):
        first = 2 * lines + index * cap
        pack[4:5, first : first + cap] = i.conv[0, index : index + 1, :].astype(F32)
    fault = i.fault_node[...] - lax.axis_index("region") * nreg
    fault = jnp.where((fault >= 0) & (fault < nreg), fault, -1)
    pack[4:5, points : points + scen] = fault.astype(F32)


def sources(amp, phase):
    instant = iota((STEPS, amp.shape[1]), 0).astype(F32)
    return amp * jnp.cos(OMEGA * instant + phase)


def rows_body(sizes, i, o, place, zcat, source_rows):
    nreg, nblk, lines, regions, cap, scen = sizes
    blk = LANES
    width = regions * cap
    points = 2 * lines + width
    whole = points + blk
    whole_row = i.pack[4:5, 0:whole]
    row = whole_row.astype(jnp.int32)
    o.row[...] = row
    column = jnp.transpose(jnp.broadcast_to(whole_row, (blk, whole))).astype(jnp.int32)
    here = (column & 127) == iota((whole, blk), 1)
    o.mark[...] = jnp.where(here, (column >> 7).astype(F32), -1.0).astype(BF16)
    for k in range(nblk):
        place[:, k * blk : (k + 1) * blk] = owned(o.mark[...], k)
    i.ready("inv")
    z_high, z_low = split2(i.inv[...].reshape(nreg, blk))
    zcat[:, 0:blk] = z_high
    zcat[:, blk:] = z_low
    o.rows[...] = dot(place[...], zcat[...]).astype(BF16)
    source = sources(i.pack[0:1, :], i.pack[1:2, :])
    for k in range(nblk):
        source_rows[k * STEPS : (k + 1) * STEPS, :] = source[:, k * blk : (k + 1) * blk]
    spread = product3(source_rows[...], o.rows[:, :blk], o.rows[:, blk:], NT)
    row_blk = row >> 7
    at_points = jnp.zeros((STEPS, whole), F32)
    for k in range(nblk):
        at_points = at_points + jnp.where(row_blk == k, spread[k * STEPS : (k + 1) * STEPS], 0.0)
    o.base_p[...] = at_points[:, :points]
    tail = jnp.concatenate(
        [at_points[:, points:], jnp.zeros((blk - STEPS, blk), F32)], axis=0
    )
    o.fault_base[...] = jnp.transpose(tail)[:scen]
    fault_rows = o.rows[points : points + scen, :].astype(F32)
    fault_z = fault_rows[:, :blk] + fault_rows[:, blk:]
    o.fault_z[...] = fault_z
    self_imp = jnp.sum(
        jnp.where(iota((scen, blk), 1) == (column[points : points + scen] & 127), fault_z, 0.0),
        axis=1,
        keepdims=True,
    )
    cond = as_column(i.pack[3:4, 0:scen], scen)
    closes = as_column(i.pack[2:3, 0:scen], scen)
    ratio = cond / (1.0 + cond * self_imp)
    o.fault_ratio[...] = jnp.where(
        closes <= iota((scen, blk), 1).astype(F32), jnp.broadcast_to(ratio, (scen, blk)), 0.0
    )


def between_body(points, scen, i, o):
    blk = LANES
    row = i.row[:, :points]
    row_blk = (row >> 7).astype(F32)
    inside = onehot(iota((blk, points), 0) == (row & 127))
    for k in range(points // blk):
        here = slice(k * blk, (k + 1) * blk)
        same = owner_of(i.mark[here, :]) == row_blk
        both = dot(jnp.concatenate([i.rows[here, :blk], i.rows[here, blk:]], axis=0), inside)
        o.m_high[here, :] = jnp.where(same, both[:blk], 0.0).astype(BF16)
        o.m_low[here, :] = jnp.where(same, both[blk:], 0.0).astype(BF16)
    here = slice(points, points + scen)
    both = dot(jnp.concatenate([i.rows[here, :blk], i.rows[here, blk:]], axis=0), inside)
    same = owner_of(i.mark[here, :]) == row_blk
    o.fault_p[...] = jnp.where(same, both[:scen] + both[scen:], 0.0)


def advance_body(sizes, pair, i, o):
    lines, width, scen, cap, maxd, packed = sizes
    t0 = 2 * pair
    delays = i.delay[...]
    scale = i.atten[...]
    twice = 2.0 * i.admit[...]
    last = STEPS - 1

    even = lax.rem(lax.axis_index("region"), 2) == 0
    fresh = {}
    if pair:
        far_in = [jnp.where(even, i.swap_far[j], i.swap_near[j]) for j in range(2)]
        for j in range(2):
            far_volts = jnp.where(even, i.swap_near[j], i.swap_far[j])
            fresh[t0 - 2 + j] = scale * (twice * far_volts - i.into_prev[j])
            if hasattr(o, "back"):
                o.back[j] = fresh[t0 - 2 + j]
    else:
        far_in = [i.far_in[j] for j in range(2)]

    def back(t):
        if t in fresh:
            return fresh[t]
        if t < 0:
            return i.hist_b[0, t + maxd]
        return i.backs[t // 2][t % 2]

    made = {}

    def out(t):
        if t in made:
            return made[t]
        if t < 0:
            return i.hist_a[0, t + maxd]
        return i.made[t // 2][t % 2]

    points = 2 * lines + width
    known = i if pair else o
    if not pair:
        between_body(points, scen, i, o)
    live = i.row[:, 2 * lines : 2 * lines + width] >= 0
    if packed:
        low = iota((1, LANES), 1) < cap
        params = []
        for row in range(6):
            pieces = []
            for j in range(width // LANES):
                one = i.recv[2 * j][scen + row : scen + row + 1, :]
                two = i.recv[2 * j + 1][scen + row : scen + row + 1, :]
                pieces.append(jnp.where(low, one, pltpu.roll(two, cap, 1)))
            params.append(jnp.concatenate(pieces, axis=1))
    else:
        params = [i.recv[0, scen + row : scen + row + 1, :] for row in range(6)]
    params[5] = jnp.where(live, params[5], 1.0)

    def drive(second):
        return params[5] * jnp.tanh((params[4] + second) / params[5])

    if pair:
        first, second, current = i.state[0], i.state[1], i.current[...]
    else:
        if packed:
            ups, downs = [], []
            for j in range(width // LANES):
                one, two = i.recv[2 * j][:scen], i.recv[2 * j + 1][:scen]
                ups.append(jnp.where(low, one, pltpu.roll(two, cap, 1)))
                downs.append(jnp.where(low, pltpu.roll(one, cap, 1), two))
            first, second = jnp.concatenate(ups, axis=1), jnp.concatenate(downs, axis=1)
        else:
            first, second = i.recv[0, :scen], i.recv[1, :scen]
        current = drive(second)

    fault_p = known.fault_p[...]
    ends = 2 * lines
    arrivals = [pick(back, delays, t0 + j, maxd) for j in range(2)]
    waves = jnp.concatenate(
        [jnp.concatenate([arrivals[j], far_in[j]], axis=1) for j in range(2)], axis=0
    )
    pairs = split2(waves)
    for part in range(2):
        o.x[part * 2 * scen : (part + 1) * 2 * scen, :ends] = pairs[part]
    both = dot(jnp.concatenate(pairs, axis=0), known.m_high[:ends, :])
    volts = both[: 2 * scen] + both[2 * scen :] + dot(pairs[0], known.m_low[:ends, :])
    base = [jnp.broadcast_to(i.base_p[t0 + j : t0 + j + 1, :], (scen, points)) for j in range(2)]
    volts = volts + jnp.concatenate(base, axis=0)
    fault_ends, fault_conv = fault_p[:, :ends], fault_p[:, ends:]
    wave_fault = jnp.sum(
        waves * jnp.concatenate([fault_ends, fault_ends], axis=0), axis=1, keepdims=True
    )
    highs, lows, coefs = [], [], []
    for j in range(2):
        here = slice(j * scen, (j + 1) * scen)
        high, low_part = split2(current)
        highs.append(high)
        lows.append(low_part)
        o.x[j * scen : (j + 1) * scen, ends:] = high
        o.x[(2 + j) * scen : (3 + j) * scen, ends:] = low_part
        both = dot(jnp.concatenate([high, low_part], axis=0), known.m_high[ends:, ends:])
        node = both[:scen] + both[scen:] + dot(high, known.m_low[ends:, ends:])
        at_fault = i.fault_base[:, t0 + j : t0 + j + 1] + wave_fault[here]
        at_fault = at_fault + jnp.sum(current * fault_conv, axis=1, keepdims=True)
        coef = i.fault_ratio[:, t0 + j : t0 + j + 1] * at_fault
        coefs.append(coef)
        o.coef[here, :] = jnp.broadcast_to(coef, (scen, LANES))
        node = node + volts[here, ends:] - fault_conv * coef
        first = params[1] * first + params[2] * (params[0] - node)
        second = second + params[3] * (first - second)
        current = drive(second)
    sides = []
    if t0 <= last - DMIN:
        both = dot(jnp.concatenate(highs + lows, axis=0), known.m_high[ends:, :ends])
        more = both[: 2 * scen] + both[2 * scen :]
        more = more + dot(jnp.concatenate(highs, axis=0), known.m_low[ends:, :ends])
        for j in range(2):
            here = slice(j * scen, (j + 1) * scen)
            line = volts[here, :ends] + more[here] - fault_ends * coefs[j]
            made[t0 + j] = scale * (twice * line[:, :lines] - arrivals[j])
            sides.append(line[:, lines:])
            if hasattr(o, "out"):
                o.out[j] = made[t0 + j]
    if hasattr(o, "into"):
        for j in range(2):
            onward = pick(out, delays, t0 + 2 + j, maxd)
            o.into[j] = onward
            o.swap_near[j] = jnp.where(even, onward, sides[j])
            o.swap_far[j] = jnp.where(even, sides[j], onward)
    if hasattr(o, "state"):
        o.state[0] = first
        o.state[1] = second
    if t0 + 2 < STEPS or not packed:
        o.current[...] = current
    else:
        half = scen // 2
        for j in range(width // LANES):
            mine = current[:, j * LANES : (j + 1) * LANES]
            top, bottom = mine[:half], mine[half:]
            o.current[2 * j] = jnp.where(low, top, pltpu.roll(bottom, cap, 1))
            o.current[2 * j + 1] = jnp.where(low, pltpu.roll(top, cap, 1), bottom)


def full_body(sizes, pair, i, o):
    nblk, points, scen = sizes
    blk = LANES
    t0 = 2 * pair
    fault_z = i.fault_z[...]
    fault_blk = owner_of(i.mark[points : points + scen, :])
    x = i.x[...]
    coef = i.coef[...]
    i.ready("inv")
    if pair:
        all_base = i.base
    else:
        all_base = o.base
        source = sources(i.pack[0:1, :], i.pack[1:2, :])
        for k in range(nblk):
            here = slice(k * blk, (k + 1) * blk)
            o.base[:, here] = product3(source[:, here], *split2(i.inv[k]))
    for k in range(0, nblk, WIDE):
        mine = jnp.concatenate([owned(i.mark[:points], k + j) for j in range(WIDE)], axis=1)
        both = dot(x, mine)
        inject = both[: 2 * scen] + both[2 * scen :]
        for j in range(WIDE):
            here = slice((k + j) * blk, (k + j + 1) * blk)
            volts = product3(inject[:, j * blk : (j + 1) * blk], *split2(i.inv[k + j]))
            base = [
                jnp.broadcast_to(all_base[t0 + m : t0 + m + 1, here], (scen, blk))
                for m in range(2)
            ]
            zcol = jnp.where(fault_blk == k + j, fault_z, 0.0)
            volts = volts + jnp.concatenate(base, axis=0)
            volts = volts - jnp.concatenate([zcol, zcol], axis=0) * coef
            total = jnp.sum(volts * volts, axis=0, keepdims=True)
            if hasattr(i, "squares"):
                total = total + i.squares[:, here]
            o.squares[:, here] = total
            if hasattr(o, "volts"):
                o.volts[:, here] = volts[scen:]


def finish_body(sizes, i, o):
    regions, cap, scen, group, count, packed = sizes
    parts = [i.parts[k][...] for k in range(count)]
    while len(parts) > 1:
        parts = [parts[k] + parts[k + 1] for k in range(0, len(parts), 2)]
    o.rms[...] = jnp.sqrt(parts[0] / (scen * count * STEPS) + EPS)
    slots = i.slots[...]
    if packed:
        half = scen // 2
        lane = iota((LANES, group), 0)
        top = bottom = None
        for region in range(regions):
            left = onehot((lane < cap) & (slots == region * cap + lane))
            right = onehot((lane >= cap) & (slots == (region - 1) * cap + lane))
            both = dot(
                jnp.concatenate(split3(i.recv[region]), axis=0),
                jnp.concatenate([left, right], axis=1),
            )
            value = both[:half] + both[half : 2 * half] + both[2 * half :]
            top = value if top is None else top + value
        o.current[:half, :] = top[:, :group]
        o.current[half:, :] = top[:, group:]
    else:
        mask = onehot(iota((regions * cap, group), 0) == slots)
        both = dot(jnp.concatenate(split3(i.recv[...]), axis=0), mask)
        o.current[...] = both[:scen] + both[scen : 2 * scen] + both[2 * scen :]


def per_device(
    inv_blocks,
    src_amp,
    src_phase,
    line_a,
    line_b,
    line_delay,
    line_yc,
    line_atten,
    hist_ua,
    hist_ub,
    send_node,
    recv_slot,
    conv_par,
    conv_state,
    fault_node,
    fault_step,
    fault_cond,
):
    nblk, blk = inv_blocks.shape[0], inv_blocks.shape[1]
    nreg = nblk * blk
    lines = line_a.shape[1]
    maxd, scen = hist_ua.shape[1], hist_ua.shape[2]
    regions, cap = send_node.shape[1], send_node.shape[2]
    group = recv_slot.shape[1]
    width = regions * cap
    points = 2 * lines + width
    count = lax.axis_size("scen")
    packed = 2 * cap == LANES
    half = scen + 8

    send_shape = (regions, half, LANES) if packed else (half, regions * 2 * cap)
    head = call(
        functools.partial(start_body, (regions, cap, half, scen, group, maxd, lines, nreg)),
        "start",
        {},
        {},
        hbm_outs=dict(
            send=(send_shape, F32), into=((2, scen, lines), F32), pack=((8, nreg), F32)
        ),
        limit=VMEM,
        hbm=dict(
            slots=recv_slot,
            par=conv_par,
            state=conv_state,
            hist=hist_ua,
            delay=line_delay,
            end_a=line_a,
            end_b=line_b,
            conv=send_node,
            amp=src_amp.reshape(1, nreg),
            phase=src_phase.reshape(1, nreg),
            fault_node=fault_node.reshape(1, scen),
            fault_step=fault_step.reshape(1, scen),
            fault_cond=fault_cond.reshape(1, scen),
        ),
    )
    send = head.send
    if packed:
        recv = lax.all_to_all(send, "region", split_axis=0, concat_axis=0, tiled=True)
    else:
        send = send.reshape(half, 2, regions, cap).transpose(2, 1, 0, 3)
        recv = lax.all_to_all(send, "region", split_axis=0, concat_axis=0, tiled=True)
        recv = recv.transpose(1, 2, 0, 3).reshape(2, half, width)
    into = head.into
    far_in = shifted(into, "region", 1)

    whole = points + blk
    model = call(
        functools.partial(rows_body, (nreg, nblk, lines, regions, cap, scen)),
        "rows",
        dict(pack=head.pack),
        dict(
            row=((1, whole), jnp.int32),
            mark=((whole, blk), BF16),
            rows=((whole, 2 * blk), BF16),
            base_p=((STEPS, points), F32),
            fault_z=((scen, blk), F32),
            fault_base=((scen, blk), F32),
            fault_ratio=((scen, blk), F32),
        ),
        hbm=dict(inv=inv_blocks),
        scratch=(
            pltpu.VMEM((whole, nreg), BF16),
            pltpu.VMEM((nreg, 2 * blk), BF16),
            pltpu.VMEM((STEPS * nblk, blk), F32),
        ),
        limit=VMEM - ROOM,
        cost=(4e9, 2e7),
    )
    wave = ((2, scen, lines), F32)
    mades, backs, carry = {}, {}, {}
    squares = swap_near = swap_far = sent = base = None
    for pair in range(STEPS // 2):
        t0 = 2 * pair
        final = t0 + 2 >= STEPS
        ins = dict(
            delay=line_delay,
            atten=line_atten,
            admit=line_yc,
            recv=recv,
            base_p=model.base_p,
            fault_base=model.fault_base,
            fault_ratio=model.fault_ratio,
            **carry,
        )
        if t0 - maxd < 0:
            ins.update(hist_b=hist_ub)
        if pair:
            ins.update(swap_near=swap_near, swap_far=swap_far, into_prev=sent, row=model.row)
            ins.update(m_high=matrix.m_high, m_low=matrix.m_low, fault_p=matrix.fault_p)
        else:
            ins.update(far_in=far_in)
            ins.update(row=model.row, mark=model.mark, rows=model.rows)
        first = max(0, pair - 3)
        ins.update(backs={k: v for k, v in backs.items() if k >= first})
        if not final:
            ins.update(made={k: v for k, v in mades.items() if k >= pair - 2})
            if t0 + 2 - maxd < 0:
                ins.update(hist_a=hist_ua)
        outs = dict(x=((4 * scen, points), BF16), coef=((2 * scen, LANES), F32))
        if not final:
            outs.update(
                swap_far=wave,
                swap_near=wave,
                into=wave,
                state=((2, scen, width), F32),
                current=((scen, width), F32),
            )
            if t0 + 4 < STEPS:
                outs.update(out=wave)
            if pair:
                outs.update(back=wave)
            else:
                outs.update(
                    m_high=((points, points), BF16),
                    m_low=((points, points), BF16),
                    fault_p=((scen, points), F32),
                )
        else:
            shape = (regions, scen // 2, LANES) if packed else (scen, width)
            outs.update(current=(shape, F32))
        made = call(
            functools.partial(advance_body, (lines, width, scen, cap, maxd, packed), pair),
            "advance",
            ins,
            outs,
        )
        if not pair:
            matrix = made
        if not final:
            sent, into = into, made.into
            swap_far = swapped(made.swap_far, "region", 1)
            swap_near = swapped(made.swap_near, "region", 0)
            if t0 + 4 < STEPS:
                mades[pair] = made.out
            if pair:
                backs[pair - 1] = made.back
            carry = dict(state=made.state, current=made.current)
        else:
            current = made.current
            if packed:
                returned = lax.all_to_all(current, "region", split_axis=0, concat_axis=0, tiled=True)
            else:
                current = current.reshape(scen, regions, cap).transpose(1, 0, 2)
                returned = lax.all_to_all(current, "region", split_axis=0, concat_axis=0, tiled=True)
                returned = returned.transpose(1, 0, 2).reshape(scen, width)
        ins = dict(
            x=made.x,
            coef=made.coef,
            mark=model.mark,
            fault_z=model.fault_z,
        )
        if pair:
            ins.update(squares=squares, base=base)
        else:
            ins.update(pack=head.pack)
        outs = dict(squares=((1, nreg), F32))
        if final:
            outs.update(volts=((scen, nreg), F32))
        if not pair:
            outs.update(base=((STEPS, nreg), F32))
        full = call(
            functools.partial(full_body, (nblk, points, scen), pair),
            "full",
            ins,
            outs,
            hbm=dict(inv=inv_blocks),
            cost=(4e9, 1e7),
        )
        squares = full.squares
        if not pair:
            base = full.base

    parts = [squares]
    for offset in range(1, count):
        pairs = [(source, source ^ offset) for source in range(count)]
        parts.append(lax.ppermute(squares, "scen", pairs))
    tail = call(
        functools.partial(finish_body, (regions, cap, scen, group, count, packed)),
        "finish",
        dict(slots=recv_slot, recv=returned, parts=parts),
        dict(rms=((1, nreg), F32), current=((scen, group), F32)),
    )
    return full.volts, tail.current, tail.rms.reshape(nreg)


def solution(mesh):
    return jax.shard_map(
        per_device,
        mesh=mesh,
        in_specs=(
            P("region", None, None),
            P("region"),
            P("region"),
            P("region", None),
            P("region", None),
            P("region", None),
            P("region", None),
            P("region", None),
            P("region", None, "scen", None),
            P("region", None, "scen", None),
            P("region", None, None),
            P("region", None),
            P(None, "region"),
            P(None, "scen", "region"),
            P("scen"),
            P("scen"),
            P("scen"),
        ),
        out_specs=(P("scen", "region"), P("scen", "region"), P("region")),
        check_vma=False,
    )
```

```python
import functools
from types import SimpleNamespace as Space

import jax
import jax.numpy as jnp
from jax import lax
from jax.experimental import pallas as pl
from jax.experimental.pallas import tpu as pltpu
from jax.sharding import PartitionSpec as P

STEPS = 8
DMIN = 2
LANES = 128
WIDE = 4
PAIR = "pair"
OMEGA = 0.01884955592153876
EPS = 1e-06
F32 = jnp.float32
BF16 = jnp.bfloat16
NN = (((1,), (0,)), ((), ()))
NT = (((1,), (1,)), ((), ()))


def shifted(value, axis, steps):
    count = lax.axis_size(axis)
    pairs = [(source, (source + steps) % count) for source in range(count)]
    return lax.ppermute(value, axis, pairs)


def mirrored(value, axis, offset):
    count = lax.axis_size(axis)
    return lax.ppermute(value, axis, [(source, source ^ offset) for source in range(count)])


def swapped(value, axis, first):
    count = lax.axis_size(axis)
    pairs = []
    for left in range(first, count, 2):
        right = (left + 1) % count
        pairs += [(left, right), (right, left)]
    return lax.ppermute(value, axis, pairs)


def call(
    body,
    name,
    ins,
    outs,
    scratch=(),
    hbm=None,
    hbm_outs=None,
    relays=None,
    scalar=(),
    limit=20 << 20,
    cost=None,
):
    leaves, tree = jax.tree.flatten(ins)
    far, far_outs = dict(hbm or {}), dict(hbm_outs or {})
    far = {key: pltpu.with_memory_space_constraint(far[key], pltpu.HBM) for key in far}
    relays = dict(relays or {})
    names = [list(far), list(outs), list(far_outs), list(relays)]
    sizes = [len(leaves)] + [len(group) for group in names] + [len(far), len(far_outs)]
    ends = [sum(sizes[:k]) for k in range(len(sizes) + 1)]
    count = len(far) + len(far_outs) + len(relays)

    def kernel(*refs):
        near, sources, near_outs, targets, relayed, held, made = [
            refs[ends[k] : ends[k + 1]] for k in range(len(sizes))
        ]
        rest = refs[ends[-1] :]
        arriving, leaving, pending = {}, {}, []
        if count:
            sems, rest = rest[0], rest[1:]
            for k, key in enumerate(far):
                arriving[key] = pltpu.make_async_copy(sources[k], held[k], sems.at[k])
                arriving[key].start()
            for k, key in enumerate(far_outs):
                leaving[key] = pltpu.make_async_copy(made[k], targets[k], sems.at[len(far) + k])
        i = Space(**jax.tree.unflatten(tree, near), **dict(zip(far, held)))
        o = Space(**dict(zip(outs, near_outs)), **dict(zip(far_outs, made)))
        for k, key in enumerate(relays):
            copy = pltpu.make_async_copy(getattr(i, key), relayed[k], sems.at[count - 1 - k])
            copy.start()
            pending.append(copy)

        def flush(key):
            pending.append(leaving.pop(key))
            pending[-1].start()

        i.ready = lambda *keys: [arriving.pop(key).wait() for key in keys]
        o.flush = flush
        body(i, o, *rest)
        for key in list(leaving):
            flush(key)
        for copy in pending:
            copy.wait()

    buffers = [
        (pltpu.SMEM if key in scalar else pltpu.VMEM)(value.shape, value.dtype)
        for key, value in far.items()
    ]
    buffers += [pltpu.VMEM(*shape) for shape in far_outs.values()]
    if count:
        buffers.append(pltpu.SemaphoreType.DMA((count,)))
    every = list(outs.values()) + list(far_outs.values()) + list(relays.values())
    near_spec, far_spec = (pl.BlockSpec(memory_space=space) for space in (pltpu.VMEM, pltpu.HBM))
    flops, moved = cost or (1e9, 4e6)
    results = pl.pallas_call(
        kernel,
        name=name,
        out_shape=[jax.ShapeDtypeStruct(*shape) for shape in every],
        in_specs=[near_spec] * len(leaves) + [far_spec] * len(far),
        out_specs=[near_spec] * len(outs) + [far_spec] * (len(far_outs) + len(relays)),
        scratch_shapes=buffers + list(scratch),
        compiler_params=pltpu.CompilerParams(vmem_limit_bytes=limit),
        cost_estimate=pl.CostEstimate(
            flops=int(flops), bytes_accessed=int(moved), transcendentals=0
        ),
    )(*leaves, *far.values())
    return Space(**dict(zip(names[1] + names[2] + names[3], results)))


def iota(shape, dim):
    return lax.broadcasted_iota(jnp.int32, shape, dim)


def onehot(mask):
    return jnp.where(mask, 1.0, 0.0).astype(BF16)


def owner_of(mark):
    return jnp.max(mark.astype(F32), axis=1, keepdims=True)


def dot(left, right, dims=NN):
    return lax.dot_general(left, right, dims, preferred_element_type=F32)


def split2(value):
    high = value.astype(BF16)
    return high, (value - high.astype(F32)).astype(BF16)


def split3(value):
    high, rest = value.astype(BF16), value
    rest = value - high.astype(F32)
    mid = rest.astype(BF16)
    return high, mid, (rest - mid.astype(F32)).astype(BF16)


def product3(left, right_high, right_low, dims=NN):
    rows = left.shape[0]
    high, low = split2(left)
    both = dot(jnp.concatenate([high, low], axis=0), right_high, dims)
    return both[:rows] + both[rows:] + dot(high, right_low, dims)


def as_column(row, size):
    wide = jnp.broadcast_to(row, (size, size))
    return jnp.sum(
        jnp.where(iota((size, size), 0) == iota((size, size), 1), wide, 0.0), axis=1, keepdims=True
    )


def pick(wave, delays, instant, maxd):
    total = None
    for lag in range(DMIN, maxd + 1):
        term = jnp.where(delays == lag, wave(instant - lag), 0.0)
        total = term if total is None else total + term
    return total


def start_body(sizes, i, o):
    regions, cap, half, scen, group, maxd = sizes
    packed = 2 * cap == LANES
    i.ready("slots", "par", "state")
    slots = i.slots[...]
    rows = iota((regions * 2 * cap, group), 0)
    away = jnp.bitwise_xor(slots // cap, lax.axis_index("region"))
    if packed:
        target = away * (2 * cap) + slots % cap
        moved = target + cap
    else:
        target = away * cap + slots % cap
        moved = target + regions * cap
    left, right = onehot(rows == target), onehot(rows == moved)
    pad = jnp.zeros((half - scen - 6, group), F32)
    upper = jnp.concatenate([i.state[0], i.par[...], pad], axis=0)
    lower = jnp.concatenate([i.state[1], jnp.zeros((half - scen, group), F32)], axis=0)
    buffer = None
    for part, mask in ((upper, left), (lower, right)):
        both = dot(jnp.concatenate(split3(part), axis=0), mask, NT)
        value = both[:half] + both[half : 2 * half] + both[2 * half :]
        buffer = value if buffer is None else buffer + value
    if packed:
        for index in range(regions):
            slot = buffer[:, index * LANES : (index + 1) * LANES]
            (o.odd if index % 2 else o.even)[index // 2] = slot
    else:
        o.send[...] = buffer
    i.ready("hist", "delay")
    delays = i.delay[...]
    for step in range(2):
        o.into[step] = pick(lambda t: i.hist[0, t + maxd], delays, step, maxd)


def pair_body(count, i, o):
    for k in range(count):
        target = getattr(o, PAIR + str(k))
        target[0], target[1] = i.even[k], i.odd[k]


def sources(amp, phase):
    instant = iota((STEPS, amp.shape[1]), 0).astype(F32)
    return amp * jnp.cos(OMEGA * instant + phase)


def rows_body(sizes, i, o, taken, source_rows):
    nreg, nblk, lines, regions, cap, scen = sizes
    blk = LANES
    width = regions * cap
    points = 2 * lines + width
    whole = points + blk
    here = lax.axis_index("region")
    groups = [jnp.bitwise_xor(here, away) for away in range(regions)]
    i.ready("end_a", "end_b", "conv", "fault_node")
    o.row[...] = jnp.full((1, whole), -1, jnp.int32)
    o.row[:, 0:lines] = i.end_a[...]
    o.row[:, lines : 2 * lines] = i.end_b[...]
    for away in range(regions):
        first = 2 * lines + away * cap
        o.row[:, first : first + cap] = i.conv[0, pl.ds(groups[away], 1), :]
    fault = i.fault_node[...] - here * nreg
    o.row[:, points : points + scen] = jnp.where((fault >= 0) & (fault < nreg), fault, -1)
    row = o.row[...]
    whole_row = row.astype(F32)
    column = jnp.transpose(jnp.broadcast_to(whole_row, (blk, whole))).astype(jnp.int32)
    inside = (column & 127) == iota((whole, blk), 1)
    o.mark[...] = jnp.where(inside, (column >> 7).astype(F32), -1.0).astype(BF16)
    o.fault_mark[...] = o.mark[points : points + scen, :].astype(F32)
    i.ready("list_a", "list_b", "list_conv", "list_fault", "inv")
    for p in range(points + scen):
        if p < lines:
            node = i.list_a[0, p]
        elif p < 2 * lines:
            node = i.list_b[0, p - lines]
        elif p < points:
            away, place = divmod(p - 2 * lines, cap)
            node = jnp.maximum(i.list_conv[0, groups[away], place], 0)
        else:
            node = jnp.clip(i.list_fault[0, p - points] - here * nreg, 0, nreg - 1)
        taken[p : p + 1, :] = i.inv[pl.ds(node, 1), :]
    taken[points + scen :, :] = jnp.zeros((blk - scen, blk), F32)
    high, low = split2(jnp.where(column >= 0, taken[...], 0.0))
    o.rows[:, :blk] = high
    o.rows[:, blk:] = low
    i.ready("amp", "phase", "fault_step", "fault_cond")
    source = sources(i.amp[...], i.phase[...])
    for k in range(nblk):
        source_rows[k * STEPS : (k + 1) * STEPS, :] = source[:, k * blk : (k + 1) * blk]
    spread = product3(source_rows[...], o.rows[:, :blk], o.rows[:, blk:], NT)
    row_blk = row >> 7
    at_points = jnp.zeros((STEPS, whole), F32)
    for k in range(nblk):
        at_points = at_points + jnp.where(row_blk == k, spread[k * STEPS : (k + 1) * STEPS], 0.0)
    o.base_p[...] = at_points[:, :points]
    tail = jnp.concatenate(
        [at_points[:, points:], jnp.zeros((blk - STEPS, blk), F32)], axis=0
    )
    o.fault_base[...] = jnp.transpose(tail)[:scen]
    fault_rows = o.rows[points : points + scen, :].astype(F32)
    fault_z = fault_rows[:, :blk] + fault_rows[:, blk:]
    o.fault_z[...] = fault_z
    self_imp = jnp.sum(
        jnp.where(iota((scen, blk), 1) == (column[points : points + scen] & 127), fault_z, 0.0),
        axis=1,
        keepdims=True,
    )
    cond = as_column(i.fault_cond[...], scen)
    closes = as_column(i.fault_step[...].astype(F32), scen)
    ratio = cond / (1.0 + cond * self_imp)
    o.fault_ratio[...] = jnp.where(
        closes <= iota((scen, blk), 1).astype(F32), jnp.broadcast_to(ratio, (scen, blk)), 0.0
    )


def between_body(points, scen, i, o):
    blk = LANES
    row = i.row[:, :points]
    row_blk = (row >> 7).astype(F32)
    inside = onehot(iota((blk, points), 0) == (row & 127))
    for k in range(points // blk):
        here = slice(k * blk, (k + 1) * blk)
        same = owner_of(i.mark[here, :]) == row_blk
        both = dot(jnp.concatenate([i.rows[here, :blk], i.rows[here, blk:]], axis=0), inside)
        o.m_high[here, :] = jnp.where(same, both[:blk], 0.0).astype(BF16)
        o.m_low[here, :] = jnp.where(same, both[blk:], 0.0).astype(BF16)
    here = slice(points, points + scen)
    both = dot(jnp.concatenate([i.rows[here, :blk], i.rows[here, blk:]], axis=0), inside)
    same = owner_of(i.mark[here, :]) == row_blk
    o.fault_p[...] = jnp.where(same, both[:scen] + both[scen:], 0.0)


def advance_body(sizes, pair, i, o):
    lines, width, scen, cap, maxd, packed = sizes
    t0 = 2 * pair
    delays = i.delay[...]
    scale = i.atten[...]
    twice = 2.0 * i.admit[...]
    last = STEPS - 1

    even = lax.rem(lax.axis_index("region"), 2) == 0
    fresh = {}
    if pair:
        far_in = [jnp.where(even, i.swap_far[j], i.swap_near[j]) for j in range(2)]
        for j in range(2):
            far_volts = jnp.where(even, i.swap_near[j], i.swap_far[j])
            fresh[t0 - 2 + j] = scale * (twice * far_volts - i.into_prev[j])
            if hasattr(o, "back"):
                o.back[j] = fresh[t0 - 2 + j]
    else:
        far_in = [i.far_in[j] for j in range(2)]

    def back(t):
        if t in fresh:
            return fresh[t]
        if t < 0:
            return i.hist_b[0, t + maxd]
        return i.backs[t // 2][t % 2]

    made = {}

    def out(t):
        if t in made:
            return made[t]
        if t < 0:
            return i.hist_a[0, t + maxd]
        return i.made[t // 2][t % 2]

    points = 2 * lines + width
    known = i if pair else o
    if not pair:
        between_body(points, scen, i, o)
    live = i.row[:, 2 * lines : 2 * lines + width] >= 0
    if packed:
        low = iota((1, LANES), 1) < cap
        params = []
        for row in range(6):
            pieces = []
            for j in range(width // LANES):
                one = i.recv[j][0, scen + row : scen + row + 1, :]
                two = i.recv[j][1, scen + row : scen + row + 1, :]
                pieces.append(jnp.where(low, one, pltpu.roll(two, cap, 1)))
            params.append(jnp.concatenate(pieces, axis=1))
    else:
        params = [i.recv[0, scen + row : scen + row + 1, :] for row in range(6)]
    params[5] = jnp.where(live, params[5], 1.0)

    def drive(second):
        return params[5] * jnp.tanh((params[4] + second) / params[5])

    if pair:
        first, second, current = i.state[0], i.state[1], i.current[...]
    else:
        if packed:
            ups, downs = [], []
            for j in range(width // LANES):
                one, two = i.recv[j][0, :scen], i.recv[j][1, :scen]
                ups.append(jnp.where(low, one, pltpu.roll(two, cap, 1)))
                downs.append(jnp.where(low, pltpu.roll(one, cap, 1), two))
            first, second = jnp.concatenate(ups, axis=1), jnp.concatenate(downs, axis=1)
        else:
            first, second = i.recv[0, :scen], i.recv[1, :scen]
        current = drive(second)

    fault_p = known.fault_p[...]
    ends = 2 * lines
    arrivals = [pick(back, delays, t0 + j, maxd) for j in range(2)]
    waves = jnp.concatenate(
        [jnp.concatenate([arrivals[j], far_in[j]], axis=1) for j in range(2)], axis=0
    )
    pairs = split2(waves)
    for part in range(2):
        o.x[part * 2 * scen : (part + 1) * 2 * scen, :ends] = pairs[part]
    both = dot(jnp.concatenate(pairs, axis=0), known.m_high[:ends, :])
    volts = both[: 2 * scen] + both[2 * scen :] + dot(pairs[0], known.m_low[:ends, :])
    base = [jnp.broadcast_to(i.base_p[t0 + j : t0 + j + 1, :], (scen, points)) for j in range(2)]
    volts = volts + jnp.concatenate(base, axis=0)
    fault_ends, fault_conv = fault_p[:, :ends], fault_p[:, ends:]
    wave_fault = jnp.sum(
        waves * jnp.concatenate([fault_ends, fault_ends], axis=0), axis=1, keepdims=True
    )
    highs, lows, coefs = [], [], []
    for j in range(2):
        here = slice(j * scen, (j + 1) * scen)
        high, low_part = split2(current)
        highs.append(high)
        lows.append(low_part)
        o.x[j * scen : (j + 1) * scen, ends:] = high
        o.x[(2 + j) * scen : (3 + j) * scen, ends:] = low_part
        both = dot(jnp.concatenate([high, low_part], axis=0), known.m_high[ends:, ends:])
        node = both[:scen] + both[scen:] + dot(high, known.m_low[ends:, ends:])
        at_fault = i.fault_base[:, t0 + j : t0 + j + 1] + wave_fault[here]
        at_fault = at_fault + jnp.sum(current * fault_conv, axis=1, keepdims=True)
        coef = i.fault_ratio[:, t0 + j : t0 + j + 1] * at_fault
        coefs.append(coef)
        o.coef[here, :] = jnp.broadcast_to(coef, (scen, LANES))
        node = node + volts[here, ends:] - fault_conv * coef
        first = params[1] * first + params[2] * (params[0] - node)
        second = second + params[3] * (first - second)
        current = drive(second)
    sides = []
    if t0 <= last - DMIN:
        both = dot(jnp.concatenate(highs + lows, axis=0), known.m_high[ends:, :ends])
        more = both[: 2 * scen] + both[2 * scen :]
        more = more + dot(jnp.concatenate(highs, axis=0), known.m_low[ends:, :ends])
        for j in range(2):
            here = slice(j * scen, (j + 1) * scen)
            line = volts[here, :ends] + more[here] - fault_ends * coefs[j]
            made[t0 + j] = scale * (twice * line[:, :lines] - arrivals[j])
            sides.append(line[:, lines:])
            if hasattr(o, "out"):
                o.out[j] = made[t0 + j]
    if hasattr(o, "into"):
        for j in range(2):
            onward = pick(out, delays, t0 + 2 + j, maxd)
            o.into[j] = onward
            o.swap_near[j] = jnp.where(even, onward, sides[j])
            o.swap_far[j] = jnp.where(even, sides[j], onward)
    if hasattr(o, "state"):
        o.state[0] = first
        o.state[1] = second
    if t0 + 2 < STEPS or not packed:
        o.current[...] = current
    else:
        half = scen // 2
        region = lax.axis_index("region")
        for j in range(width // LANES):
            mine = current[:, j * LANES : (j + 1) * LANES]
            top, bottom = mine[:half], mine[half:]
            pieces = (
                jnp.where(low, top, pltpu.roll(bottom, cap, 1)),
                jnp.where(low, pltpu.roll(top, cap, 1), bottom),
            )
            for k in range(2):
                o.current[jnp.bitwise_xor(region, 2 * j + k)] = pieces[k]


def full_body(sizes, pair, i, o):
    nblk, points, scen = sizes
    blk = LANES
    t0 = 2 * pair
    fault_z = i.fault_z[...]
    fault_blk = owner_of(i.fault_mark[...])
    x = i.x[...]
    coef = i.coef[...]
    if pair:
        known = i
    else:
        known = o
        mark = i.mark[:points].astype(F32)
        node = jnp.where(mark >= 0.0, mark * blk + iota((points, blk), 1).astype(F32), -1.0)
        node = jnp.max(node, axis=1, keepdims=True)
        o.column[...] = jnp.broadcast_to(node, (points, blk)).astype(jnp.int32)
        i.ready("inv", "amp", "phase")
        for k in range(nblk):
            here = slice(k * blk, (k + 1) * blk)
            o.zcat[here, :blk], o.zcat[here, blk:] = split2(i.inv[k])
        source = sources(i.amp[...], i.phase[...])
        for k in range(nblk):
            here = slice(k * blk, (k + 1) * blk)
            o.base[:, here] = product3(source[:, here], o.zcat[here, :blk], o.zcat[here, blk:])
    lane = iota((points, blk), 1)
    for k in range(0, nblk, WIDE):
        mine = jnp.concatenate(
            [onehot(known.column[...] == lane + (k + j) * blk) for j in range(WIDE)], axis=1
        )
        both = dot(x, mine)
        inject = both[: 2 * scen] + both[2 * scen :]
        for j in range(WIDE):
            here = slice((k + j) * blk, (k + j + 1) * blk)
            z = known.zcat[here, :]
            volts = product3(inject[:, j * blk : (j + 1) * blk], z[:, :blk], z[:, blk:])
            base = [
                jnp.broadcast_to(known.base[t0 + m : t0 + m + 1, here], (scen, blk))
                for m in range(2)
            ]
            zcol = jnp.where(fault_blk == k + j, fault_z, 0.0)
            volts = volts + jnp.concatenate(base, axis=0)
            volts = volts - jnp.concatenate([zcol, zcol], axis=0) * coef
            total = jnp.sum(volts * volts, axis=0, keepdims=True)
            if hasattr(i, "squares"):
                total = total + i.squares[:, here]
            o.squares[:, here] = total
            if hasattr(o, "volts"):
                o.volts[:, here] = volts[scen:]


def rms_body(scen, count, i, o):
    parts = [i.parts[k][...] for k in range(count)]
    while len(parts) > 1:
        parts = [parts[k] + parts[k + 1] for k in range(0, len(parts), 2)]
    o.rms[...] = jnp.sqrt(parts[0] / (scen * count * STEPS) + EPS)


def settle_body(sizes, i, o):
    regions, cap, scen, group, packed = sizes
    slots = i.slots[...]
    if packed:
        half = scen // 2
        lane = iota((LANES, group), 0)
        top = bottom = None
        for region in range(regions):
            left = onehot((lane < cap) & (slots == region * cap + lane))
            right = onehot((lane >= cap) & (slots == (region - 1) * cap + lane))
            both = dot(
                jnp.concatenate(split3(i.recv[region]), axis=0),
                jnp.concatenate([left, right], axis=1),
            )
            value = both[:half] + both[half : 2 * half] + both[2 * half :]
            top = value if top is None else top + value
        o.current[:half, :] = top[:, :group]
        o.current[half:, :] = top[:, group:]
    else:
        mask = onehot(iota((regions * cap, group), 0) == slots)
        both = dot(jnp.concatenate(split3(i.recv[...]), axis=0), mask)
        o.current[...] = both[:scen] + both[scen : 2 * scen] + both[2 * scen :]


def per_device(
    inv_blocks,
    src_amp,
    src_phase,
    line_a,
    line_b,
    line_delay,
    line_yc,
    line_atten,
    hist_ua,
    hist_ub,
    send_node,
    recv_slot,
    conv_par,
    conv_state,
    fault_node,
    fault_step,
    fault_cond,
):
    nblk, blk = inv_blocks.shape[0], inv_blocks.shape[1]
    nreg = nblk * blk
    lines = line_a.shape[1]
    maxd, scen = hist_ua.shape[1], hist_ua.shape[2]
    regions, cap = send_node.shape[1], send_node.shape[2]
    group = recv_slot.shape[1]
    width = regions * cap
    points = 2 * lines + width
    count = lax.axis_size("scen")
    packed = 2 * cap == LANES
    half = scen + 8

    amp, phase = src_amp.reshape(1, nreg), src_phase.reshape(1, nreg)
    if packed:
        slot_outs = dict.fromkeys(("even", "odd"), ((regions // 2, half, LANES), F32))
    else:
        slot_outs = dict(send=((half, regions * 2 * cap), F32))
    head = call(
        functools.partial(start_body, (regions, cap, half, scen, group, maxd)),
        "start",
        {},
        dict(into=((2, scen, lines), F32), **slot_outs),
        hbm=dict(
            slots=recv_slot, par=conv_par, state=conv_state, hist=hist_ua, delay=line_delay
        ),
    )
    if packed:
        even, odd = head.even, head.odd
    else:
        slots = head.send.reshape(half, 2, regions, cap).transpose(2, 1, 0, 3)
        even, odd = slots[0::2], slots[1::2]
    odd = mirrored(odd, "region", 1)
    into = head.into
    far_in = shifted(into, "region", 1)
    if packed:
        shape = ((2, half, LANES), F32)
        couples = call(
            functools.partial(pair_body, regions // 2),
            "couple",
            dict(even=even, odd=odd),
            {PAIR + str(k): shape for k in range(regions // 2)},
        )
        couples = [getattr(couples, PAIR + str(k)) for k in range(regions // 2)]
    else:
        couples = [jnp.stack([even[k], odd[k]]) for k in range(regions // 2)]
    recv = couples[:1]
    for k in range(1, regions // 2):
        recv.append(mirrored(couples[k], "region", 2 * k))
    if not packed:
        recv = jnp.concatenate(recv, axis=0).transpose(1, 2, 0, 3).reshape(2, half, width)

    whole = points + blk
    model = call(
        functools.partial(rows_body, (nreg, nblk, lines, regions, cap, scen)),
        "rows",
        {},
        dict(
            row=((1, whole), jnp.int32),
            mark=((whole, blk), BF16),
            fault_mark=((scen, blk), F32),
            rows=((whole, 2 * blk), BF16),
            base_p=((STEPS, points), F32),
            fault_z=((scen, blk), F32),
            fault_base=((scen, blk), F32),
            fault_ratio=((scen, blk), F32),
        ),
        hbm=dict(
            end_a=line_a,
            end_b=line_b,
            conv=send_node,
            fault_node=fault_node.reshape(1, scen),
            list_a=line_a,
            list_b=line_b,
            list_conv=send_node,
            list_fault=fault_node.reshape(1, scen),
            inv=inv_blocks.reshape(nreg, blk),
            amp=amp,
            phase=phase,
            fault_step=fault_step.reshape(1, scen),
            fault_cond=fault_cond.reshape(1, scen),
        ),
        scalar=("list_a", "list_b", "list_conv", "list_fault"),
        scratch=(
            pltpu.VMEM((whole, blk), F32),
            pltpu.VMEM((STEPS * nblk, blk), F32),
        ),
        cost=(4e9, 2e7),
    )
    wave = ((2, scen, lines), F32)
    mades, backs, carry = {}, {}, {}
    squares = swap_near = swap_far = sent = shared = None
    for pair in range(STEPS // 2):
        t0 = 2 * pair
        final = t0 + 2 >= STEPS
        ins = dict(
            delay=line_delay,
            atten=line_atten,
            admit=line_yc,
            recv=recv,
            base_p=model.base_p,
            fault_base=model.fault_base,
            fault_ratio=model.fault_ratio,
            **carry,
        )
        if t0 - maxd < 0:
            ins.update(hist_b=hist_ub)
        if pair:
            ins.update(swap_near=swap_near, swap_far=swap_far, into_prev=sent, row=model.row)
            ins.update(m_high=matrix.m_high, m_low=matrix.m_low, fault_p=matrix.fault_p)
        else:
            ins.update(far_in=far_in)
            ins.update(row=model.row, mark=model.mark, rows=model.rows)
        first = max(0, pair - 3)
        ins.update(backs={k: v for k, v in backs.items() if k >= first})
        if not final:
            ins.update(made={k: v for k, v in mades.items() if k >= pair - 2})
            if t0 + 2 - maxd < 0:
                ins.update(hist_a=hist_ua)
        outs = dict(x=((4 * scen, points), BF16), coef=((2 * scen, LANES), F32))
        if not final:
            outs.update(
                swap_far=wave,
                swap_near=wave,
                into=wave,
                state=((2, scen, width), F32),
                current=((scen, width), F32),
            )
            if t0 + 4 < STEPS:
                outs.update(out=wave)
            if pair:
                outs.update(back=wave)
            else:
                outs.update(
                    m_high=((points, points), BF16),
                    m_low=((points, points), BF16),
                    fault_p=((scen, points), F32),
                )
        else:
            shape = (regions, scen // 2, LANES) if packed else (scen, width)
            outs.update(current=(shape, F32))
        made = call(
            functools.partial(advance_body, (lines, width, scen, cap, maxd, packed), pair),
            "advance",
            ins,
            outs,
        )
        if not pair:
            matrix = made
        if not final:
            sent, into = into, made.into
            swap_far = swapped(made.swap_far, "region", 1)
            swap_near = swapped(made.swap_near, "region", 0)
            if t0 + 4 < STEPS:
                mades[pair] = made.out
            if pair:
                backs[pair - 1] = made.back
            carry = dict(state=made.state, current=made.current)
        else:
            current = made.current
            if packed:
                returned = lax.all_to_all(current, "region", split_axis=0, concat_axis=0, tiled=True)
            else:
                order = jnp.bitwise_xor(lax.axis_index("region"), jnp.arange(regions))
                current = current.reshape(scen, regions, cap).transpose(1, 0, 2)[order]
                returned = lax.all_to_all(current, "region", split_axis=0, concat_axis=0, tiled=True)
                returned = returned.transpose(1, 0, 2).reshape(scen, width)
        ins = dict(
            x=made.x,
            coef=made.coef,
            fault_mark=model.fault_mark,
            fault_z=model.fault_z,
        )
        if pair:
            ins.update(squares=squares, **shared)
        else:
            ins.update(mark=model.mark)
        outs = dict(squares=((1, nreg), F32))
        if final:
            outs.update(volts=((scen, nreg), F32))
        if not pair:
            outs.update(
                base=((STEPS, nreg), F32),
                column=((points, blk), jnp.int32),
                zcat=((nreg, 2 * blk), BF16),
            )
        full = call(
            functools.partial(full_body, (nblk, points, scen), pair),
            "full",
            ins,
            outs,
            hbm={} if pair else dict(inv=inv_blocks, amp=amp, phase=phase),
            cost=(4e9, 1e7),
        )
        squares = full.squares
        if not pair:
            shared = dict(base=full.base, column=full.column, zcat=full.zcat)

    parts = [squares]
    for offset in range(1, count):
        pairs = [(source, source ^ offset) for source in range(count)]
        parts.append(lax.ppermute(squares, "scen", pairs))
    settled = call(
        functools.partial(settle_body, (regions, cap, scen, group, packed)),
        "settle",
        dict(slots=recv_slot, recv=returned, volts=full.volts),
        dict(current=((scen, group), F32)),
        relays=dict(volts=((scen, nreg), F32)),
    )
    tail = call(
        functools.partial(rms_body, scen, count),
        "rms",
        dict(parts=parts),
        dict(rms=((1, nreg), F32)),
    )
    return settled.volts, settled.current, tail.rms.reshape(nreg)


def solution(mesh):
    return jax.shard_map(
        per_device,
        mesh=mesh,
        in_specs=(
            P("region", None, None),
            P("region"),
            P("region"),
            P("region", None),
            P("region", None),
            P("region", None),
            P("region", None),
            P("region", None),
            P("region", None, "scen", None),
            P("region", None, "scen", None),
            P("region", None, None),
            P("region", None),
            P(None, "region"),
            P(None, "scen", "region"),
            P("scen"),
            P("scen"),
            P("scen"),
        ),
        out_specs=(P("scen", "region"), P("scen", "region"), P("region")),
        check_vma=False,
    )
```

```python
import functools
from types import SimpleNamespace as Space

import jax
import jax.numpy as jnp
from jax import lax
from jax.experimental import pallas as pl
from jax.experimental.pallas import tpu as pltpu
from jax.sharding import PartitionSpec as P

STEPS = 8
DMIN = 2
LANES = 128
WIDE = 4
PAIR = "pair"
OMEGA = 0.01884955592153876
EPS = 1e-06
F32 = jnp.float32
BF16 = jnp.bfloat16
NN = (((1,), (0,)), ((), ()))
NT = (((1,), (1,)), ((), ()))


def shifted(value, axis, steps):
    count = lax.axis_size(axis)
    pairs = [(source, (source + steps) % count) for source in range(count)]
    return lax.ppermute(value, axis, pairs)


def mirrored(value, axis, offset):
    count = lax.axis_size(axis)
    return lax.ppermute(value, axis, [(source, source ^ offset) for source in range(count)])


def swapped(value, axis, first):
    count = lax.axis_size(axis)
    pairs = []
    for left in range(first, count, 2):
        right = (left + 1) % count
        pairs += [(left, right), (right, left)]
    return lax.ppermute(value, axis, pairs)


def call(
    body,
    name,
    ins,
    outs,
    scratch=(),
    hbm=None,
    hbm_outs=None,
    relays=None,
    scalar=(),
    limit=20 << 20,
    cost=None,
):
    leaves, tree = jax.tree.flatten(ins)
    far, far_outs = dict(hbm or {}), dict(hbm_outs or {})
    far = {key: pltpu.with_memory_space_constraint(far[key], pltpu.HBM) for key in far}
    relays = dict(relays or {})
    names = [list(far), list(outs), list(far_outs), list(relays)]
    sizes = [len(leaves)] + [len(group) for group in names] + [len(far), len(far_outs)]
    ends = [sum(sizes[:k]) for k in range(len(sizes) + 1)]
    count = len(far) + len(far_outs) + len(relays)

    def kernel(*refs):
        near, sources, near_outs, targets, relayed, held, made = [
            refs[ends[k] : ends[k + 1]] for k in range(len(sizes))
        ]
        rest = refs[ends[-1] :]
        arriving, leaving, pending = {}, {}, []
        if count:
            sems, rest = rest[0], rest[1:]
            for k, key in enumerate(far):
                arriving[key] = pltpu.make_async_copy(sources[k], held[k], sems.at[k])
                arriving[key].start()
            for k, key in enumerate(far_outs):
                leaving[key] = pltpu.make_async_copy(made[k], targets[k], sems.at[len(far) + k])
        i = Space(**jax.tree.unflatten(tree, near), **dict(zip(far, held)))
        o = Space(**dict(zip(outs, near_outs)), **dict(zip(far_outs, made)))
        for k, key in enumerate(relays):
            copy = pltpu.make_async_copy(getattr(i, key), relayed[k], sems.at[count - 1 - k])
            copy.start()
            pending.append(copy)

        def flush(key):
            pending.append(leaving.pop(key))
            pending[-1].start()

        i.ready = lambda *keys: [arriving.pop(key).wait() for key in keys]
        o.flush = flush
        body(i, o, *rest)
        for key in list(leaving):
            flush(key)
        for copy in pending:
            copy.wait()

    buffers = [
        (pltpu.SMEM if key in scalar else pltpu.VMEM)(value.shape, value.dtype)
        for key, value in far.items()
    ]
    buffers += [pltpu.VMEM(*shape) for shape in far_outs.values()]
    if count:
        buffers.append(pltpu.SemaphoreType.DMA((count,)))
    every = list(outs.values()) + list(far_outs.values()) + list(relays.values())
    near_spec, far_spec = (pl.BlockSpec(memory_space=space) for space in (pltpu.VMEM, pltpu.HBM))
    flops, moved = cost or (1e9, 4e6)
    results = pl.pallas_call(
        kernel,
        name=name,
        out_shape=[jax.ShapeDtypeStruct(*shape) for shape in every],
        in_specs=[near_spec] * len(leaves) + [far_spec] * len(far),
        out_specs=[near_spec] * len(outs) + [far_spec] * (len(far_outs) + len(relays)),
        scratch_shapes=buffers + list(scratch),
        compiler_params=pltpu.CompilerParams(vmem_limit_bytes=limit),
        cost_estimate=pl.CostEstimate(
            flops=int(flops), bytes_accessed=int(moved), transcendentals=0
        ),
    )(*leaves, *far.values())
    return Space(**dict(zip(names[1] + names[2] + names[3], results)))


def iota(shape, dim):
    return lax.broadcasted_iota(jnp.int32, shape, dim)


def onehot(mask):
    return jnp.where(mask, 1.0, 0.0).astype(BF16)


def owner_of(mark):
    return jnp.max(mark.astype(F32), axis=1, keepdims=True)


def dot(left, right, dims=NN):
    return lax.dot_general(left, right, dims, preferred_element_type=F32)


def split2(value):
    high = value.astype(BF16)
    return high, (value - high.astype(F32)).astype(BF16)


def split3(value):
    high, rest = value.astype(BF16), value
    rest = value - high.astype(F32)
    mid = rest.astype(BF16)
    return high, mid, (rest - mid.astype(F32)).astype(BF16)


def product3(left, right_high, right_low, dims=NN):
    rows = left.shape[0]
    high, low = split2(left)
    both = dot(jnp.concatenate([high, low], axis=0), right_high, dims)
    return both[:rows] + both[rows:] + dot(high, right_low, dims)


def as_column(row, size):
    wide = jnp.broadcast_to(row, (size, size))
    return jnp.sum(
        jnp.where(iota((size, size), 0) == iota((size, size), 1), wide, 0.0), axis=1, keepdims=True
    )


def pick(wave, delays, instant, maxd):
    total = None
    for lag in range(DMIN, maxd + 1):
        term = jnp.where(delays == lag, wave(instant - lag), 0.0)
        total = term if total is None else total + term
    return total


def start_body(sizes, i, o):
    regions, cap, half, scen, group, maxd = sizes
    packed = 2 * cap == LANES
    i.ready("slots", "par", "state")
    slots = i.slots[...]
    rows = iota((regions * 2 * cap, group), 0)
    away = jnp.bitwise_xor(slots // cap, lax.axis_index("region"))
    if packed:
        target = away * (2 * cap) + slots % cap
        moved = target + cap
    else:
        target = away * cap + slots % cap
        moved = target + regions * cap
    left, right = onehot(rows == target), onehot(rows == moved)
    pad = jnp.zeros((half - scen - 6, group), F32)
    upper = jnp.concatenate([i.state[0], i.par[...], pad], axis=0)
    lower = jnp.concatenate([i.state[1], jnp.zeros((half - scen, group), F32)], axis=0)
    buffer = None
    for part, mask in ((upper, left), (lower, right)):
        both = dot(jnp.concatenate(split3(part), axis=0), mask, NT)
        value = both[:half] + both[half : 2 * half] + both[2 * half :]
        buffer = value if buffer is None else buffer + value
    if packed:
        for index in range(regions):
            slot = buffer[:, index * LANES : (index + 1) * LANES]
            (o.odd if index % 2 else o.even)[index // 2] = slot
    else:
        o.send[...] = buffer
    i.ready("hist", "delay")
    delays = i.delay[...]
    for step in range(2):
        o.into[step] = pick(lambda t: i.hist[0, t + maxd], delays, step, maxd)


def pair_body(count, i, o):
    for k in range(count):
        target = getattr(o, PAIR + str(k))
        target[0], target[1] = i.even[k], i.odd[k]


def sources(amp, phase):
    instant = iota((STEPS, amp.shape[1]), 0).astype(F32)
    return amp * jnp.cos(OMEGA * instant + phase)


def rows_body(sizes, i, o, taken, source_rows):
    nreg, nblk, lines, regions, cap, scen = sizes
    blk = LANES
    width = regions * cap
    points = 2 * lines + width
    whole = points + blk
    region = lax.axis_index("region")
    groups = [jnp.bitwise_xor(region, away) for away in range(regions)]
    i.ready("end_a", "end_b", "conv", "fault_node")
    o.row[...] = jnp.full((1, whole), -1, jnp.int32)
    o.row[:, 0:lines] = i.end_a[...]
    o.row[:, lines : 2 * lines] = i.end_b[...]
    for away in range(regions):
        first = 2 * lines + away * cap
        o.row[:, first : first + cap] = i.conv[0, pl.ds(groups[away], 1), :]
    fault = i.fault_node[...] - region * nreg
    o.row[:, points : points + scen] = jnp.where((fault >= 0) & (fault < nreg), fault, -1)
    row = o.row[...]
    whole_row = row.astype(F32)
    column = jnp.transpose(jnp.broadcast_to(whole_row, (blk, whole))).astype(jnp.int32)
    inside = (column & 127) == iota((whole, blk), 1)
    o.mark[...] = jnp.where(inside, (column >> 7).astype(F32), -1.0).astype(BF16)
    o.fault_mark[...] = o.mark[points : points + scen, :].astype(F32)
    o.column[...] = column[:points]
    i.ready("list_a", "list_b", "list_conv", "list_fault", "inv")
    for p in range(points + scen):
        if p < lines:
            node = i.list_a[0, p]
        elif p < 2 * lines:
            node = i.list_b[0, p - lines]
        elif p < points:
            away, place = divmod(p - 2 * lines, cap)
            node = jnp.maximum(i.list_conv[0, groups[away], place], 0)
        else:
            node = jnp.clip(i.list_fault[0, p - points] - region * nreg, 0, nreg - 1)
        taken[p : p + 1, :] = i.inv[pl.ds(node, 1), :]
    taken[points + scen :, :] = jnp.zeros((blk - scen, blk), F32)
    high, low = split2(jnp.where(column >= 0, taken[...], 0.0))
    o.rows[:, :blk] = high
    o.rows[:, blk:] = low
    i.ready("amp", "phase", "fault_step", "fault_cond")
    source = sources(i.amp[...], i.phase[...])
    for k in range(nblk):
        here = slice(k * blk, (k + 1) * blk)
        source_rows[k * STEPS : (k + 1) * STEPS, :] = source[:, here]
        z_high, z_low = split2(i.inv[here, :])
        o.zcat[here, :blk], o.zcat[here, blk:] = z_high, z_low
        o.base[:, here] = product3(source[:, here], z_high, z_low)
    spread = product3(source_rows[...], o.rows[:, :blk], o.rows[:, blk:], NT)
    row_blk = row >> 7
    at_points = jnp.zeros((STEPS, whole), F32)
    for k in range(nblk):
        at_points = at_points + jnp.where(row_blk == k, spread[k * STEPS : (k + 1) * STEPS], 0.0)
    o.base_p[...] = at_points[:, :points]
    tail = jnp.concatenate(
        [at_points[:, points:], jnp.zeros((blk - STEPS, blk), F32)], axis=0
    )
    o.fault_base[...] = jnp.transpose(tail)[:scen]
    fault_rows = o.rows[points : points + scen, :].astype(F32)
    fault_z = fault_rows[:, :blk] + fault_rows[:, blk:]
    o.fault_z[...] = fault_z
    self_imp = jnp.sum(
        jnp.where(iota((scen, blk), 1) == (column[points : points + scen] & 127), fault_z, 0.0),
        axis=1,
        keepdims=True,
    )
    cond = as_column(i.fault_cond[...], scen)
    closes = as_column(i.fault_step[...].astype(F32), scen)
    ratio = cond / (1.0 + cond * self_imp)
    o.fault_ratio[...] = jnp.where(
        closes <= iota((scen, blk), 1).astype(F32), jnp.broadcast_to(ratio, (scen, blk)), 0.0
    )


def between_body(points, scen, i, o):
    blk = LANES
    row = i.row[:, :points]
    row_blk = (row >> 7).astype(F32)
    inside = onehot(iota((blk, points), 0) == (row & 127))
    for k in range(points // blk):
        here = slice(k * blk, (k + 1) * blk)
        same = owner_of(i.mark[here, :]) == row_blk
        both = dot(jnp.concatenate([i.rows[here, :blk], i.rows[here, blk:]], axis=0), inside)
        o.m_high[here, :] = jnp.where(same, both[:blk], 0.0).astype(BF16)
        o.m_low[here, :] = jnp.where(same, both[blk:], 0.0).astype(BF16)
    here = slice(points, points + scen)
    both = dot(jnp.concatenate([i.rows[here, :blk], i.rows[here, blk:]], axis=0), inside)
    same = owner_of(i.mark[here, :]) == row_blk
    o.fault_p[...] = jnp.where(same, both[:scen] + both[scen:], 0.0)


def advance_body(sizes, pair, i, o):
    lines, width, scen, cap, maxd, packed = sizes
    t0 = 2 * pair
    delays = i.delay[...]
    scale = i.atten[...]
    twice = 2.0 * i.admit[...]
    last = STEPS - 1

    even = lax.rem(lax.axis_index("region"), 2) == 0
    fresh = {}
    if pair:
        far_in = [jnp.where(even, i.swap_far[j], i.swap_near[j]) for j in range(2)]
        for j in range(2):
            far_volts = jnp.where(even, i.swap_near[j], i.swap_far[j])
            fresh[t0 - 2 + j] = scale * (twice * far_volts - i.into_prev[j])
            if hasattr(o, "back"):
                o.back[j] = fresh[t0 - 2 + j]
    else:
        far_in = [i.far_in[j] for j in range(2)]

    def back(t):
        if t in fresh:
            return fresh[t]
        if t < 0:
            return i.hist_b[0, t + maxd]
        return i.backs[t // 2][t % 2]

    made = {}

    def out(t):
        if t in made:
            return made[t]
        if t < 0:
            return i.hist_a[0, t + maxd]
        return i.made[t // 2][t % 2]

    points = 2 * lines + width
    known = i if pair else o
    if not pair:
        between_body(points, scen, i, o)
    live = i.row[:, 2 * lines : 2 * lines + width] >= 0
    if packed:
        recv = i.recv[::-1]
        low = iota((1, LANES), 1) < cap
        params = []
        for row in range(6):
            pieces = []
            for j in range(width // LANES):
                one = recv[j][0, scen + row : scen + row + 1, :]
                two = recv[j][1, scen + row : scen + row + 1, :]
                pieces.append(jnp.where(low, one, pltpu.roll(two, cap, 1)))
            params.append(jnp.concatenate(pieces, axis=1))
    else:
        params = [i.recv[0, scen + row : scen + row + 1, :] for row in range(6)]
    params[5] = jnp.where(live, params[5], 1.0)

    def drive(second):
        return params[5] * jnp.tanh((params[4] + second) / params[5])

    if pair:
        first, second, current = i.state[0], i.state[1], i.current[...]
    else:
        if packed:
            ups, downs = [], []
            for j in range(width // LANES):
                one, two = recv[j][0, :scen], recv[j][1, :scen]
                ups.append(jnp.where(low, one, pltpu.roll(two, cap, 1)))
                downs.append(jnp.where(low, pltpu.roll(one, cap, 1), two))
            first, second = jnp.concatenate(ups, axis=1), jnp.concatenate(downs, axis=1)
        else:
            first, second = i.recv[0, :scen], i.recv[1, :scen]
        current = drive(second)

    fault_p = known.fault_p[...]
    ends = 2 * lines
    arrivals = [pick(back, delays, t0 + j, maxd) for j in range(2)]
    waves = jnp.concatenate(
        [jnp.concatenate([arrivals[j], far_in[j]], axis=1) for j in range(2)], axis=0
    )
    pairs = split2(waves)
    for part in range(2):
        o.x[part * 2 * scen : (part + 1) * 2 * scen, :ends] = pairs[part]
    both = dot(jnp.concatenate(pairs, axis=0), known.m_high[:ends, :])
    volts = both[: 2 * scen] + both[2 * scen :] + dot(pairs[0], known.m_low[:ends, :])
    base = [jnp.broadcast_to(i.base_p[t0 + j : t0 + j + 1, :], (scen, points)) for j in range(2)]
    volts = volts + jnp.concatenate(base, axis=0)
    fault_ends, fault_conv = fault_p[:, :ends], fault_p[:, ends:]
    wave_fault = jnp.sum(
        waves * jnp.concatenate([fault_ends, fault_ends], axis=0), axis=1, keepdims=True
    )
    highs, lows, coefs = [], [], []
    for j in range(2):
        here = slice(j * scen, (j + 1) * scen)
        high, low_part = split2(current)
        highs.append(high)
        lows.append(low_part)
        o.x[j * scen : (j + 1) * scen, ends:] = high
        o.x[(2 + j) * scen : (3 + j) * scen, ends:] = low_part
        both = dot(jnp.concatenate([high, low_part], axis=0), known.m_high[ends:, ends:])
        node = both[:scen] + both[scen:] + dot(high, known.m_low[ends:, ends:])
        at_fault = i.fault_base[:, t0 + j : t0 + j + 1] + wave_fault[here]
        at_fault = at_fault + jnp.sum(current * fault_conv, axis=1, keepdims=True)
        coef = i.fault_ratio[:, t0 + j : t0 + j + 1] * at_fault
        coefs.append(coef)
        o.coef[here, :] = jnp.broadcast_to(coef, (scen, LANES))
        node = node + volts[here, ends:] - fault_conv * coef
        first = params[1] * first + params[2] * (params[0] - node)
        second = second + params[3] * (first - second)
        current = drive(second)
    sides = []
    if t0 <= last - DMIN:
        both = dot(jnp.concatenate(highs + lows, axis=0), known.m_high[ends:, :ends])
        more = both[: 2 * scen] + both[2 * scen :]
        more = more + dot(jnp.concatenate(highs, axis=0), known.m_low[ends:, :ends])
        for j in range(2):
            here = slice(j * scen, (j + 1) * scen)
            line = volts[here, :ends] + more[here] - fault_ends * coefs[j]
            made[t0 + j] = scale * (twice * line[:, :lines] - arrivals[j])
            sides.append(line[:, lines:])
            if hasattr(o, "out"):
                o.out[j] = made[t0 + j]
    if sides:
        for j in range(2):
            onward = pick(out, delays, t0 + 2 + j, maxd)
            if hasattr(o, "into"):
                o.into[j] = onward
            o.swap_near[j] = jnp.where(even, onward, sides[j])
            o.swap_far[j] = jnp.where(even, sides[j], onward)
    if hasattr(o, "state"):
        o.state[0] = first
        o.state[1] = second
    if t0 + 2 < STEPS or not packed:
        o.current[...] = current
    else:
        half = scen // 2
        region = lax.axis_index("region")
        for j in range(width // LANES):
            mine = current[:, j * LANES : (j + 1) * LANES]
            top, bottom = mine[:half], mine[half:]
            pieces = (
                jnp.where(low, top, pltpu.roll(bottom, cap, 1)),
                jnp.where(low, pltpu.roll(top, cap, 1), bottom),
            )
            for k in range(2):
                o.current[jnp.bitwise_xor(region, 2 * j + k)] = pieces[k]


def full_body(sizes, pair, i, o):
    nblk, points, scen = sizes
    blk = LANES
    t0 = 2 * pair
    fault_z = i.fault_z[...]
    fault_blk = owner_of(i.fault_mark[...])
    x = i.x[...]
    coef = i.coef[...]
    lane = iota((points, blk), 1)
    for k in range(0, nblk, WIDE):
        mine = jnp.concatenate(
            [onehot(i.column[...] == lane + (k + j) * blk) for j in range(WIDE)], axis=1
        )
        both = dot(x, mine)
        inject = both[: 2 * scen] + both[2 * scen :]
        for j in range(WIDE):
            here = slice((k + j) * blk, (k + j + 1) * blk)
            z = i.zcat[here, :]
            volts = product3(inject[:, j * blk : (j + 1) * blk], z[:, :blk], z[:, blk:])
            base = [
                jnp.broadcast_to(i.base[t0 + m : t0 + m + 1, here], (scen, blk))
                for m in range(2)
            ]
            zcol = jnp.where(fault_blk == k + j, fault_z, 0.0)
            volts = volts + jnp.concatenate(base, axis=0)
            volts = volts - jnp.concatenate([zcol, zcol], axis=0) * coef
            total = jnp.sum(volts * volts, axis=0, keepdims=True)
            if hasattr(i, "squares"):
                total = total + i.squares[:, here]
            o.squares[:, here] = total
            if hasattr(o, "volts"):
                o.volts[:, here] = volts[scen:]


def place_body(i, o):
    o.done[...] = jnp.zeros((1, LANES), F32)


def finish_body(sizes, i, o):
    regions, cap, scen, group, count, packed = sizes
    parts = [i.parts[k][...] for k in range(count)]
    while len(parts) > 1:
        parts = [parts[k] + parts[k + 1] for k in range(0, len(parts), 2)]
    o.rms[...] = jnp.sqrt(parts[0] / (scen * count * STEPS) + EPS)
    slots = i.slots[...]
    if packed:
        half = scen // 2
        lane = iota((LANES, group), 0)
        top = bottom = None
        for region in range(regions):
            left = onehot((lane < cap) & (slots == region * cap + lane))
            right = onehot((lane >= cap) & (slots == (region - 1) * cap + lane))
            both = dot(
                jnp.concatenate(split3(i.recv[region]), axis=0),
                jnp.concatenate([left, right], axis=1),
            )
            value = both[:half] + both[half : 2 * half] + both[2 * half :]
            top = value if top is None else top + value
        o.current[:half, :] = top[:, :group]
        o.current[half:, :] = top[:, group:]
    else:
        mask = onehot(iota((regions * cap, group), 0) == slots)
        both = dot(jnp.concatenate(split3(i.recv[...]), axis=0), mask)
        o.current[...] = both[:scen] + both[scen : 2 * scen] + both[2 * scen :]


def per_device(
    inv_blocks,
    src_amp,
    src_phase,
    line_a,
    line_b,
    line_delay,
    line_yc,
    line_atten,
    hist_ua,
    hist_ub,
    send_node,
    recv_slot,
    conv_par,
    conv_state,
    fault_node,
    fault_step,
    fault_cond,
):
    nblk, blk = inv_blocks.shape[0], inv_blocks.shape[1]
    nreg = nblk * blk
    lines = line_a.shape[1]
    maxd, scen = hist_ua.shape[1], hist_ua.shape[2]
    regions, cap = send_node.shape[1], send_node.shape[2]
    group = recv_slot.shape[1]
    width = regions * cap
    points = 2 * lines + width
    count = lax.axis_size("scen")
    packed = 2 * cap == LANES
    half = scen + 8

    amp, phase = src_amp.reshape(1, nreg), src_phase.reshape(1, nreg)
    if packed:
        slot_outs = dict.fromkeys(("even", "odd"), ((regions // 2, half, LANES), F32))
    else:
        slot_outs = dict(send=((half, regions * 2 * cap), F32))
    head = call(
        functools.partial(start_body, (regions, cap, half, scen, group, maxd)),
        "start",
        {},
        dict(into=((2, scen, lines), F32), **slot_outs),
        hbm=dict(
            slots=recv_slot, par=conv_par, state=conv_state, hist=hist_ua, delay=line_delay
        ),
    )
    if packed:
        even, odd = head.even, head.odd
    else:
        slots = head.send.reshape(half, 2, regions, cap).transpose(2, 1, 0, 3)
        even, odd = slots[0::2], slots[1::2]
    odd = mirrored(odd, "region", 1)
    into = head.into
    far_in = shifted(into, "region", 1)
    if packed:
        shape = ((2, half, LANES), F32)
        couples = call(
            functools.partial(pair_body, regions // 2),
            "couple",
            dict(even=even, odd=odd),
            {PAIR + str(k): shape for k in range(regions // 2)},
        )
        couples = [getattr(couples, PAIR + str(k)) for k in range(regions // 2)]
    else:
        couples = [jnp.stack([even[k], odd[k]]) for k in range(regions // 2)]
    recv = couples[:1]
    for k in range(1, regions // 2):
        recv.append(mirrored(couples[k], "region", 2 * k))
    recv.reverse()
    if not packed:
        recv = jnp.concatenate(recv[::-1], axis=0).transpose(1, 2, 0, 3).reshape(2, half, width)

    whole = points + blk
    model = call(
        functools.partial(rows_body, (nreg, nblk, lines, regions, cap, scen)),
        "rows",
        {},
        dict(
            row=((1, whole), jnp.int32),
            mark=((whole, blk), BF16),
            fault_mark=((scen, blk), F32),
            column=((points, blk), jnp.int32),
            zcat=((nreg, 2 * blk), BF16),
            base=((STEPS, nreg), F32),
            rows=((whole, 2 * blk), BF16),
            base_p=((STEPS, points), F32),
            fault_z=((scen, blk), F32),
            fault_base=((scen, blk), F32),
            fault_ratio=((scen, blk), F32),
        ),
        hbm=dict(
            end_a=line_a,
            end_b=line_b,
            conv=send_node,
            fault_node=fault_node.reshape(1, scen),
            list_a=line_a,
            list_b=line_b,
            list_conv=send_node,
            list_fault=fault_node.reshape(1, scen),
            inv=inv_blocks.reshape(nreg, blk),
            amp=amp,
            phase=phase,
            fault_step=fault_step.reshape(1, scen),
            fault_cond=fault_cond.reshape(1, scen),
        ),
        scalar=("list_a", "list_b", "list_conv", "list_fault"),
        scratch=(
            pltpu.VMEM((whole, blk), F32),
            pltpu.VMEM((STEPS * nblk, blk), F32),
        ),
        cost=(4e9, 2e7),
    )
    wave = ((2, scen, lines), F32)
    mades, backs, carry = {}, {}, {}
    squares = swap_near = swap_far = sent = None
    for pair in range(STEPS // 2):
        t0 = 2 * pair
        final = t0 + 2 >= STEPS
        ins = dict(
            delay=line_delay,
            atten=line_atten,
            admit=line_yc,
            recv=recv,
            base_p=model.base_p,
            fault_base=model.fault_base,
            fault_ratio=model.fault_ratio,
            **carry,
        )
        if t0 - maxd < 0:
            ins.update(hist_b=hist_ub)
        if pair:
            ins.update(swap_near=swap_near, swap_far=swap_far, into_prev=sent, row=model.row)
            ins.update(m_high=matrix.m_high, m_low=matrix.m_low, fault_p=matrix.fault_p)
        else:
            ins.update(far_in=far_in)
            ins.update(row=model.row, mark=model.mark, rows=model.rows)
        first = max(0, pair - 3)
        ins.update(backs={k: v for k, v in backs.items() if k >= first})
        if not final:
            ins.update(made={k: v for k, v in mades.items() if k >= pair - 2})
            if t0 + 2 - maxd < 0:
                ins.update(hist_a=hist_ua)
        outs = dict(x=((4 * scen, points), BF16), coef=((2 * scen, LANES), F32))
        if not final:
            outs.update(
                swap_far=wave,
                swap_near=wave,
                state=((2, scen, width), F32),
                current=((scen, width), F32),
            )
            if t0 + 4 < STEPS:
                outs.update(out=wave, into=wave)
            if pair:
                outs.update(back=wave)
            else:
                outs.update(
                    m_high=((points, points), BF16),
                    m_low=((points, points), BF16),
                    fault_p=((scen, points), F32),
                )
        else:
            shape = (regions, scen // 2, LANES) if packed else (scen, width)
            outs.update(current=(shape, F32))
        made = call(
            functools.partial(advance_body, (lines, width, scen, cap, maxd, packed), pair),
            "advance",
            ins,
            outs,
        )
        if not pair:
            matrix = made
        if not final:
            sent = into
            if t0 + 4 < STEPS:
                into = made.into
            swap_far = swapped(made.swap_far, "region", 1)
            swap_near = swapped(made.swap_near, "region", 0)
            if t0 + 4 < STEPS:
                mades[pair] = made.out
            if pair:
                backs[pair - 1] = made.back
            carry = dict(state=made.state, current=made.current)
        else:
            current = made.current
            if packed:
                returned = lax.all_to_all(current, "region", split_axis=0, concat_axis=0, tiled=True)
            else:
                order = jnp.bitwise_xor(lax.axis_index("region"), jnp.arange(regions))
                current = current.reshape(scen, regions, cap).transpose(1, 0, 2)[order]
                returned = lax.all_to_all(current, "region", split_axis=0, concat_axis=0, tiled=True)
                returned = returned.transpose(1, 0, 2).reshape(scen, width)
        ins = dict(
            x=made.x,
            coef=made.coef,
            fault_mark=model.fault_mark,
            fault_z=model.fault_z,
            column=model.column,
            zcat=model.zcat,
            base=model.base,
        )
        if pair:
            ins.update(squares=squares)
        outs = dict(squares=((1, nreg), F32))
        if final:
            outs.update(volts=((scen, nreg), F32))
        full = call(
            functools.partial(full_body, (nblk, points, scen), pair),
            "full",
            ins,
            outs,
            cost=(4e9, 1e7),
        )
        squares = full.squares

    parts = [squares]
    for offset in range(1, count):
        pairs = [(source, source ^ offset) for source in range(count)]
        parts.append(lax.ppermute(squares, "scen", pairs))
    placed = call(
        place_body,
        "place",
        dict(volts=full.volts),
        dict(done=((1, LANES), F32)),
        relays=dict(volts=((scen, nreg), F32)),
    )
    tail = call(
        functools.partial(finish_body, (regions, cap, scen, group, count, packed)),
        "finish",
        dict(slots=recv_slot, recv=returned, parts=parts, after=placed.done),
        dict(rms=((1, nreg), F32), current=((scen, group), F32)),
    )
    return placed.volts, tail.current, tail.rms.reshape(nreg)


def solution(mesh):
    return jax.shard_map(
        per_device,
        mesh=mesh,
        in_specs=(
            P("region", None, None),
            P("region"),
            P("region"),
            P("region", None),
            P("region", None),
            P("region", None),
            P("region", None),
            P("region", None),
            P("region", None, "scen", None),
            P("region", None, "scen", None),
            P("region", None, None),
            P("region", None),
            P(None, "region"),
            P(None, "scen", "region"),
            P("scen"),
            P("scen"),
            P("scen"),
        ),
        out_specs=(P("scen", "region"), P("scen", "region"), P("region")),
        check_vma=False,
    )
```

```python
import functools
from types import SimpleNamespace as Space

import jax
import jax.numpy as jnp
from jax import lax
from jax.experimental import pallas as pl
from jax.experimental.pallas import tpu as pltpu
from jax.sharding import PartitionSpec as P

STEPS = 8
DMIN = 2
LANES = 128
WIDE = 4
PAIR = "pair"
OMEGA = 0.01884955592153876
EPS = 1e-06
F32 = jnp.float32
BF16 = jnp.bfloat16
NN = (((1,), (0,)), ((), ()))
NT = (((1,), (1,)), ((), ()))


def shifted(value, axis, steps):
    count = lax.axis_size(axis)
    pairs = [(source, (source + steps) % count) for source in range(count)]
    return lax.ppermute(value, axis, pairs)


def mirrored(value, axis, offset):
    count = lax.axis_size(axis)
    return lax.ppermute(value, axis, [(source, source ^ offset) for source in range(count)])


def swapped(value, axis, first):
    count = lax.axis_size(axis)
    pairs = []
    for left in range(first, count, 2):
        right = (left + 1) % count
        pairs += [(left, right), (right, left)]
    return lax.ppermute(value, axis, pairs)


def call(
    body,
    name,
    ins,
    outs,
    scratch=(),
    hbm=None,
    hbm_outs=None,
    relays=None,
    scalar=(),
    limit=20 << 20,
    cost=None,
):
    leaves, tree = jax.tree.flatten(ins)
    far, far_outs = dict(hbm or {}), dict(hbm_outs or {})
    far = {key: pltpu.with_memory_space_constraint(far[key], pltpu.HBM) for key in far}
    relays = dict(relays or {})
    names = [list(far), list(outs), list(far_outs), list(relays)]
    sizes = [len(leaves)] + [len(group) for group in names] + [len(far), len(far_outs)]
    ends = [sum(sizes[:k]) for k in range(len(sizes) + 1)]
    count = len(far) + len(far_outs) + len(relays)

    def kernel(*refs):
        near, sources, near_outs, targets, relayed, held, made = [
            refs[ends[k] : ends[k + 1]] for k in range(len(sizes))
        ]
        rest = refs[ends[-1] :]
        arriving, leaving, pending = {}, {}, []
        if count:
            sems, rest = rest[0], rest[1:]
            for k, key in enumerate(far):
                arriving[key] = pltpu.make_async_copy(sources[k], held[k], sems.at[k])
                arriving[key].start()
            for k, key in enumerate(far_outs):
                leaving[key] = pltpu.make_async_copy(made[k], targets[k], sems.at[len(far) + k])
        i = Space(**jax.tree.unflatten(tree, near), **dict(zip(far, held)))
        o = Space(**dict(zip(outs, near_outs)), **dict(zip(far_outs, made)))
        for k, key in enumerate(relays):
            copy = pltpu.make_async_copy(getattr(i, key), relayed[k], sems.at[count - 1 - k])
            copy.start()
            pending.append(copy)

        def flush(key):
            pending.append(leaving.pop(key))
            pending[-1].start()

        i.ready = lambda *keys: [arriving.pop(key).wait() for key in keys]
        o.flush = flush
        body(i, o, *rest)
        for key in list(leaving):
            flush(key)
        for copy in pending:
            copy.wait()

    buffers = [
        (pltpu.SMEM if key in scalar else pltpu.VMEM)(value.shape, value.dtype)
        for key, value in far.items()
    ]
    buffers += [pltpu.VMEM(*shape) for shape in far_outs.values()]
    if count:
        buffers.append(pltpu.SemaphoreType.DMA((count,)))
    every = list(outs.values()) + list(far_outs.values()) + list(relays.values())
    near_spec, far_spec = (pl.BlockSpec(memory_space=space) for space in (pltpu.VMEM, pltpu.HBM))
    flops, moved = cost or (1e9, 4e6)
    results = pl.pallas_call(
        kernel,
        name=name,
        out_shape=[jax.ShapeDtypeStruct(*shape) for shape in every],
        in_specs=[near_spec] * len(leaves) + [far_spec] * len(far),
        out_specs=[near_spec] * len(outs) + [far_spec] * (len(far_outs) + len(relays)),
        scratch_shapes=buffers + list(scratch),
        compiler_params=pltpu.CompilerParams(vmem_limit_bytes=limit),
        cost_estimate=pl.CostEstimate(
            flops=int(flops), bytes_accessed=int(moved), transcendentals=0
        ),
    )(*leaves, *far.values())
    return Space(**dict(zip(names[1] + names[2] + names[3], results)))


def iota(shape, dim):
    return lax.broadcasted_iota(jnp.int32, shape, dim)


def onehot(mask):
    return jnp.where(mask, 1.0, 0.0).astype(BF16)


def owner_of(mark):
    return jnp.max(mark.astype(F32), axis=1, keepdims=True)


def dot(left, right, dims=NN):
    return lax.dot_general(left, right, dims, preferred_element_type=F32)


def split2(value):
    high = value.astype(BF16)
    return high, (value - high.astype(F32)).astype(BF16)


def split3(value):
    high, rest = value.astype(BF16), value
    rest = value - high.astype(F32)
    mid = rest.astype(BF16)
    return high, mid, (rest - mid.astype(F32)).astype(BF16)


def product3(left, right_high, right_low, dims=NN):
    rows = left.shape[0]
    high, low = split2(left)
    both = dot(jnp.concatenate([high, low], axis=0), right_high, dims)
    return both[:rows] + both[rows:] + dot(high, right_low, dims)


def as_column(row, size):
    wide = jnp.broadcast_to(row, (size, size))
    return jnp.sum(
        jnp.where(iota((size, size), 0) == iota((size, size), 1), wide, 0.0), axis=1, keepdims=True
    )


def pick(wave, delays, instant, maxd):
    total = None
    for lag in range(DMIN, maxd + 1):
        term = jnp.where(delays == lag, wave(instant - lag), 0.0)
        total = term if total is None else total + term
    return total


def start_body(sizes, i, o):
    regions, cap, half, scen, group, maxd = sizes
    packed = 2 * cap == LANES
    i.ready("slots", "par", "state")
    slots = i.slots[...]
    rows = iota((regions * 2 * cap, group), 0)
    away = jnp.bitwise_xor(slots // cap, lax.axis_index("region"))
    if packed:
        target = away * (2 * cap) + slots % cap
        moved = target + cap
    else:
        target = away * cap + slots % cap
        moved = target + regions * cap
    left, right = onehot(rows == target), onehot(rows == moved)
    pad = jnp.zeros((half - scen - 6, group), F32)
    upper = jnp.concatenate([i.state[0], i.par[...], pad], axis=0)
    lower = jnp.concatenate([i.state[1], jnp.zeros((half - scen, group), F32)], axis=0)
    buffer = None
    for part, mask in ((upper, left), (lower, right)):
        both = dot(jnp.concatenate(split3(part), axis=0), mask, NT)
        value = both[:half] + both[half : 2 * half] + both[2 * half :]
        buffer = value if buffer is None else buffer + value
    if packed:
        for index in range(regions):
            slot = buffer[:, index * LANES : (index + 1) * LANES]
            (o.odd if index % 2 else o.even)[index // 2] = slot
    else:
        o.send[...] = buffer
    i.ready("hist", "delay")
    delays = i.delay[...]
    for step in range(2):
        o.into[step] = pick(lambda t: i.hist[0, t + maxd], delays, step, maxd)


def pair_body(count, i, o):
    for k in range(count):
        target = getattr(o, PAIR + str(k))
        target[0], target[1] = i.even[k], i.odd[k]


def sources(amp, phase):
    instant = iota((STEPS, amp.shape[1]), 0).astype(F32)
    return amp * jnp.cos(OMEGA * instant + phase)


def tables_body(sizes, i, o):
    nreg, nblk, lines, regions, cap, scen = sizes
    blk = LANES
    width = regions * cap
    points = 2 * lines + width
    whole = points + blk
    region = lax.axis_index("region")
    groups = [jnp.bitwise_xor(region, away) for away in range(regions)]
    i.ready("end_a", "end_b", "conv", "fault_node")
    o.row[...] = jnp.full((1, whole), -1, jnp.int32)
    o.row[:, 0:lines] = i.end_a[...]
    o.row[:, lines : 2 * lines] = i.end_b[...]
    for away in range(regions):
        first = 2 * lines + away * cap
        o.row[:, first : first + cap] = i.conv[0, pl.ds(groups[away], 1), :]
    fault = i.fault_node[...] - region * nreg
    o.row[:, points : points + scen] = jnp.where((fault >= 0) & (fault < nreg), fault, -1)
    row = o.row[...]
    whole_row = row.astype(F32)
    column = jnp.transpose(jnp.broadcast_to(whole_row, (blk, whole))).astype(jnp.int32)
    inside = (column & 127) == iota((whole, blk), 1)
    o.mark[...] = jnp.where(inside, (column >> 7).astype(F32), -1.0).astype(BF16)
    o.fault_mark[...] = o.mark[points : points + scen, :].astype(F32)
    o.column[...] = column
    i.ready("amp", "phase", "inv")
    source = sources(i.amp[...], i.phase[...])
    for k in range(nblk):
        here = slice(k * blk, (k + 1) * blk)
        o.source_rows[k * STEPS : (k + 1) * STEPS, :] = source[:, here]
        z_high, z_low = split2(i.inv[here, :])
        o.zcat[here, :blk], o.zcat[here, blk:] = z_high, z_low
        o.base[:, here] = product3(source[:, here], z_high, z_low)


def rows_body(sizes, i, o, taken):
    nreg, nblk, lines, regions, cap, scen = sizes
    blk = LANES
    points = 2 * lines + regions * cap
    whole = points + blk
    region = lax.axis_index("region")
    groups = [jnp.bitwise_xor(region, away) for away in range(regions)]
    row, column = i.row[...], i.column[...]
    i.ready("list_a", "list_b", "list_conv", "list_fault", "inv")
    for p in range(points + scen):
        if p < lines:
            node = i.list_a[0, p]
        elif p < 2 * lines:
            node = i.list_b[0, p - lines]
        elif p < points:
            away, place = divmod(p - 2 * lines, cap)
            node = jnp.maximum(i.list_conv[0, groups[away], place], 0)
        else:
            node = jnp.clip(i.list_fault[0, p - points] - region * nreg, 0, nreg - 1)
        taken[p : p + 1, :] = i.inv[pl.ds(node, 1), :]
    taken[points + scen :, :] = jnp.zeros((blk - scen, blk), F32)
    high, low = split2(jnp.where(column >= 0, taken[...], 0.0))
    o.rows[:, :blk] = high
    o.rows[:, blk:] = low
    i.ready("fault_step", "fault_cond")
    spread = product3(i.source_rows[...], o.rows[:, :blk], o.rows[:, blk:], NT)
    row_blk = row >> 7
    at_points = jnp.zeros((STEPS, whole), F32)
    for k in range(nblk):
        at_points = at_points + jnp.where(row_blk == k, spread[k * STEPS : (k + 1) * STEPS], 0.0)
    o.base_p[...] = at_points[:, :points]
    tail = jnp.concatenate(
        [at_points[:, points:], jnp.zeros((blk - STEPS, blk), F32)], axis=0
    )
    o.fault_base[...] = jnp.transpose(tail)[:scen]
    fault_rows = o.rows[points : points + scen, :].astype(F32)
    fault_z = fault_rows[:, :blk] + fault_rows[:, blk:]
    o.fault_z[...] = fault_z
    self_imp = jnp.sum(
        jnp.where(iota((scen, blk), 1) == (column[points : points + scen] & 127), fault_z, 0.0),
        axis=1,
        keepdims=True,
    )
    cond = as_column(i.fault_cond[...], scen)
    closes = as_column(i.fault_step[...].astype(F32), scen)
    ratio = cond / (1.0 + cond * self_imp)
    o.fault_ratio[...] = jnp.where(
        closes <= iota((scen, blk), 1).astype(F32), jnp.broadcast_to(ratio, (scen, blk)), 0.0
    )


def between_body(points, scen, i, o):
    blk = LANES
    row = i.row[:, :points]
    row_blk = (row >> 7).astype(F32)
    inside = onehot(iota((blk, points), 0) == (row & 127))
    for k in range(points // blk):
        here = slice(k * blk, (k + 1) * blk)
        same = owner_of(i.mark[here, :]) == row_blk
        both = dot(jnp.concatenate([i.rows[here, :blk], i.rows[here, blk:]], axis=0), inside)
        o.m_high[here, :] = jnp.where(same, both[:blk], 0.0).astype(BF16)
        o.m_low[here, :] = jnp.where(same, both[blk:], 0.0).astype(BF16)
    here = slice(points, points + scen)
    both = dot(jnp.concatenate([i.rows[here, :blk], i.rows[here, blk:]], axis=0), inside)
    same = owner_of(i.mark[here, :]) == row_blk
    o.fault_p[...] = jnp.where(same, both[:scen] + both[scen:], 0.0)


def advance_body(sizes, pair, i, o):
    lines, width, scen, cap, maxd, packed = sizes
    t0 = 2 * pair
    delays = i.delay[...]
    scale = i.atten[...]
    twice = 2.0 * i.admit[...]
    last = STEPS - 1

    even = lax.rem(lax.axis_index("region"), 2) == 0
    fresh = {}
    if pair:
        far_in = [jnp.where(even, i.swap_far[j], i.swap_near[j]) for j in range(2)]
        for j in range(2):
            far_volts = jnp.where(even, i.swap_near[j], i.swap_far[j])
            fresh[t0 - 2 + j] = scale * (twice * far_volts - i.into_prev[j])
            if hasattr(o, "back"):
                o.back[j] = fresh[t0 - 2 + j]
    else:
        far_in = [i.far_in[j] for j in range(2)]

    def back(t):
        if t in fresh:
            return fresh[t]
        if t < 0:
            return i.hist_b[0, t + maxd]
        return i.backs[t // 2][t % 2]

    made = {}

    def out(t):
        if t in made:
            return made[t]
        if t < 0:
            return i.hist_a[0, t + maxd]
        return i.made[t // 2][t % 2]

    points = 2 * lines + width
    known = i if pair else o
    if not pair:
        between_body(points, scen, i, o)
    live = i.row[:, 2 * lines : 2 * lines + width] >= 0
    if packed:
        recv = i.recv[::-1]
        low = iota((1, LANES), 1) < cap
        params = []
        for row in range(6):
            pieces = []
            for j in range(width // LANES):
                one = recv[j][0, scen + row : scen + row + 1, :]
                two = recv[j][1, scen + row : scen + row + 1, :]
                pieces.append(jnp.where(low, one, pltpu.roll(two, cap, 1)))
            params.append(jnp.concatenate(pieces, axis=1))
    else:
        params = [i.recv[0, scen + row : scen + row + 1, :] for row in range(6)]
    params[5] = jnp.where(live, params[5], 1.0)

    def drive(second):
        return params[5] * jnp.tanh((params[4] + second) / params[5])

    if pair:
        first, second, current = i.state[0], i.state[1], i.current[...]
    else:
        if packed:
            ups, downs = [], []
            for j in range(width // LANES):
                one, two = recv[j][0, :scen], recv[j][1, :scen]
                ups.append(jnp.where(low, one, pltpu.roll(two, cap, 1)))
                downs.append(jnp.where(low, pltpu.roll(one, cap, 1), two))
            first, second = jnp.concatenate(ups, axis=1), jnp.concatenate(downs, axis=1)
        else:
            first, second = i.recv[0, :scen], i.recv[1, :scen]
        current = drive(second)

    fault_p = known.fault_p[...]
    ends = 2 * lines
    arrivals = [pick(back, delays, t0 + j, maxd) for j in range(2)]
    waves = jnp.concatenate(
        [jnp.concatenate([arrivals[j], far_in[j]], axis=1) for j in range(2)], axis=0
    )
    pairs = split2(waves)
    for part in range(2):
        o.x[part * 2 * scen : (part + 1) * 2 * scen, :ends] = pairs[part]
    both = dot(jnp.concatenate(pairs, axis=0), known.m_high[:ends, :])
    volts = both[: 2 * scen] + both[2 * scen :] + dot(pairs[0], known.m_low[:ends, :])
    base = [jnp.broadcast_to(i.base_p[t0 + j : t0 + j + 1, :], (scen, points)) for j in range(2)]
    volts = volts + jnp.concatenate(base, axis=0)
    fault_ends, fault_conv = fault_p[:, :ends], fault_p[:, ends:]
    wave_fault = jnp.sum(
        waves * jnp.concatenate([fault_ends, fault_ends], axis=0), axis=1, keepdims=True
    )
    highs, lows, coefs = [], [], []
    for j in range(2):
        here = slice(j * scen, (j + 1) * scen)
        high, low_part = split2(current)
        highs.append(high)
        lows.append(low_part)
        o.x[j * scen : (j + 1) * scen, ends:] = high
        o.x[(2 + j) * scen : (3 + j) * scen, ends:] = low_part
        both = dot(jnp.concatenate([high, low_part], axis=0), known.m_high[ends:, ends:])
        node = both[:scen] + both[scen:] + dot(high, known.m_low[ends:, ends:])
        at_fault = i.fault_base[:, t0 + j : t0 + j + 1] + wave_fault[here]
        at_fault = at_fault + jnp.sum(current * fault_conv, axis=1, keepdims=True)
        coef = i.fault_ratio[:, t0 + j : t0 + j + 1] * at_fault
        coefs.append(coef)
        o.coef[here, :] = jnp.broadcast_to(coef, (scen, LANES))
        node = node + volts[here, ends:] - fault_conv * coef
        first = params[1] * first + params[2] * (params[0] - node)
        second = second + params[3] * (first - second)
        current = drive(second)
    sides = []
    if t0 <= last - DMIN:
        both = dot(jnp.concatenate(highs + lows, axis=0), known.m_high[ends:, :ends])
        more = both[: 2 * scen] + both[2 * scen :]
        more = more + dot(jnp.concatenate(highs, axis=0), known.m_low[ends:, :ends])
        for j in range(2):
            here = slice(j * scen, (j + 1) * scen)
            line = volts[here, :ends] + more[here] - fault_ends * coefs[j]
            made[t0 + j] = scale * (twice * line[:, :lines] - arrivals[j])
            sides.append(line[:, lines:])
            if hasattr(o, "out"):
                o.out[j] = made[t0 + j]
    if sides:
        for j in range(2):
            onward = pick(out, delays, t0 + 2 + j, maxd)
            if hasattr(o, "into"):
                o.into[j] = onward
            o.swap_near[j] = jnp.where(even, onward, sides[j])
            o.swap_far[j] = jnp.where(even, sides[j], onward)
    if hasattr(o, "state"):
        o.state[0] = first
        o.state[1] = second
    if t0 + 2 < STEPS or not packed:
        o.current[...] = current
    else:
        half = scen // 2
        region = lax.axis_index("region")
        for j in range(width // LANES):
            mine = current[:, j * LANES : (j + 1) * LANES]
            top, bottom = mine[:half], mine[half:]
            pieces = (
                jnp.where(low, top, pltpu.roll(bottom, cap, 1)),
                jnp.where(low, pltpu.roll(top, cap, 1), bottom),
            )
            for k in range(2):
                o.current[jnp.bitwise_xor(region, 2 * j + k)] = pieces[k]


def full_body(sizes, pair, i, o):
    nblk, points, scen = sizes
    blk = LANES
    t0 = 2 * pair
    fault_z = i.fault_z[...]
    fault_blk = owner_of(i.fault_mark[...])
    x = i.x[...]
    coef = i.coef[...]
    lane = iota((points, blk), 1)
    for k in range(0, nblk, WIDE):
        mine = jnp.concatenate(
            [onehot(i.column[:points, :] == lane + (k + j) * blk) for j in range(WIDE)], axis=1
        )
        both = dot(x, mine)
        inject = both[: 2 * scen] + both[2 * scen :]
        for j in range(WIDE):
            here = slice((k + j) * blk, (k + j + 1) * blk)
            z = i.zcat[here, :]
            volts = product3(inject[:, j * blk : (j + 1) * blk], z[:, :blk], z[:, blk:])
            base = [
                jnp.broadcast_to(i.base[t0 + m : t0 + m + 1, here], (scen, blk))
                for m in range(2)
            ]
            zcol = jnp.where(fault_blk == k + j, fault_z, 0.0)
            volts = volts + jnp.concatenate(base, axis=0)
            volts = volts - jnp.concatenate([zcol, zcol], axis=0) * coef
            total = jnp.sum(volts * volts, axis=0, keepdims=True)
            if hasattr(i, "squares"):
                total = total + i.squares[:, here]
            o.squares[:, here] = total
            if hasattr(o, "volts"):
                o.volts[:, here] = volts[scen:]


def place_body(i, o):
    o.done[...] = jnp.zeros((1, LANES), F32)


def finish_body(sizes, i, o):
    regions, cap, scen, group, count, packed = sizes
    parts = [i.parts[k][...] for k in range(count)]
    while len(parts) > 1:
        parts = [parts[k] + parts[k + 1] for k in range(0, len(parts), 2)]
    o.rms[...] = jnp.sqrt(parts[0] / (scen * count * STEPS) + EPS)
    slots = i.slots[...]
    if packed:
        half = scen // 2
        lane = iota((LANES, group), 0)
        top = bottom = None
        for region in range(regions):
            left = onehot((lane < cap) & (slots == region * cap + lane))
            right = onehot((lane >= cap) & (slots == (region - 1) * cap + lane))
            both = dot(
                jnp.concatenate(split3(i.recv[region]), axis=0),
                jnp.concatenate([left, right], axis=1),
            )
            value = both[:half] + both[half : 2 * half] + both[2 * half :]
            top = value if top is None else top + value
        o.current[:half, :] = top[:, :group]
        o.current[half:, :] = top[:, group:]
    else:
        mask = onehot(iota((regions * cap, group), 0) == slots)
        both = dot(jnp.concatenate(split3(i.recv[...]), axis=0), mask)
        o.current[...] = both[:scen] + both[scen : 2 * scen] + both[2 * scen :]


def per_device(
    inv_blocks,
    src_amp,
    src_phase,
    line_a,
    line_b,
    line_delay,
    line_yc,
    line_atten,
    hist_ua,
    hist_ub,
    send_node,
    recv_slot,
    conv_par,
    conv_state,
    fault_node,
    fault_step,
    fault_cond,
):
    nblk, blk = inv_blocks.shape[0], inv_blocks.shape[1]
    nreg = nblk * blk
    lines = line_a.shape[1]
    maxd, scen = hist_ua.shape[1], hist_ua.shape[2]
    regions, cap = send_node.shape[1], send_node.shape[2]
    group = recv_slot.shape[1]
    width = regions * cap
    points = 2 * lines + width
    count = lax.axis_size("scen")
    packed = 2 * cap == LANES
    half = scen + 8

    amp, phase = src_amp.reshape(1, nreg), src_phase.reshape(1, nreg)
    if packed:
        slot_outs = dict.fromkeys(("even", "odd"), ((regions // 2, half, LANES), F32))
    else:
        slot_outs = dict(send=((half, regions * 2 * cap), F32))
    head = call(
        functools.partial(start_body, (regions, cap, half, scen, group, maxd)),
        "start",
        {},
        dict(into=((2, scen, lines), F32), **slot_outs),
        hbm=dict(
            slots=recv_slot, par=conv_par, state=conv_state, hist=hist_ua, delay=line_delay
        ),
    )
    if packed:
        even, odd = head.even, head.odd
    else:
        slots = head.send.reshape(half, 2, regions, cap).transpose(2, 1, 0, 3)
        even, odd = slots[0::2], slots[1::2]
    odd = mirrored(odd, "region", 1)
    into = head.into
    whole = points + blk
    inv_flat = inv_blocks.reshape(nreg, blk)
    tables = call(
        functools.partial(tables_body, (nreg, nblk, lines, regions, cap, scen)),
        "tables",
        {},
        dict(
            row=((1, whole), jnp.int32),
            mark=((whole, blk), BF16),
            fault_mark=((scen, blk), F32),
            column=((whole, blk), jnp.int32),
            zcat=((nreg, 2 * blk), BF16),
            base=((STEPS, nreg), F32),
            source_rows=((STEPS * nblk, blk), F32),
        ),
        hbm=dict(
            end_a=line_a,
            end_b=line_b,
            conv=send_node,
            fault_node=fault_node.reshape(1, scen),
            inv=inv_flat,
            amp=amp,
            phase=phase,
        ),
        cost=(4e9, 2e7),
    )
    later, fault_mark = lax.optimization_barrier((into, tables.fault_mark))
    far_in = shifted(later, "region", 1)
    if packed:
        shape = ((2, half, LANES), F32)
        couples = call(
            functools.partial(pair_body, regions // 2),
            "couple",
            dict(even=even, odd=odd, after=fault_mark),
            {PAIR + str(k): shape for k in range(regions // 2)},
        )
        couples = [getattr(couples, PAIR + str(k)) for k in range(regions // 2)]
    else:
        couples = [jnp.stack([even[k], odd[k]]) for k in range(regions // 2)]
    recv = couples[:1]
    for k in range(1, regions // 2):
        recv.append(mirrored(couples[k], "region", 2 * k))
    recv.reverse()
    if not packed:
        recv = jnp.concatenate(recv[::-1], axis=0).transpose(1, 2, 0, 3).reshape(2, half, width)

    model = call(
        functools.partial(rows_body, (nreg, nblk, lines, regions, cap, scen)),
        "rows",
        dict(row=tables.row, column=tables.column, source_rows=tables.source_rows),
        dict(
            rows=((whole, 2 * blk), BF16),
            base_p=((STEPS, points), F32),
            fault_z=((scen, blk), F32),
            fault_base=((scen, blk), F32),
            fault_ratio=((scen, blk), F32),
        ),
        hbm=dict(
            list_a=line_a,
            list_b=line_b,
            list_conv=send_node,
            list_fault=fault_node.reshape(1, scen),
            inv=inv_flat,
            fault_step=fault_step.reshape(1, scen),
            fault_cond=fault_cond.reshape(1, scen),
        ),
        scalar=("list_a", "list_b", "list_conv", "list_fault"),
        scratch=(pltpu.VMEM((whole, blk), F32),),
        cost=(4e9, 2e7),
    )

    wave = ((2, scen, lines), F32)
    mades, backs, carry = {}, {}, {}
    squares = swap_near = swap_far = sent = None
    for pair in range(STEPS // 2):
        t0 = 2 * pair
        final = t0 + 2 >= STEPS
        ins = dict(
            delay=line_delay,
            atten=line_atten,
            admit=line_yc,
            recv=recv,
            base_p=model.base_p,
            fault_base=model.fault_base,
            fault_ratio=model.fault_ratio,
            **carry,
        )
        if t0 - maxd < 0:
            ins.update(hist_b=hist_ub)
        if pair:
            ins.update(swap_near=swap_near, swap_far=swap_far, into_prev=sent, row=tables.row)
            ins.update(m_high=matrix.m_high, m_low=matrix.m_low, fault_p=matrix.fault_p)
        else:
            ins.update(far_in=far_in)
            ins.update(row=tables.row, mark=tables.mark, rows=model.rows)
        first = max(0, pair - 3)
        ins.update(backs={k: v for k, v in backs.items() if k >= first})
        if not final:
            ins.update(made={k: v for k, v in mades.items() if k >= pair - 2})
            if t0 + 2 - maxd < 0:
                ins.update(hist_a=hist_ua)
        outs = dict(x=((4 * scen, points), BF16), coef=((2 * scen, LANES), F32))
        if not final:
            outs.update(
                swap_far=wave,
                swap_near=wave,
                state=((2, scen, width), F32),
                current=((scen, width), F32),
            )
            if t0 + 4 < STEPS:
                outs.update(out=wave, into=wave)
            if pair:
                outs.update(back=wave)
            else:
                outs.update(
                    m_high=((points, points), BF16),
                    m_low=((points, points), BF16),
                    fault_p=((scen, points), F32),
                )
        else:
            shape = (regions, scen // 2, LANES) if packed else (scen, width)
            outs.update(current=(shape, F32))
        made = call(
            functools.partial(advance_body, (lines, width, scen, cap, maxd, packed), pair),
            "advance",
            ins,
            outs,
        )
        if not pair:
            matrix = made
        if not final:
            sent = into
            if t0 + 4 < STEPS:
                into = made.into
            swap_far = swapped(made.swap_far, "region", 1)
            swap_near = swapped(made.swap_near, "region", 0)
            if t0 + 4 < STEPS:
                mades[pair] = made.out
            if pair:
                backs[pair - 1] = made.back
            carry = dict(state=made.state, current=made.current)
        else:
            current = made.current
            if packed:
                returned = lax.all_to_all(current, "region", split_axis=0, concat_axis=0, tiled=True)
            else:
                order = jnp.bitwise_xor(lax.axis_index("region"), jnp.arange(regions))
                current = current.reshape(scen, regions, cap).transpose(1, 0, 2)[order]
                returned = lax.all_to_all(current, "region", split_axis=0, concat_axis=0, tiled=True)
                returned = returned.transpose(1, 0, 2).reshape(scen, width)
        ins = dict(
            x=made.x,
            coef=made.coef,
            fault_mark=tables.fault_mark,
            fault_z=model.fault_z,
            column=tables.column,
            zcat=tables.zcat,
            base=tables.base,
        )
        if pair:
            ins.update(squares=squares)
        outs = dict(squares=((1, nreg), F32))
        if final:
            outs.update(volts=((scen, nreg), F32))
        full = call(
            functools.partial(full_body, (nblk, points, scen), pair),
            "full",
            ins,
            outs,
            cost=(4e9, 1e7),
        )
        squares = full.squares

    parts = [squares]
    for offset in range(1, count):
        pairs = [(source, source ^ offset) for source in range(count)]
        parts.append(lax.ppermute(squares, "scen", pairs))
    placed = call(
        place_body,
        "place",
        dict(volts=full.volts),
        dict(done=((1, LANES), F32)),
        relays=dict(volts=((scen, nreg), F32)),
    )
    tail = call(
        functools.partial(finish_body, (regions, cap, scen, group, count, packed)),
        "finish",
        dict(slots=recv_slot, recv=returned, parts=parts, after=placed.done),
        dict(rms=((1, nreg), F32), current=((scen, group), F32)),
    )
    return placed.volts, tail.current, tail.rms.reshape(nreg)


def solution(mesh):
    return jax.shard_map(
        per_device,
        mesh=mesh,
        in_specs=(
            P("region", None, None),
            P("region"),
            P("region"),
            P("region", None),
            P("region", None),
            P("region", None),
            P("region", None),
            P("region", None),
            P("region", None, "scen", None),
            P("region", None, "scen", None),
            P("region", None, None),
            P("region", None),
            P(None, "region"),
            P(None, "scen", "region"),
            P("scen"),
            P("scen"),
            P("scen"),
        ),
        out_specs=(P("scen", "region"), P("scen", "region"), P("region")),
        check_vma=False,
    )
```

```python
import functools
from types import SimpleNamespace as Space

import jax
import jax.numpy as jnp
from jax import lax
from jax.experimental import pallas as pl
from jax.experimental.pallas import tpu as pltpu
from jax.sharding import PartitionSpec as P

STEPS = 8
DMIN = 2
LANES = 128
WIDE = 4
PAIR = "pair"
OMEGA = 0.01884955592153876
EPS = 1e-06
F32 = jnp.float32
BF16 = jnp.bfloat16
NN = (((1,), (0,)), ((), ()))
NT = (((1,), (1,)), ((), ()))


def shifted(value, axis, steps):
    count = lax.axis_size(axis)
    pairs = [(source, (source + steps) % count) for source in range(count)]
    return lax.ppermute(value, axis, pairs)


def mirrored(value, axis, offset):
    count = lax.axis_size(axis)
    return lax.ppermute(value, axis, [(source, source ^ offset) for source in range(count)])


def swapped(value, axis, first):
    count = lax.axis_size(axis)
    pairs = []
    for left in range(first, count, 2):
        right = (left + 1) % count
        pairs += [(left, right), (right, left)]
    return lax.ppermute(value, axis, pairs)


def call(
    body,
    name,
    ins,
    outs,
    scratch=(),
    hbm=None,
    hbm_outs=None,
    relays=None,
    scalar=(),
    limit=20 << 20,
    cost=None,
):
    leaves, tree = jax.tree.flatten(ins)
    far, far_outs = dict(hbm or {}), dict(hbm_outs or {})
    far = {key: pltpu.with_memory_space_constraint(far[key], pltpu.HBM) for key in far}
    relays = dict(relays or {})
    names = [list(far), list(outs), list(far_outs), list(relays)]
    sizes = [len(leaves)] + [len(group) for group in names] + [len(far), len(far_outs)]
    ends = [sum(sizes[:k]) for k in range(len(sizes) + 1)]
    count = len(far) + len(far_outs) + len(relays)

    def kernel(*refs):
        near, sources, near_outs, targets, relayed, held, made = [
            refs[ends[k] : ends[k + 1]] for k in range(len(sizes))
        ]
        rest = refs[ends[-1] :]
        arriving, leaving, pending = {}, {}, []
        if count:
            sems, rest = rest[0], rest[1:]
            for k, key in enumerate(far):
                arriving[key] = pltpu.make_async_copy(sources[k], held[k], sems.at[k])
                arriving[key].start()
            for k, key in enumerate(far_outs):
                leaving[key] = pltpu.make_async_copy(made[k], targets[k], sems.at[len(far) + k])
        i = Space(**jax.tree.unflatten(tree, near), **dict(zip(far, held)))
        o = Space(**dict(zip(outs, near_outs)), **dict(zip(far_outs, made)))
        for k, key in enumerate(relays):
            copy = pltpu.make_async_copy(getattr(i, key), relayed[k], sems.at[count - 1 - k])
            copy.start()
            pending.append(copy)

        def flush(key):
            pending.append(leaving.pop(key))
            pending[-1].start()

        i.ready = lambda *keys: [arriving.pop(key).wait() for key in keys]
        o.flush = flush
        body(i, o, *rest)
        for key in list(leaving):
            flush(key)
        for copy in pending:
            copy.wait()

    buffers = [
        (pltpu.SMEM if key in scalar else pltpu.VMEM)(value.shape, value.dtype)
        for key, value in far.items()
    ]
    buffers += [pltpu.VMEM(*shape) for shape in far_outs.values()]
    if count:
        buffers.append(pltpu.SemaphoreType.DMA((count,)))
    every = list(outs.values()) + list(far_outs.values()) + list(relays.values())
    near_spec, far_spec = (pl.BlockSpec(memory_space=space) for space in (pltpu.VMEM, pltpu.HBM))
    flops, moved = cost or (1e9, 4e6)
    results = pl.pallas_call(
        kernel,
        name=name,
        out_shape=[jax.ShapeDtypeStruct(*shape) for shape in every],
        in_specs=[near_spec] * len(leaves) + [far_spec] * len(far),
        out_specs=[near_spec] * len(outs) + [far_spec] * (len(far_outs) + len(relays)),
        scratch_shapes=buffers + list(scratch),
        compiler_params=pltpu.CompilerParams(vmem_limit_bytes=limit),
        cost_estimate=pl.CostEstimate(
            flops=int(flops), bytes_accessed=int(moved), transcendentals=0
        ),
    )(*leaves, *far.values())
    return Space(**dict(zip(names[1] + names[2] + names[3], results)))


def iota(shape, dim):
    return lax.broadcasted_iota(jnp.int32, shape, dim)


def onehot(mask):
    return jnp.where(mask, 1.0, 0.0).astype(BF16)


def owner_of(mark):
    return jnp.max(mark.astype(F32), axis=1, keepdims=True)


def dot(left, right, dims=NN):
    return lax.dot_general(left, right, dims, preferred_element_type=F32)


def split2(value):
    high = value.astype(BF16)
    return high, (value - high.astype(F32)).astype(BF16)


def split3(value):
    high, rest = value.astype(BF16), value
    rest = value - high.astype(F32)
    mid = rest.astype(BF16)
    return high, mid, (rest - mid.astype(F32)).astype(BF16)


def product3(left, right_high, right_low, dims=NN):
    rows = left.shape[0]
    high, low = split2(left)
    both = dot(jnp.concatenate([high, low], axis=0), right_high, dims)
    return both[:rows] + both[rows:] + dot(high, right_low, dims)


def as_column(row, size):
    wide = jnp.broadcast_to(row, (size, size))
    return jnp.sum(
        jnp.where(iota((size, size), 0) == iota((size, size), 1), wide, 0.0), axis=1, keepdims=True
    )


def pick(wave, delays, instant, maxd):
    total = None
    for lag in range(DMIN, maxd + 1):
        term = jnp.where(delays == lag, wave(instant - lag), 0.0)
        total = term if total is None else total + term
    return total


def start_body(sizes, i, o):
    regions, cap, half, scen, group, maxd = sizes
    packed = 2 * cap == LANES
    i.ready("slots", "par", "state")
    slots = i.slots[...]
    rows = iota((regions * 2 * cap, group), 0)
    away = jnp.bitwise_xor(slots // cap, lax.axis_index("region"))
    if packed:
        target = away * (2 * cap) + slots % cap
        moved = target + cap
    else:
        target = away * cap + slots % cap
        moved = target + regions * cap
    left, right = onehot(rows == target), onehot(rows == moved)
    pad = jnp.zeros((half - scen - 6, group), F32)
    upper = jnp.concatenate([i.state[0], i.par[...], pad], axis=0)
    lower = jnp.concatenate([i.state[1], jnp.zeros((half - scen, group), F32)], axis=0)
    buffer = None
    for part, mask in ((upper, left), (lower, right)):
        both = dot(jnp.concatenate(split3(part), axis=0), mask, NT)
        value = both[:half] + both[half : 2 * half] + both[2 * half :]
        buffer = value if buffer is None else buffer + value
    if packed:
        for index in range(regions):
            slot = buffer[:, index * LANES : (index + 1) * LANES]
            (o.odd if index % 2 else o.even)[index // 2] = slot
    else:
        o.send[...] = buffer
    i.ready("hist", "delay")
    delays = i.delay[...]
    for step in range(2):
        o.into[step] = pick(lambda t: i.hist[0, t + maxd], delays, step, maxd)


def pair_body(count, i, o):
    for k in range(count):
        target = getattr(o, PAIR + str(k))
        target[0], target[1] = i.even[k], i.odd[k]


def sources(amp, phase):
    instant = iota((STEPS, amp.shape[1]), 0).astype(F32)
    return amp * jnp.cos(OMEGA * instant + phase)


def tables_body(sizes, i, o):
    nreg, nblk, lines, regions, cap, scen = sizes
    blk = LANES
    width = regions * cap
    points = 2 * lines + width
    whole = points + blk
    region = lax.axis_index("region")
    groups = [jnp.bitwise_xor(region, away) for away in range(regions)]
    i.ready("end_a", "end_b", "conv", "fault_node")
    o.row[...] = jnp.full((1, whole), -1, jnp.int32)
    o.row[:, 0:lines] = i.end_a[...]
    o.row[:, lines : 2 * lines] = i.end_b[...]
    for away in range(regions):
        first = 2 * lines + away * cap
        o.row[:, first : first + cap] = i.conv[0, pl.ds(groups[away], 1), :]
    fault = i.fault_node[...] - region * nreg
    o.row[:, points : points + scen] = jnp.where((fault >= 0) & (fault < nreg), fault, -1)
    row = o.row[...]
    whole_row = row.astype(F32)
    column = jnp.transpose(jnp.broadcast_to(whole_row, (blk, whole))).astype(jnp.int32)
    inside = (column & 127) == iota((whole, blk), 1)
    o.mark[...] = jnp.where(inside, (column >> 7).astype(F32), -1.0).astype(BF16)
    o.fault_mark[...] = o.mark[points : points + scen, :].astype(F32)
    o.column[...] = column
    i.ready("amp", "phase", "inv")
    source = sources(i.amp[...], i.phase[...])
    for k in range(nblk):
        here = slice(k * blk, (k + 1) * blk)
        o.source_rows[k * STEPS : (k + 1) * STEPS, :] = source[:, here]
        z_high, z_low = split2(i.inv[here, :])
        o.zcat[here, :blk], o.zcat[here, blk:] = z_high, z_low
        o.base[:, here] = product3(source[:, here], z_high, z_low)


def rows_body(sizes, i, o, taken):
    nreg, nblk, lines, regions, cap, scen = sizes
    blk = LANES
    points = 2 * lines + regions * cap
    whole = points + blk
    region = lax.axis_index("region")
    groups = [jnp.bitwise_xor(region, away) for away in range(regions)]
    row, column = i.row[...], i.column[...]
    i.ready("list_a", "list_b", "list_conv", "list_fault", "inv")
    for p in range(points + scen):
        if p < lines:
            node = i.list_a[0, p]
        elif p < 2 * lines:
            node = i.list_b[0, p - lines]
        elif p < points:
            away, place = divmod(p - 2 * lines, cap)
            node = jnp.maximum(i.list_conv[0, groups[away], place], 0)
        else:
            node = jnp.clip(i.list_fault[0, p - points] - region * nreg, 0, nreg - 1)
        taken[p : p + 1, :] = i.inv[pl.ds(node, 1), :]
    taken[points + scen :, :] = jnp.zeros((blk - scen, blk), F32)
    high, low = split2(jnp.where(column >= 0, taken[...], 0.0))
    o.rows[:, :blk] = high
    o.rows[:, blk:] = low
    i.ready("fault_step", "fault_cond")
    spread = product3(i.source_rows[...], o.rows[:, :blk], o.rows[:, blk:], NT)
    row_blk = row >> 7
    at_points = jnp.zeros((STEPS, whole), F32)
    for k in range(nblk):
        at_points = at_points + jnp.where(row_blk == k, spread[k * STEPS : (k + 1) * STEPS], 0.0)
    o.base_p[...] = at_points[:, :points]
    tail = jnp.concatenate(
        [at_points[:, points:], jnp.zeros((blk - STEPS, blk), F32)], axis=0
    )
    o.fault_base[...] = jnp.transpose(tail)[:scen]
    fault_rows = o.rows[points : points + scen, :].astype(F32)
    fault_z = fault_rows[:, :blk] + fault_rows[:, blk:]
    o.fault_z[...] = fault_z
    self_imp = jnp.sum(
        jnp.where(iota((scen, blk), 1) == (column[points : points + scen] & 127), fault_z, 0.0),
        axis=1,
        keepdims=True,
    )
    cond = as_column(i.fault_cond[...], scen)
    closes = as_column(i.fault_step[...].astype(F32), scen)
    ratio = cond / (1.0 + cond * self_imp)
    o.fault_ratio[...] = jnp.where(
        closes <= iota((scen, blk), 1).astype(F32), jnp.broadcast_to(ratio, (scen, blk)), 0.0
    )
    between_body(points, scen, Space(row=i.row, mark=i.mark, rows=o.rows), o)


def between_body(points, scen, i, o):
    blk = LANES
    row = i.row[:, :points]
    row_blk = (row >> 7).astype(F32)
    inside = onehot(iota((blk, points), 0) == (row & 127))
    for k in range(points // blk):
        here = slice(k * blk, (k + 1) * blk)
        same = owner_of(i.mark[here, :]) == row_blk
        both = dot(jnp.concatenate([i.rows[here, :blk], i.rows[here, blk:]], axis=0), inside)
        o.m_high[here, :] = jnp.where(same, both[:blk], 0.0).astype(BF16)
        o.m_low[here, :] = jnp.where(same, both[blk:], 0.0).astype(BF16)
    here = slice(points, points + scen)
    both = dot(jnp.concatenate([i.rows[here, :blk], i.rows[here, blk:]], axis=0), inside)
    same = owner_of(i.mark[here, :]) == row_blk
    o.fault_p[...] = jnp.where(same, both[:scen] + both[scen:], 0.0)


def advance_body(sizes, pair, i, o):
    lines, width, scen, cap, maxd, packed = sizes
    t0 = 2 * pair
    delays = i.delay[...]
    scale = i.atten[...]
    twice = 2.0 * i.admit[...]
    last = STEPS - 1

    even = lax.rem(lax.axis_index("region"), 2) == 0
    fresh = {}
    if pair:
        far_in = [jnp.where(even, i.swap_far[j], i.swap_near[j]) for j in range(2)]
        for j in range(2):
            far_volts = jnp.where(even, i.swap_near[j], i.swap_far[j])
            fresh[t0 - 2 + j] = scale * (twice * far_volts - i.into_prev[j])
            if hasattr(o, "back"):
                o.back[j] = fresh[t0 - 2 + j]
    else:
        far_in = [i.far_in[j] for j in range(2)]

    def back(t):
        if t in fresh:
            return fresh[t]
        if t < 0:
            return i.hist_b[0, t + maxd]
        return i.backs[t // 2][t % 2]

    made = {}

    def out(t):
        if t in made:
            return made[t]
        if t < 0:
            return i.hist_a[0, t + maxd]
        return i.made[t // 2][t % 2]

    points = 2 * lines + width
    known = i
    live = i.row[:, 2 * lines : 2 * lines + width] >= 0
    if packed:
        recv = i.recv[::-1]
        low = iota((1, LANES), 1) < cap
        params = []
        for row in range(6):
            pieces = []
            for j in range(width // LANES):
                one = recv[j][0, scen + row : scen + row + 1, :]
                two = recv[j][1, scen + row : scen + row + 1, :]
                pieces.append(jnp.where(low, one, pltpu.roll(two, cap, 1)))
            params.append(jnp.concatenate(pieces, axis=1))
    else:
        params = [i.recv[0, scen + row : scen + row + 1, :] for row in range(6)]
    params[5] = jnp.where(live, params[5], 1.0)

    def drive(second):
        return params[5] * jnp.tanh((params[4] + second) / params[5])

    if pair:
        first, second, current = i.state[0], i.state[1], i.current[...]
    else:
        if packed:
            ups, downs = [], []
            for j in range(width // LANES):
                one, two = recv[j][0, :scen], recv[j][1, :scen]
                ups.append(jnp.where(low, one, pltpu.roll(two, cap, 1)))
                downs.append(jnp.where(low, pltpu.roll(one, cap, 1), two))
            first, second = jnp.concatenate(ups, axis=1), jnp.concatenate(downs, axis=1)
        else:
            first, second = i.recv[0, :scen], i.recv[1, :scen]
        current = drive(second)

    fault_p = known.fault_p[...]
    ends = 2 * lines
    arrivals = [pick(back, delays, t0 + j, maxd) for j in range(2)]
    waves = jnp.concatenate(
        [jnp.concatenate([arrivals[j], far_in[j]], axis=1) for j in range(2)], axis=0
    )
    pairs = split2(waves)
    for part in range(2):
        o.x[part * 2 * scen : (part + 1) * 2 * scen, :ends] = pairs[part]
    both = dot(jnp.concatenate(pairs, axis=0), known.m_high[:ends, :])
    volts = both[: 2 * scen] + both[2 * scen :] + dot(pairs[0], known.m_low[:ends, :])
    base = [jnp.broadcast_to(i.base_p[t0 + j : t0 + j + 1, :], (scen, points)) for j in range(2)]
    volts = volts + jnp.concatenate(base, axis=0)
    fault_ends, fault_conv = fault_p[:, :ends], fault_p[:, ends:]
    wave_fault = jnp.sum(
        waves * jnp.concatenate([fault_ends, fault_ends], axis=0), axis=1, keepdims=True
    )
    highs, lows, coefs = [], [], []
    for j in range(2):
        here = slice(j * scen, (j + 1) * scen)
        high, low_part = split2(current)
        highs.append(high)
        lows.append(low_part)
        o.x[j * scen : (j + 1) * scen, ends:] = high
        o.x[(2 + j) * scen : (3 + j) * scen, ends:] = low_part
        both = dot(jnp.concatenate([high, low_part], axis=0), known.m_high[ends:, ends:])
        node = both[:scen] + both[scen:] + dot(high, known.m_low[ends:, ends:])
        at_fault = i.fault_base[:, t0 + j : t0 + j + 1] + wave_fault[here]
        at_fault = at_fault + jnp.sum(current * fault_conv, axis=1, keepdims=True)
        coef = i.fault_ratio[:, t0 + j : t0 + j + 1] * at_fault
        coefs.append(coef)
        o.coef[here, :] = jnp.broadcast_to(coef, (scen, LANES))
        node = node + volts[here, ends:] - fault_conv * coef
        first = params[1] * first + params[2] * (params[0] - node)
        second = second + params[3] * (first - second)
        current = drive(second)
    sides = []
    if t0 <= last - DMIN:
        both = dot(jnp.concatenate(highs + lows, axis=0), known.m_high[ends:, :ends])
        more = both[: 2 * scen] + both[2 * scen :]
        more = more + dot(jnp.concatenate(highs, axis=0), known.m_low[ends:, :ends])
        for j in range(2):
            here = slice(j * scen, (j + 1) * scen)
            line = volts[here, :ends] + more[here] - fault_ends * coefs[j]
            made[t0 + j] = scale * (twice * line[:, :lines] - arrivals[j])
            sides.append(line[:, lines:])
            if hasattr(o, "out"):
                o.out[j] = made[t0 + j]
    if sides:
        for j in range(2):
            onward = pick(out, delays, t0 + 2 + j, maxd)
            if hasattr(o, "into"):
                o.into[j] = onward
            o.swap_near[j] = jnp.where(even, onward, sides[j])
            o.swap_far[j] = jnp.where(even, sides[j], onward)
    if hasattr(o, "state"):
        o.state[0] = first
        o.state[1] = second
    if t0 + 2 < STEPS or not packed:
        o.current[...] = current
    else:
        half = scen // 2
        region = lax.axis_index("region")
        for j in range(width // LANES):
            mine = current[:, j * LANES : (j + 1) * LANES]
            top, bottom = mine[:half], mine[half:]
            pieces = (
                jnp.where(low, top, pltpu.roll(bottom, cap, 1)),
                jnp.where(low, pltpu.roll(top, cap, 1), bottom),
            )
            for k in range(2):
                o.current[jnp.bitwise_xor(region, 2 * j + k)] = pieces[k]


def full_body(sizes, pair, i, o):
    nblk, points, scen = sizes
    blk = LANES
    t0 = 2 * pair
    fault_z = i.fault_z[...]
    fault_blk = owner_of(i.fault_mark[...])
    x = i.x[...]
    coef = i.coef[...]
    lane = iota((points, blk), 1)
    for k in range(0, nblk, WIDE):
        mine = jnp.concatenate(
            [onehot(i.column[:points, :] == lane + (k + j) * blk) for j in range(WIDE)], axis=1
        )
        both = dot(x, mine)
        inject = both[: 2 * scen] + both[2 * scen :]
        for j in range(WIDE):
            here = slice((k + j) * blk, (k + j + 1) * blk)
            z = i.zcat[here, :]
            volts = product3(inject[:, j * blk : (j + 1) * blk], z[:, :blk], z[:, blk:])
            base = [
                jnp.broadcast_to(i.base[t0 + m : t0 + m + 1, here], (scen, blk))
                for m in range(2)
            ]
            zcol = jnp.where(fault_blk == k + j, fault_z, 0.0)
            volts = volts + jnp.concatenate(base, axis=0)
            volts = volts - jnp.concatenate([zcol, zcol], axis=0) * coef
            total = jnp.sum(volts * volts, axis=0, keepdims=True)
            if hasattr(i, "squares"):
                total = total + i.squares[:, here]
            o.squares[:, here] = total
            if hasattr(o, "volts"):
                o.volts[:, here] = volts[scen:]


def place_body(i, o):
    o.done[...] = jnp.zeros((1, LANES), F32)


def finish_body(sizes, i, o):
    regions, cap, scen, group, count, packed = sizes
    parts = [i.parts[k][...] for k in range(count)]
    while len(parts) > 1:
        parts = [parts[k] + parts[k + 1] for k in range(0, len(parts), 2)]
    o.rms[...] = jnp.sqrt(parts[0] / (scen * count * STEPS) + EPS)
    slots = i.slots[...]
    if packed:
        half = scen // 2
        lane = iota((LANES, group), 0)
        top = bottom = None
        for region in range(regions):
            left = onehot((lane < cap) & (slots == region * cap + lane))
            right = onehot((lane >= cap) & (slots == (region - 1) * cap + lane))
            both = dot(
                jnp.concatenate(split3(i.recv[region]), axis=0),
                jnp.concatenate([left, right], axis=1),
            )
            value = both[:half] + both[half : 2 * half] + both[2 * half :]
            top = value if top is None else top + value
        o.current[:half, :] = top[:, :group]
        o.current[half:, :] = top[:, group:]
    else:
        mask = onehot(iota((regions * cap, group), 0) == slots)
        both = dot(jnp.concatenate(split3(i.recv[...]), axis=0), mask)
        o.current[...] = both[:scen] + both[scen : 2 * scen] + both[2 * scen :]


def per_device(
    inv_blocks,
    src_amp,
    src_phase,
    line_a,
    line_b,
    line_delay,
    line_yc,
    line_atten,
    hist_ua,
    hist_ub,
    send_node,
    recv_slot,
    conv_par,
    conv_state,
    fault_node,
    fault_step,
    fault_cond,
):
    nblk, blk = inv_blocks.shape[0], inv_blocks.shape[1]
    nreg = nblk * blk
    lines = line_a.shape[1]
    maxd, scen = hist_ua.shape[1], hist_ua.shape[2]
    regions, cap = send_node.shape[1], send_node.shape[2]
    group = recv_slot.shape[1]
    width = regions * cap
    points = 2 * lines + width
    count = lax.axis_size("scen")
    packed = 2 * cap == LANES
    half = scen + 8

    amp, phase = src_amp.reshape(1, nreg), src_phase.reshape(1, nreg)
    if packed:
        slot_outs = dict.fromkeys(("even", "odd"), ((regions // 2, half, LANES), F32))
    else:
        slot_outs = dict(send=((half, regions * 2 * cap), F32))
    head = call(
        functools.partial(start_body, (regions, cap, half, scen, group, maxd)),
        "start",
        {},
        dict(into=((2, scen, lines), F32), **slot_outs),
        hbm=dict(
            slots=recv_slot, par=conv_par, state=conv_state, hist=hist_ua, delay=line_delay
        ),
    )
    if packed:
        even, odd = head.even, head.odd
    else:
        slots = head.send.reshape(half, 2, regions, cap).transpose(2, 1, 0, 3)
        even, odd = slots[0::2], slots[1::2]
    odd = mirrored(odd, "region", 1)
    into = head.into
    whole = points + blk
    inv_flat = inv_blocks.reshape(nreg, blk)
    tables = call(
        functools.partial(tables_body, (nreg, nblk, lines, regions, cap, scen)),
        "tables",
        {},
        dict(
            row=((1, whole), jnp.int32),
            mark=((whole, blk), BF16),
            fault_mark=((scen, blk), F32),
            column=((whole, blk), jnp.int32),
            zcat=((nreg, 2 * blk), BF16),
            base=((STEPS, nreg), F32),
            source_rows=((STEPS * nblk, blk), F32),
        ),
        hbm=dict(
            end_a=line_a,
            end_b=line_b,
            conv=send_node,
            fault_node=fault_node.reshape(1, scen),
            inv=inv_flat,
            amp=amp,
            phase=phase,
        ),
        cost=(4e9, 2e7),
    )
    later, fault_mark = lax.optimization_barrier((into, tables.fault_mark))
    far_in = shifted(later, "region", 1)
    if packed:
        shape = ((2, half, LANES), F32)
        couples = call(
            functools.partial(pair_body, regions // 2),
            "couple",
            dict(even=even, odd=odd, after=fault_mark),
            {PAIR + str(k): shape for k in range(regions // 2)},
        )
        couples = [getattr(couples, PAIR + str(k)) for k in range(regions // 2)]
    else:
        couples = [jnp.stack([even[k], odd[k]]) for k in range(regions // 2)]
    recv = couples[:1]
    for k in range(1, regions // 2):
        recv.append(mirrored(couples[k], "region", 2 * k))
    recv.reverse()
    if not packed:
        recv = jnp.concatenate(recv[::-1], axis=0).transpose(1, 2, 0, 3).reshape(2, half, width)

    model = call(
        functools.partial(rows_body, (nreg, nblk, lines, regions, cap, scen)),
        "rows",
        dict(
            row=tables.row,
            mark=tables.mark,
            column=tables.column,
            source_rows=tables.source_rows,
        ),
        dict(
            rows=((whole, 2 * blk), BF16),
            base_p=((STEPS, points), F32),
            fault_z=((scen, blk), F32),
            fault_base=((scen, blk), F32),
            fault_ratio=((scen, blk), F32),
            m_high=((points, points), BF16),
            m_low=((points, points), BF16),
            fault_p=((scen, points), F32),
        ),
        hbm=dict(
            list_a=line_a,
            list_b=line_b,
            list_conv=send_node,
            list_fault=fault_node.reshape(1, scen),
            inv=inv_flat,
            fault_step=fault_step.reshape(1, scen),
            fault_cond=fault_cond.reshape(1, scen),
        ),
        scalar=("list_a", "list_b", "list_conv", "list_fault"),
        scratch=(pltpu.VMEM((whole, blk), F32),),
        cost=(4e9, 2e7),
    )

    wave = ((2, scen, lines), F32)
    mades, backs, carry = {}, {}, {}
    squares = swap_near = swap_far = sent = None
    for pair in range(STEPS // 2):
        t0 = 2 * pair
        final = t0 + 2 >= STEPS
        ins = dict(
            delay=line_delay,
            atten=line_atten,
            admit=line_yc,
            recv=recv,
            base_p=model.base_p,
            m_high=model.m_high,
            m_low=model.m_low,
            fault_p=model.fault_p,
            fault_base=model.fault_base,
            fault_ratio=model.fault_ratio,
            **carry,
        )
        if t0 - maxd < 0:
            ins.update(hist_b=hist_ub)
        if pair:
            ins.update(swap_near=swap_near, swap_far=swap_far, into_prev=sent, row=tables.row)
        else:
            ins.update(far_in=far_in)
            ins.update(row=tables.row)
        first = max(0, pair - 3)
        ins.update(backs={k: v for k, v in backs.items() if k >= first})
        if not final:
            ins.update(made={k: v for k, v in mades.items() if k >= pair - 2})
            if t0 + 2 - maxd < 0:
                ins.update(hist_a=hist_ua)
        outs = dict(x=((4 * scen, points), BF16), coef=((2 * scen, LANES), F32))
        if not final:
            outs.update(
                swap_far=wave,
                swap_near=wave,
                state=((2, scen, width), F32),
                current=((scen, width), F32),
            )
            if t0 + 4 < STEPS:
                outs.update(out=wave, into=wave)
            if pair:
                outs.update(back=wave)
        else:
            shape = (regions, scen // 2, LANES) if packed else (scen, width)
            outs.update(current=(shape, F32))
        made = call(
            functools.partial(advance_body, (lines, width, scen, cap, maxd, packed), pair),
            "advance",
            ins,
            outs,
        )
        if not final:
            sent = into
            if t0 + 4 < STEPS:
                into = made.into
            swap_far = swapped(made.swap_far, "region", 1)
            swap_near = swapped(made.swap_near, "region", 0)
            if t0 + 4 < STEPS:
                mades[pair] = made.out
            if pair:
                backs[pair - 1] = made.back
            carry = dict(state=made.state, current=made.current)
        else:
            current = made.current
            if packed:
                returned = lax.all_to_all(current, "region", split_axis=0, concat_axis=0, tiled=True)
            else:
                order = jnp.bitwise_xor(lax.axis_index("region"), jnp.arange(regions))
                current = current.reshape(scen, regions, cap).transpose(1, 0, 2)[order]
                returned = lax.all_to_all(current, "region", split_axis=0, concat_axis=0, tiled=True)
                returned = returned.transpose(1, 0, 2).reshape(scen, width)
        ins = dict(
            x=made.x,
            coef=made.coef,
            fault_mark=tables.fault_mark,
            fault_z=model.fault_z,
            column=tables.column,
            zcat=tables.zcat,
            base=tables.base,
        )
        if pair:
            ins.update(squares=squares)
        outs = dict(squares=((1, nreg), F32))
        if final:
            outs.update(volts=((scen, nreg), F32))
        full = call(
            functools.partial(full_body, (nblk, points, scen), pair),
            "full",
            ins,
            outs,
            cost=(4e9, 1e7),
        )
        squares = full.squares

    parts = [squares]
    for offset in range(1, count):
        pairs = [(source, source ^ offset) for source in range(count)]
        parts.append(lax.ppermute(squares, "scen", pairs))
    placed = call(
        place_body,
        "place",
        dict(volts=full.volts),
        dict(done=((1, LANES), F32)),
        relays=dict(volts=((scen, nreg), F32)),
    )
    tail = call(
        functools.partial(finish_body, (regions, cap, scen, group, count, packed)),
        "finish",
        dict(slots=recv_slot, recv=returned, parts=parts, after=placed.done),
        dict(rms=((1, nreg), F32), current=((scen, group), F32)),
    )
    return placed.volts, tail.current, tail.rms.reshape(nreg)


def solution(mesh):
    return jax.shard_map(
        per_device,
        mesh=mesh,
        in_specs=(
            P("region", None, None),
            P("region"),
            P("region"),
            P("region", None),
            P("region", None),
            P("region", None),
            P("region", None),
            P("region", None),
            P("region", None, "scen", None),
            P("region", None, "scen", None),
            P("region", None, None),
            P("region", None),
            P(None, "region"),
            P(None, "scen", "region"),
            P("scen"),
            P("scen"),
            P("scen"),
        ),
        out_specs=(P("scen", "region"), P("scen", "region"), P("region")),
        check_vma=False,
    )
```
